128 devices in a mesh: row: 16 (over x, z), col: 8 (over y, core).
Axes of the slice: x: 4, y: 4, z: 4, core: 2. Of those that a mesh axis runs over, the one named last changes fastest.
Arguments:
- qkv: bfloat16 [3, 1408, 32768], P(None, 'col', 'row'), may hold values from -12.1 to 12.1
- residual_in: bfloat16 [1408, 32768], P('col', 'row'), may hold values from -3 to 3
- out_weight: bfloat16 [1408, 1408], replicated, may hold values from -0.625 to 0.625
- merge_weight: bfloat16 [1408, 5632], P('col'), may hold values from -0.078125 to 0.078125
- merge_gain: float32 [1408], replicated, may hold values from 0.1 to 1.9
- image_groups: int32 [64], replicated, may hold values from 1 to 256, 8192 in all
- dest_row: int32 [8192], P('row'), may hold values from 0 to 8191, as said below
Outputs:
- layer_out: bfloat16 [1408, 32768], P('col', 'row')
- image_rows: bfloat16 [1408, 8192], P('col', 'row')
The draws below stay inside these ranges and needn't reach their ends.
Inputs may be any that keep to these rules, and one draw needn't show every extreme that they name: dest_row is a permutation of 0 to 8191. Of the 512 entries held by each index of row, exactly 32 fall in each aligned block of 512 output rows.
All inputs are finite; a program needn't handle non-finite values.
Results may differ from the reference program's by a relative error of at most 0.0064.
Values may be sent and summed in bfloat16 or wider, within the bound.
A program may use at most 128 MiB of HBM per device.

```python
import math
import jax
import jax.numpy as jnp
import numpy as np
from jax import lax

D = 1408
HEADS = 16
HEAD_DIM = 88
TOK_DEV = 2048
TOKENS = 32768
GROUPS = 8192
IMAGES = 64
MOST_GROUPS = 256
N_ROW = 16


def draw_qkv(key, part):
    key_base = jax.random.fold_in(jax.random.fold_in(key, 11), 0)
    scales = jnp.array([1.2, 1.2, 1.0], jnp.float32)[:, None, None]
    base = jnp.clip(jax.random.normal(key_base, (3, D, TOKENS), jnp.float32), -8.0, 8.0) * scales
    return base.astype(jnp.bfloat16)


def draw_dest_row(key, part):
    group_rows = TOK_DEV // 4
    share_rows = group_rows // N_ROW
    key_source, key_owner = jax.random.split(jax.random.fold_in(key, 23))
    source_perm = jax.vmap(lambda sub_key: jax.random.permutation(sub_key, group_rows))(jax.random.split(key_source, N_ROW)).astype(jnp.int32)
    owner_perm = jax.vmap(lambda sub_key: jax.random.permutation(sub_key, group_rows))(jax.random.split(key_owner, N_ROW)).astype(jnp.int32)
    offsets = (jnp.arange(N_ROW, dtype=jnp.int32) * group_rows)[:, None]
    source_index = (source_perm + offsets).reshape(N_ROW, N_ROW, share_rows)
    target_index = (owner_perm + offsets).reshape(N_ROW, N_ROW, share_rows).transpose(1, 0, 2)
    result = jnp.zeros((N_ROW * group_rows,), jnp.int32)
    return result.at[source_index.reshape(-1)].set(target_index.reshape(-1))


def steps_of(key, extent, cuts, least, largest):
    gain = 1.0
    for axis_at, parts in cuts:
        heights = jax.random.uniform(jax.random.fold_in(jax.random.fold_in(key, 6), axis_at), (parts,), jnp.float32, least / len(cuts), largest / len(cuts))
        gain = gain * jnp.repeat(jnp.exp(heights), extent[axis_at] // parts).reshape((-1,) + (1,) * (len(extent) - 1 - axis_at))
    return gain


def length_profile(count, total, bound, lean):
    weights = [(1 << 20) // math.isqrt(rank ** lean) + 1 for rank in range(2, count + 1)]
    surplus, counts = total - bound - (count - 1), [1] * (count - 1)
    while surplus > 0:
        candidates = [i for i in range(count - 1) if counts[i] < bound]
        whole, left = sum([weights[i] for i in candidates]), surplus
        for i in candidates:
            extra = min(bound - counts[i], max(1, left * weights[i] // whole), surplus)
            counts[i] = counts[i] + extra
            surplus = surplus - extra
    return np.array([bound] + counts)


def uneven_parts(rng, number_of, total, reach, slope):
    if number_of == 2:
        one = jax.random.randint(rng, (), max(1, total - reach), min(reach, total - 1) + 1)
        return jnp.stack([one, total - one])
    lengths = jnp.asarray(length_profile(number_of, total, reach, slope), jnp.int32)
    couples = (number_of - 1) // 2
    giver, taker = lengths[1:1 + 2 * couples:2], lengths[2:2 + 2 * couples:2]
    room = jnp.minimum(giver - 1, reach - taker)
    moved = jax.random.randint(jax.random.fold_in(rng, 1), (couples,), 0, 1 << 20) % (room + 1)
    lengths = lengths.at[1:1 + 2 * couples:2].set(giver - moved).at[2:2 + 2 * couples:2].set(taker + moved)
    return lengths[jax.random.permutation(jax.random.fold_in(rng, 2), number_of)]


def centred(stream_key, extent, width, bound, pieces=(), held_as=jnp.bfloat16):
    entries = width * jax.random.normal(stream_key, extent, jnp.float32)
    if pieces:
        entries = entries * steps_of(stream_key, extent, pieces, -0.22, 0.18)
    return jnp.clip(entries, -bound, bound).astype(held_as)


def setup_inputs(seed: int = 0) -> dict:
    arg_keys = jax.random.split(jax.random.key(seed), 8)
    return {
        "qkv": draw_qkv(jax.random.fold_in(arg_keys[7], 71), 0),
        "residual_in": centred(arg_keys[1], (D, TOKENS), 0.5, 3.0, ((0, 8), (1, 16))),
        "out_weight": centred(arg_keys[2], (D, D), HEAD_DIM ** -0.5, 0.625),
        "merge_weight": centred(arg_keys[3], (D, 4 * D), (4 * D) ** -0.5, 0.078125, ((0, 8),)),
        "merge_gain": jnp.clip(1.0 + 0.18 * jax.random.normal(arg_keys[4], (D,), jnp.float32), 0.1, 1.9),
        "image_groups": uneven_parts(arg_keys[5], IMAGES, GROUPS, MOST_GROUPS, 2).astype(jnp.int32),
        "dest_row": draw_dest_row(jax.random.fold_in(arg_keys[7], 71), 0),
    }


def image_labels(positions, image_ends, all_tokens):
    inside = (positions >= 0) & (positions < all_tokens)
    counted = lax.optimization_barrier(jnp.sum((positions[:, None] >= image_ends[None, :]).astype(jnp.int32), axis=1)).astype(jnp.int32)
    return jnp.where(inside, counted, -1)

def reference(qkv, residual_in, out_weight, merge_weight, merge_gain, image_groups, dest_row):
    reach_rows = TOK_DEV // 2
    block_rows = min(512, TOK_DEV)
    window = block_rows + 2 * reach_rows
    score_scale = 1.0 / math.sqrt(HEAD_DIM)
    token_major = jnp.transpose(qkv, (0, 2, 1))
    image_ends = jnp.cumsum(image_groups).astype(jnp.int32) * 4
    positions = jnp.arange(TOKENS + 2 * reach_rows, dtype=jnp.int32) - reach_rows
    labels = image_labels(positions, image_ends, TOKENS)
    padded = jnp.pad(token_major[1:], ((0, 0), (reach_rows, reach_rows), (0, 0)))

    def attend(block_id):
        first_row = block_id * block_rows
        queries = lax.dynamic_slice_in_dim(token_major[0], first_row, block_rows, 0).astype(jnp.float32).reshape(block_rows, HEADS, HEAD_DIM)
        key_block = lax.dynamic_slice_in_dim(padded[0], first_row, window, 0).astype(jnp.float32).reshape(window, HEADS, HEAD_DIM)
        value_block = lax.dynamic_slice_in_dim(padded[1], first_row, window, 0).astype(jnp.float32).reshape(window, HEADS, HEAD_DIM)
        query_labels = lax.dynamic_slice_in_dim(labels, first_row + reach_rows, block_rows, 0)
        key_labels = lax.dynamic_slice_in_dim(labels, first_row, window, 0)
        scores = jnp.einsum('qhd,khd->hqk', queries, key_block) * score_scale
        same_image = (query_labels[:, None] == key_labels[None, :])[None]
        scores = jnp.where(same_image, scores, -1e+30)
        row_max = lax.optimization_barrier(jnp.max(scores, axis=2, keepdims=True))
        exponent = jnp.exp(scores - row_max)
        totals = lax.optimization_barrier(jnp.sum(exponent, axis=2))
        weights = exponent.astype(jnp.bfloat16).astype(jnp.float32)
        weighted = jnp.einsum('hqk,khd->qhd', weights, value_block)
        weighted = weighted / jnp.transpose(totals)[:, :, None]
        return weighted.astype(jnp.bfloat16).reshape(block_rows, D)
    attended = lax.map(attend, jnp.arange(TOKENS // block_rows, dtype=jnp.int32)).reshape(TOKENS, D)
    projected = jnp.dot(attended, out_weight, preferred_element_type=jnp.float32)
    layer_rows = (jnp.transpose(residual_in).astype(jnp.float32) + projected).astype(jnp.bfloat16)
    values32 = layer_rows.astype(jnp.float32)
    centre = lax.optimization_barrier(jnp.mean(values32, axis=1, keepdims=True))
    spread = lax.optimization_barrier(jnp.mean(jnp.square(values32 - centre), axis=1, keepdims=True))
    normed = ((values32 - centre) * lax.rsqrt(spread + 1e-06) * merge_gain.astype(jnp.float32)).astype(jnp.bfloat16)
    grouped = normed.reshape(GROUPS, 4 * D)
    merged = jnp.dot(grouped, jnp.transpose(merge_weight), preferred_element_type=jnp.float32).astype(jnp.bfloat16)
    image_rows = jnp.zeros((GROUPS, D), jnp.bfloat16).at[dest_row].set(merged)
    return (jnp.transpose(layer_rows), jnp.transpose(image_rows))
```

```python
import functools
import math

import jax
import jax.numpy as jnp
from jax import lax
from jax.experimental import pallas as pl
from jax.experimental.pallas import tpu as pltpu
from jax.sharding import PartitionSpec as P

HEAD_DIM = 88
QB = 256
KB = 256
STEP = 128
NEG = -1e30


def tile_step(kt, v0, v1, qcat, ok, coef, row, m_ref, l_ref, acc_ref):
    scores = lax.dot_general(
        kt, qcat, (((1,), (0,)), ((), ())), preferred_element_type=jnp.float32
    )
    width = qcat.shape[1] // 2
    for head in range(2):
        part = jnp.where(ok, scores[:, head * width : (head + 1) * width], NEG)
        old = m_ref[row + head]
        new = jnp.maximum(old, jnp.max(part, axis=0, keepdims=True))
        fade = jnp.exp2((old - new) * coef)
        expo = jnp.exp2(part * coef - new * coef)
        l_ref[row + head] = l_ref[row + head] * fade + jnp.sum(expo, axis=0, keepdims=True)
        m_ref[row + head] = new
        values = v1 if head else v0
        acc_ref[row + head] = acc_ref[row + head] * fade + lax.dot_general(
            values,
            expo.astype(jnp.bfloat16),
            (((1,), (0,)), ((), ())),
            preferred_element_type=jnp.float32,
        )


def stage_keys(k_src, v_src, kt_ref, v_ref, count, offset):
    def one(i, carry):
        at = pl.multiple_of(i * 256, 256)
        to = pl.multiple_of(offset + i * 256, 256)
        kt_ref[pl.ds(to, 256), :] = jnp.transpose(k_src[:, pl.ds(at, 256)])
        values = v_src[:, pl.ds(at, 256)].astype(jnp.float32)
        v_ref[0, :, pl.ds(to, 256)] = values[:HEAD_DIM].astype(jnp.bfloat16)
        v_ref[1, :, pl.ds(to, 256)] = values[HEAD_DIM:].astype(jnp.bfloat16)
        return carry

    lax.fori_loop(0, count, one, 0)


def query_pair(q_ref, at):
    block = q_ref[:, pl.ds(at, QB)]
    feature = lax.broadcasted_iota(jnp.int32, block.shape, 0)
    zero = jnp.zeros_like(block)
    return jnp.concatenate(
        [jnp.where(feature < HEAD_DIM, block, zero), jnp.where(feature < HEAD_DIM, zero, block)],
        axis=1,
    )


def local_kernel(coef, lo_ref, n_ref, qkv_ref, start_ref, len_ref, m_ref, l_ref, acc_ref, kt, vt):
    blocks = qkv_ref.shape[2] // QB
    stage_keys(qkv_ref.at[1], qkv_ref.at[2], kt, vt, qkv_ref.shape[2] // 256, 0)

    def per_block(b, carry):
        at = pl.multiple_of(b * QB, QB)
        qcat = query_pair(qkv_ref.at[0], at)
        start = start_ref[0:1, pl.ds(at, QB)]
        length = len_ref[0:1, pl.ds(at, QB)]
        row = b * 2
        for head in range(2):
            m_ref[row + head] = jnp.full((1, QB), NEG, jnp.float32)
            l_ref[row + head] = jnp.zeros((1, QB), jnp.float32)
            acc_ref[row + head] = jnp.zeros((HEAD_DIM, QB), jnp.float32)

        def per_tile(t, inner):
            key = pl.multiple_of(lo_ref[b] * STEP + t * KB, STEP)
            place = lax.broadcasted_iota(jnp.int32, (KB, QB), 0) + (key - start)
            ok = (place >= 0) & (place < length)
            tile_step(
                kt[pl.ds(key, KB), :],
                vt[0, :, pl.ds(key, KB)],
                vt[1, :, pl.ds(key, KB)],
                qcat,
                ok,
                coef,
                row,
                m_ref,
                l_ref,
                acc_ref,
            )
            return inner

        lax.fori_loop(0, n_ref[b], per_tile, 0)
        return carry

    lax.fori_loop(0, blocks, per_block, 0)


def halo_kernel(
    coef,
    first_ref,
    n_ref,
    qkv_ref,
    left_ref,
    right_ref,
    start_ref,
    len_ref,
    m_in,
    l_in,
    acc_in,
    out_ref,
    kt,
    vt,
    m_ref,
    l_ref,
    acc_ref,
):
    reach = left_ref.shape[2]
    tokens = qkv_ref.shape[2]
    blocks = tokens // QB
    stage_keys(left_ref.at[0], left_ref.at[1], kt, vt, reach // 256, 0)
    stage_keys(right_ref.at[0], right_ref.at[1], kt, vt, reach // 256, reach)

    def per_block(b, carry):
        at = pl.multiple_of(b * QB, QB)
        start = start_ref[0:1, pl.ds(at, QB)]
        length = len_ref[0:1, pl.ds(at, QB)]
        row = b * 2
        for head in range(2):
            m_ref[head] = m_in[row + head]
            l_ref[head] = l_in[row + head]
            acc_ref[head] = acc_in[row + head]
        for side in range(2):
            shift = tokens if side else -reach
            base = side * reach

            @pl.when(n_ref[side * blocks + b] > 0)
            def _():
                qcat = query_pair(qkv_ref.at[0], at)

                def per_tile(t, inner):
                    key = pl.multiple_of(first_ref[side * blocks + b] * STEP + t * KB, STEP)
                    place = lax.broadcasted_iota(jnp.int32, (KB, QB), 0) + (key + shift - start)
                    ok = (place >= 0) & (place < length)
                    slot = pl.multiple_of(key + base, STEP)
                    tile_step(
                        kt[pl.ds(slot, KB), :],
                        vt[0, :, pl.ds(slot, KB)],
                        vt[1, :, pl.ds(slot, KB)],
                        qcat,
                        ok,
                        coef,
                        0,
                        m_ref,
                        l_ref,
                        acc_ref,
                    )
                    return inner

                lax.fori_loop(0, n_ref[side * blocks + b], per_tile, 0)

        both = [acc_ref[head] / l_ref[head] for head in range(2)]
        out_ref[:, pl.ds(at, QB)] = jnp.concatenate(both, axis=0).astype(jnp.bfloat16)
        return carry

    lax.fori_loop(0, blocks, per_block, 0)


def attention(qkv, left, right, image_groups, row_id, all_tokens):
    _, width, tokens = qkv.shape
    reach = left.shape[2]
    blocks = tokens // QB
    coef = math.log2(math.e) / math.sqrt(HEAD_DIM)
    ends = jnp.cumsum(image_groups) * 4
    begins = ends - image_groups * 4
    position = row_id * tokens + jnp.arange(tokens, dtype=jnp.int32)
    mine = (position[:, None] >= begins[None, :]) & (position[:, None] < ends[None, :])
    start = jnp.sum(jnp.where(mine, begins[None, :], 0), axis=1) - row_id * tokens
    length = jnp.sum(jnp.where(mine, (image_groups * 4)[None, :], 0), axis=1)
    first = start[::QB]
    last = (start + length)[QB - 1 :: QB]

    def tiles(low, high, extent):
        low_step = low // STEP
        count = jnp.maximum(-((low_step * STEP - high) // KB), 0)
        low_step = jnp.clip(low_step, 0, extent // STEP - count * (KB // STEP))
        return low_step, jnp.where(high > low, count, 0)

    local_lo, local_n = tiles(jnp.maximum(first, 0), jnp.minimum(last, tokens), tokens)
    left_lo, left_n = tiles(
        jnp.clip(first + reach, 0, reach), jnp.full_like(first, reach), reach
    )
    right_lo, right_n = tiles(jnp.zeros_like(first), jnp.clip(last - tokens, 0, reach), reach)
    halo_lo = jnp.concatenate([left_lo, right_lo])
    halo_n = jnp.concatenate([left_n, right_n])
    start2, length2 = start[None, :], length[None, :]
    smem = pl.BlockSpec(memory_space=pltpu.SMEM)
    vmem = pl.BlockSpec(memory_space=pltpu.VMEM)
    stat = jax.ShapeDtypeStruct((2 * blocks, 1, QB), jnp.float32)
    m, l, acc = pl.pallas_call(
        functools.partial(local_kernel, coef),
        out_shape=(stat, stat, jax.ShapeDtypeStruct((2 * blocks, HEAD_DIM, QB), jnp.float32)),
        in_specs=[smem, smem, vmem, vmem, vmem],
        out_specs=(vmem, vmem, vmem),
        scratch_shapes=[
            pltpu.VMEM((tokens, width), jnp.bfloat16),
            pltpu.VMEM((2, HEAD_DIM, tokens), jnp.bfloat16),
        ],
        compiler_params=pltpu.CompilerParams(vmem_limit_bytes=32 << 20),
        cost_estimate=pl.CostEstimate(
            flops=4 * width * tokens * 1200, bytes_accessed=8 << 20, transcendentals=2 * tokens * 1200
        ),
    )(local_lo, local_n, qkv, start2, length2)
    return pl.pallas_call(
        functools.partial(halo_kernel, coef),
        out_shape=jax.ShapeDtypeStruct((width, tokens), jnp.bfloat16),
        in_specs=[smem, smem] + [vmem] * 8,
        out_specs=vmem,
        scratch_shapes=[
            pltpu.VMEM((2 * reach, width), jnp.bfloat16),
            pltpu.VMEM((2, HEAD_DIM, 2 * reach), jnp.bfloat16),
            pltpu.VMEM((2, 1, QB), jnp.float32),
            pltpu.VMEM((2, 1, QB), jnp.float32),
            pltpu.VMEM((2, HEAD_DIM, QB), jnp.float32),
        ],
        compiler_params=pltpu.CompilerParams(vmem_limit_bytes=32 << 20),
        cost_estimate=pl.CostEstimate(
            flops=4 * width * tokens * 300, bytes_accessed=8 << 20, transcendentals=2 * tokens * 300
        ),
    )(halo_lo, halo_n, qkv, left, right, start2, length2, m, l, acc)


def body(qkv, residual_in, out_weight, merge_weight, merge_gain, image_groups, dest_row):
    width_here = qkv.shape[1]
    tok_rows = qkv.shape[2]
    full_width = out_weight.shape[0]
    reach = tok_rows // 2
    rows = lax.axis_size("row")
    cols = lax.axis_size("col")
    row_id = lax.axis_index("row")
    all_tokens = tok_rows * rows
    chunk = tok_rows // cols
    group_rows = tok_rows // 4
    share = group_rows // rows

    left = lax.ppermute(
        qkv[1:, :, tok_rows - reach :], "row", [(i, i + 1) for i in range(rows - 1)]
    )
    right = lax.ppermute(qkv[1:, :, :reach], "row", [(i + 1, i) for i in range(rows - 1)])
    residual = lax.all_to_all(residual_in, "col", 1, 0, tiled=True)

    owner = dest_row // group_rows
    ids = jnp.arange(group_rows, dtype=jnp.int32)
    earlier = (owner[None, :] == owner[:, None]) & (ids[None, :] < ids[:, None])
    spot = owner * share + jnp.sum(earlier.astype(jnp.int32), axis=1)
    slots = jnp.arange(group_rows, dtype=jnp.int32)
    picked = spot[:, None] == slots[None, :]
    sent_dest = jnp.sum(jnp.where(picked, (dest_row % group_rows)[:, None], 0), axis=0)
    got_dest = lax.all_to_all(sent_dest, "row", 0, 0, tiled=True)
    placed = (got_dest[:, None] == slots[None, :]).astype(jnp.bfloat16)
    picked = picked.astype(jnp.bfloat16)

    attended = attention(qkv, left, right, image_groups, row_id, all_tokens)
    attended = lax.all_to_all(attended, "col", 1, 0, tiled=True)
    projected = lax.dot_general(
        out_weight, attended, (((0,), (0,)), ((), ())), preferred_element_type=jnp.float32
    )
    layer_rows = (residual.astype(jnp.float32) + projected).astype(jnp.bfloat16)
    layer_out = lax.all_to_all(layer_rows, "col", 0, 1, tiled=True)
    values32 = layer_rows.astype(jnp.float32)
    centre = jnp.mean(values32, axis=0, keepdims=True)
    spread = jnp.mean(jnp.square(values32 - centre), axis=0, keepdims=True)
    normed = ((values32 - centre) * lax.rsqrt(spread + 1e-06) * merge_gain[:, None]).astype(
        jnp.bfloat16
    )
    t = jnp.arange(chunk, dtype=jnp.int32)
    order = ((t % 4) * (chunk // 4) + t // 4)[:, None] == t[None, :]
    by_part = jnp.dot(normed, order.astype(jnp.bfloat16)).astype(jnp.bfloat16)
    by_part = by_part.reshape(full_width, 4, chunk // 4).transpose(1, 0, 2)
    gathered = lax.all_gather(by_part, "col", axis=2, tiled=True)
    parts = merge_weight.reshape(width_here, 4, full_width)
    merged = sum(
        jnp.dot(parts[:, j], gathered[j], preferred_element_type=jnp.float32) for j in range(4)
    ).astype(jnp.bfloat16)
    sorted_rows = lax.dot_general(
        picked, merged, (((0,), (1,)), ((), ())), preferred_element_type=jnp.float32
    ).astype(jnp.bfloat16)
    got_rows = lax.all_to_all(sorted_rows, "row", 0, 0, tiled=True)
    image_rows = lax.dot_general(
        got_rows, placed, (((0,), (0,)), ((), ())), preferred_element_type=jnp.float32
    ).astype(jnp.bfloat16)
    return (layer_out, image_rows)


def solution(mesh):
    return jax.shard_map(
        body,
        mesh=mesh,
        in_specs=(P(None, "col", "row"), P("col", "row"), P(), P("col", None), P(), P(), P("row")),
        out_specs=(P("col", "row"), P("col", "row")),
        check_vma=False,
    )
```

```python
import functools
import math

import jax
import jax.numpy as jnp
from jax import lax
from jax.experimental import pallas as pl
from jax.experimental.pallas import tpu as pltpu
from jax.sharding import PartitionSpec as P

HEAD_DIM = 88
QB = 256
KB = 256
STEP = 128
NEG = -1e30


def tile_step(kt, v0, v1, qcat, ok, coef, row, m_ref, l_ref, acc_ref):
    scores = lax.dot_general(
        kt, qcat, (((1,), (0,)), ((), ())), preferred_element_type=jnp.float32
    )
    width = qcat.shape[1] // 2
    for head in range(2):
        part = jnp.where(ok, scores[:, head * width : (head + 1) * width], NEG)
        old = m_ref[row + head]
        new = jnp.maximum(old, jnp.max(part, axis=0, keepdims=True))
        fade = jnp.exp2((old - new) * coef)
        expo = jnp.exp2(part * coef - new * coef)
        l_ref[row + head] = l_ref[row + head] * fade + jnp.sum(expo, axis=0, keepdims=True)
        m_ref[row + head] = new
        values = v1 if head else v0
        acc_ref[row + head] = acc_ref[row + head] * fade + lax.dot_general(
            values,
            expo.astype(jnp.bfloat16),
            (((1,), (0,)), ((), ())),
            preferred_element_type=jnp.float32,
        )


def stage_keys(k_src, v_src, kt_ref, v_ref, count, offset):
    def one(i, carry):
        at = pl.multiple_of(i * 256, 256)
        to = pl.multiple_of(offset + i * 256, 256)
        kt_ref[pl.ds(to, 256), :] = jnp.transpose(k_src[:, pl.ds(at, 256)])
        values = v_src[:, pl.ds(at, 256)].astype(jnp.float32)
        v_ref[0, :, pl.ds(to, 256)] = values[:HEAD_DIM].astype(jnp.bfloat16)
        v_ref[1, :, pl.ds(to, 256)] = values[HEAD_DIM:].astype(jnp.bfloat16)
        return carry

    lax.fori_loop(0, count, one, 0)


def query_pair(q_ref, at):
    block = q_ref[:, pl.ds(at, QB)]
    feature = lax.broadcasted_iota(jnp.int32, block.shape, 0)
    zero = jnp.zeros_like(block)
    return jnp.concatenate(
        [jnp.where(feature < HEAD_DIM, block, zero), jnp.where(feature < HEAD_DIM, zero, block)],
        axis=1,
    )


def local_kernel(coef, lo_ref, n_ref, qkv_ref, start_ref, len_ref, m_ref, l_ref, acc_ref, kt, vt):
    blocks = qkv_ref.shape[2] // QB
    stage_keys(qkv_ref.at[1], qkv_ref.at[2], kt, vt, qkv_ref.shape[2] // 256, 0)

    def per_block(b, carry):
        at = pl.multiple_of(b * QB, QB)
        qcat = query_pair(qkv_ref.at[0], at)
        start = start_ref[0:1, pl.ds(at, QB)]
        length = len_ref[0:1, pl.ds(at, QB)]
        row = b * 2
        for head in range(2):
            m_ref[row + head] = jnp.full((1, QB), NEG, jnp.float32)
            l_ref[row + head] = jnp.zeros((1, QB), jnp.float32)
            acc_ref[row + head] = jnp.zeros((HEAD_DIM, QB), jnp.float32)

        def per_tile(t, inner):
            key = pl.multiple_of(lo_ref[b] * STEP + t * KB, STEP)
            place = lax.broadcasted_iota(jnp.int32, (KB, QB), 0) + (key - start)
            ok = (place >= 0) & (place < length)
            tile_step(
                kt[pl.ds(key, KB), :],
                vt[0, :, pl.ds(key, KB)],
                vt[1, :, pl.ds(key, KB)],
                qcat,
                ok,
                coef,
                row,
                m_ref,
                l_ref,
                acc_ref,
            )
            return inner

        lax.fori_loop(0, n_ref[b], per_tile, 0)
        return carry

    lax.fori_loop(0, blocks, per_block, 0)


def halo_kernel(
    coef,
    first_ref,
    n_ref,
    qkv_ref,
    left_ref,
    right_ref,
    start_ref,
    len_ref,
    m_in,
    l_in,
    acc_in,
    out_ref,
    kt,
    vt,
    m_ref,
    l_ref,
    acc_ref,
):
    reach = left_ref.shape[2]
    tokens = qkv_ref.shape[2]
    blocks = tokens // QB
    stage_keys(left_ref.at[0], left_ref.at[1], kt, vt, reach // 256, 0)
    stage_keys(right_ref.at[0], right_ref.at[1], kt, vt, reach // 256, reach)

    def per_block(b, carry):
        at = pl.multiple_of(b * QB, QB)
        start = start_ref[0:1, pl.ds(at, QB)]
        length = len_ref[0:1, pl.ds(at, QB)]
        row = b * 2
        for head in range(2):
            m_ref[head] = m_in[row + head]
            l_ref[head] = l_in[row + head]
            acc_ref[head] = acc_in[row + head]
        for side in range(2):
            shift = tokens if side else -reach
            base = side * reach

            @pl.when(n_ref[side * blocks + b] > 0)
            def _():
                qcat = query_pair(qkv_ref.at[0], at)

                def per_tile(t, inner):
                    key = pl.multiple_of(first_ref[side * blocks + b] * STEP + t * KB, STEP)
                    place = lax.broadcasted_iota(jnp.int32, (KB, QB), 0) + (key + shift - start)
                    ok = (place >= 0) & (place < length)
                    slot = pl.multiple_of(key + base, STEP)
                    tile_step(
                        kt[pl.ds(slot, KB), :],
                        vt[0, :, pl.ds(slot, KB)],
                        vt[1, :, pl.ds(slot, KB)],
                        qcat,
                        ok,
                        coef,
                        0,
                        m_ref,
                        l_ref,
                        acc_ref,
                    )
                    return inner

                lax.fori_loop(0, n_ref[side * blocks + b], per_tile, 0)

        both = [acc_ref[head] / l_ref[head] for head in range(2)]
        out_ref[:, pl.ds(at, QB)] = jnp.concatenate(both, axis=0).astype(jnp.bfloat16)
        return carry

    lax.fori_loop(0, blocks, per_block, 0)


def attention(qkv, left, right, image_groups, row_id, all_tokens):
    _, width, tokens = qkv.shape
    reach = left.shape[2]
    blocks = tokens // QB
    coef = math.log2(math.e) / math.sqrt(HEAD_DIM)
    ends = jnp.cumsum(image_groups) * 4
    begins = ends - image_groups * 4
    position = row_id * tokens + jnp.arange(tokens, dtype=jnp.int32)
    mine = (position[:, None] >= begins[None, :]) & (position[:, None] < ends[None, :])
    start = jnp.sum(jnp.where(mine, begins[None, :], 0), axis=1) - row_id * tokens
    length = jnp.sum(jnp.where(mine, (image_groups * 4)[None, :], 0), axis=1)
    first = start[::QB]
    last = (start + length)[QB - 1 :: QB]

    def tiles(low, high, extent):
        low_step = low // STEP
        count = jnp.maximum(-((low_step * STEP - high) // KB), 0)
        low_step = jnp.clip(low_step, 0, extent // STEP - count * (KB // STEP))
        return low_step, jnp.where(high > low, count, 0)

    local_lo, local_n = tiles(jnp.maximum(first, 0), jnp.minimum(last, tokens), tokens)
    left_lo, left_n = tiles(
        jnp.clip(first + reach, 0, reach), jnp.full_like(first, reach), reach
    )
    right_lo, right_n = tiles(jnp.zeros_like(first), jnp.clip(last - tokens, 0, reach), reach)
    halo_lo = jnp.concatenate([left_lo, right_lo])
    halo_n = jnp.concatenate([left_n, right_n])
    start2, length2 = start[None, :], length[None, :]
    smem = pl.BlockSpec(memory_space=pltpu.SMEM)
    vmem = pl.BlockSpec(memory_space=pltpu.VMEM)
    stat = jax.ShapeDtypeStruct((2 * blocks, 1, QB), jnp.float32)
    m, l, acc = pl.pallas_call(
        functools.partial(local_kernel, coef),
        out_shape=(stat, stat, jax.ShapeDtypeStruct((2 * blocks, HEAD_DIM, QB), jnp.float32)),
        in_specs=[smem, smem, vmem, vmem, vmem],
        out_specs=(vmem, vmem, vmem),
        scratch_shapes=[
            pltpu.VMEM((tokens, width), jnp.bfloat16),
            pltpu.VMEM((2, HEAD_DIM, tokens), jnp.bfloat16),
        ],
        compiler_params=pltpu.CompilerParams(vmem_limit_bytes=32 << 20),
        cost_estimate=pl.CostEstimate(
            flops=4 * width * tokens * 1200, bytes_accessed=8 << 20, transcendentals=2 * tokens * 1200
        ),
    )(local_lo, local_n, qkv, start2, length2)
    return pl.pallas_call(
        functools.partial(halo_kernel, coef),
        out_shape=jax.ShapeDtypeStruct((width, tokens), jnp.bfloat16),
        in_specs=[smem, smem] + [vmem] * 8,
        out_specs=vmem,
        scratch_shapes=[
            pltpu.VMEM((2 * reach, width), jnp.bfloat16),
            pltpu.VMEM((2, HEAD_DIM, 2 * reach), jnp.bfloat16),
            pltpu.VMEM((2, 1, QB), jnp.float32),
            pltpu.VMEM((2, 1, QB), jnp.float32),
            pltpu.VMEM((2, HEAD_DIM, QB), jnp.float32),
        ],
        compiler_params=pltpu.CompilerParams(vmem_limit_bytes=32 << 20),
        cost_estimate=pl.CostEstimate(
            flops=4 * width * tokens * 300, bytes_accessed=8 << 20, transcendentals=2 * tokens * 300
        ),
    )(halo_lo, halo_n, qkv, left, right, start2, length2, m, l, acc)


MESH = pl.DeviceIdType.MESH


def tail_kernel(
    rows,
    cols,
    attended_ref,
    residual_ref,
    out_weight_hbm,
    merge_weight_hbm,
    far_weight_hbm,
    gain_ref,
    dest_line_ref,
    dest_column_ref,
    layer_ref,
    image_ref,
    att,
    weight,
    weight_t,
    merge_w,
    layer_rows,
    held,
    far_rows,
    merged,
    pick,
    sorted_rows,
    got_rows,
    load_sem,
    spread_send,
    spread_recv,
    back_send,
    back_recv,
    near_send,
    near_recv,
    sib_send,
    sib_recv,
    far_send,
    far_recv,
    row_send,
    row_recv,
):
    row = lax.axis_index("row")
    me = lax.axis_index("col")
    width, tokens = attended_ref.shape
    full = weight.shape[0]
    chunk = tokens // cols
    part = chunk // 4
    groups = tokens // 4
    share = groups // rows
    chips = cols // 2
    core = me % 2
    chip = me // 2
    sibling = me + 1 - 2 * core
    half = full // 2

    barrier = pltpu.get_barrier_semaphore()
    for k in range(1, cols):
        pl.semaphore_signal(
            barrier, inc=1, device_id={"col": (me + k) % cols}, device_id_type=MESH
        )
    for k in range(1, rows):
        pl.semaphore_signal(
            barrier, inc=1, device_id={"row": (row + k) % rows}, device_id_type=MESH
        )
    loads = [
        pltpu.make_async_copy(out_weight_hbm, weight, load_sem.at[0]),
        pltpu.make_async_copy(merge_weight_hbm, merge_w.at[0:width], load_sem.at[1]),
    ]
    pieces, _, piece = far_weight_hbm.shape
    used = -(-merge_w.shape[1] // piece)
    for r in range(used):
        at = min(r * piece, merge_w.shape[1] - piece)
        loads.append(
            pltpu.make_async_copy(
                far_weight_hbm.at[r],
                merge_w.at[width : 2 * width, at : at + piece],
                load_sem.at[2 + r],
            )
        )
    for r, load in enumerate(loads):
        if r != len(loads) - 1:
            load.start()
    pl.semaphore_wait(barrier, rows + cols - 2)

    spread = []
    for k in range(1, cols):
        to = (me + k) % cols
        copy = pltpu.make_async_remote_copy(
            src_ref=attended_ref.at[:, pl.ds(pl.multiple_of(to * chunk, chunk), chunk)],
            dst_ref=att.at[pl.ds(pl.multiple_of(me * width, 16), width)],
            send_sem=spread_send.at[k],
            recv_sem=spread_recv.at[k],
            device_id={"col": to},
            device_id_type=MESH,
        )
        copy.start()
        spread.append(copy)
    mine = pl.ds(pl.multiple_of(me * chunk, chunk), chunk)
    att[pl.ds(pl.multiple_of(me * width, 16), width), :] = attended_ref[:, mine]

    line = dest_line_ref[...]
    owner_line = line // groups
    owner_column = dest_column_ref[...] // groups
    down = lax.broadcasted_iota(jnp.int32, (groups, groups), 0)
    across = lax.broadcasted_iota(jnp.int32, (groups, groups), 1)
    earlier = (owner_column == owner_line) & (down < across)
    rank = jnp.sum(earlier.astype(jnp.int32), axis=0, keepdims=True)
    spot = owner_line * share + rank
    pick[...] = jnp.where(down == spot, 1.0, 0.0).astype(jnp.bfloat16)
    slot = line % groups
    extra = merged.shape[0] - width
    which = lax.broadcasted_iota(jnp.int32, (extra, groups), 0)
    digits = jnp.where(which == 0, slot // 16, jnp.where(which == 1, slot % 16, 0))
    merged[width:, :] = digits.astype(jnp.float32).astype(jnp.bfloat16)

    loads[0].wait()

    def turn(i, carry):
        at = pl.multiple_of(i * 128, 128)
        weight_t[pl.ds(at, 128), :] = jnp.transpose(weight[:, pl.ds(at, 128)])
        return carry

    lax.fori_loop(0, full // 128, turn, 0)
    for load in loads[1:-1]:
        load.wait()
    loads[-1].start()

    for copy in spread:
        copy.wait()
    strip = full // 4
    for i in range(4):
        at = i * strip
        projected = jnp.dot(
            weight_t[at : at + strip, :], att[...], preferred_element_type=jnp.float32
        )
        layer_rows[at : at + strip, :] = (
            residual_ref[at : at + strip, :].astype(jnp.float32) + projected
        ).astype(jnp.bfloat16)

    values32 = layer_rows[...].astype(jnp.float32)
    centre = jnp.sum(values32, axis=0, keepdims=True) * (1.0 / full)
    spread_of = jnp.sum(jnp.square(values32 - centre), axis=0, keepdims=True) * (1.0 / full)
    scale = lax.rsqrt(spread_of + 1e-06)
    normed = ((values32 - centre) * scale * gain_ref[...]).astype(jnp.bfloat16)
    here = lax.broadcasted_iota(jnp.int32, (chunk, chunk), 0)
    there = lax.broadcasted_iota(jnp.int32, (chunk, chunk), 1)
    order = jnp.where((here % 4) * part + here // 4 == there, 1.0, 0.0).astype(jnp.bfloat16)
    held[core] = jnp.dot(normed, order, preferred_element_type=jnp.float32).astype(jnp.bfloat16)

    goal = (chip + 1 + 2 * core) % chips
    near = []
    for h in range(2):
        span = pl.ds(h * half, half)
        copy = pltpu.make_async_remote_copy(
            src_ref=held.at[core, span],
            dst_ref=held.at[2 + core, span],
            send_sem=near_send.at[h],
            recv_sem=near_recv.at[core],
            device_id={"col": goal * 2 + h},
            device_id_type=MESH,
        )
        copy.start()
        near.append(copy)
    own = pltpu.make_async_remote_copy(
        src_ref=held.at[core],
        dst_ref=held.at[core],
        send_sem=sib_send.at[0],
        recv_sem=sib_recv.at[0],
        device_id={"col": sibling},
        device_id_type=MESH,
    )
    own.start()

    back = []
    for k in range(1, cols):
        to = (me + k) % cols
        copy = pltpu.make_async_remote_copy(
            src_ref=layer_rows.at[pl.ds(pl.multiple_of(to * width, 16), width)],
            dst_ref=layer_ref.at[:, mine],
            send_sem=back_send.at[k],
            recv_sem=back_recv.at[k],
            device_id={"col": to},
            device_id_type=MESH,
        )
        copy.start()
        back.append(copy)
    layer_ref[:, mine] = layer_rows[pl.ds(pl.multiple_of(me * width, 16), width), :]
    loads[-1].wait()

    passed = []
    my_half = pl.ds(pl.multiple_of(core * half, 16), half)
    for s in range(2):
        arrive = pltpu.make_async_remote_copy(
            src_ref=held.at[core, my_half],
            dst_ref=held.at[2 + s, my_half],
            send_sem=near_send.at[s],
            recv_sem=near_recv.at[s],
            device_id={"col": sibling},
            device_id_type=MESH,
        )
        arrive.wait_recv()
        copy = pltpu.make_async_remote_copy(
            src_ref=held.at[2 + s, my_half],
            dst_ref=held.at[2 + s, my_half],
            send_sem=sib_send.at[1 + s],
            recv_sem=sib_recv.at[1 + s],
            device_id={"col": sibling},
            device_id_type=MESH,
        )
        copy.start()
        passed.append(copy)
    for copy in near:
        copy.wait_send()
    own.wait()
    for copy in passed:
        copy.wait()

    total = None
    for j in range(4):
        side = jnp.concatenate(
            [held[s, :, j * part : (j + 1) * part] for s in range(4)], axis=1
        )
        term = jnp.dot(
            merge_w[:, j * full : (j + 1) * full], side, preferred_element_type=jnp.float32
        )
        total = term if total is None else total + term
    far_rows[...] = total[width:].astype(jnp.bfloat16)
    across_y = pltpu.make_async_remote_copy(
        src_ref=far_rows,
        dst_ref=merged.at[0:width, chunk : 2 * chunk],
        send_sem=far_send,
        recv_sem=far_recv,
        device_id={"col": (me + cols // 2) % cols},
        device_id_type=MESH,
    )
    across_y.start()
    merged[0:width, 0:chunk] = total[:width].astype(jnp.bfloat16)
    across_y.wait()

    sorted_rows[...] = lax.dot_general(
        pick[...], merged[...], (((1,), (1,)), ((), ())), preferred_element_type=jnp.float32
    ).astype(jnp.bfloat16)
    moves = []
    for k in range(1, rows):
        to = (row + k) % rows
        copy = pltpu.make_async_remote_copy(
            src_ref=sorted_rows.at[pl.ds(pl.multiple_of(to * share, share), share)],
            dst_ref=got_rows.at[pl.ds(pl.multiple_of(row * share, share), share)],
            send_sem=row_send.at[k],
            recv_sem=row_recv.at[k],
            device_id={"row": to},
            device_id_type=MESH,
        )
        copy.start()
        moves.append(copy)
    keep = pl.ds(pl.multiple_of(row * share, share), share)
    got_rows[keep, :] = sorted_rows[keep, :]
    for copy in moves:
        copy.wait()
    got = got_rows[...]
    target = got[:, width : width + 1].astype(jnp.float32) * 16.0 + got[
        :, width + 1 : width + 2
    ].astype(jnp.float32)
    put = jnp.where(target == across.astype(jnp.float32), 1.0, 0.0).astype(jnp.bfloat16)
    image_ref[...] = lax.dot_general(
        got, put, (((0,), (0,)), ((), ())), preferred_element_type=jnp.float32
    )[:width].astype(jnp.bfloat16)
    for copy in back:
        copy.wait()


def tail(attended, residual, out_weight, merge_weight, far_weight, gain, dest_slots, rows, cols):
    width, tokens = attended.shape
    full = out_weight.shape[0]
    chunk = tokens // cols
    groups = tokens // 4
    bf16 = jnp.bfloat16
    vmem = pl.BlockSpec(memory_space=pltpu.VMEM)
    hbm = pl.BlockSpec(memory_space=pl.ANY)
    dma = pltpu.SemaphoreType.DMA
    return pl.pallas_call(
        functools.partial(tail_kernel, rows, cols),
        out_shape=(
            jax.ShapeDtypeStruct((width, tokens), bf16),
            jax.ShapeDtypeStruct((width, groups), bf16),
        ),
        in_specs=[vmem, vmem, hbm, hbm, hbm, vmem, vmem, vmem],
        out_specs=(vmem, vmem),
        scratch_shapes=[
            pltpu.VMEM((full, chunk), bf16),
            pltpu.VMEM((full, full), bf16),
            pltpu.VMEM((full, full), bf16),
            pltpu.VMEM((2 * width, merge_weight.shape[1]), bf16),
            pltpu.VMEM((full, chunk), bf16),
            pltpu.VMEM((4, full, chunk), bf16),
            pltpu.VMEM((width, chunk), bf16),
            pltpu.VMEM((width + 16, groups), bf16),
            pltpu.VMEM((groups, groups), bf16),
            pltpu.VMEM((groups, width + 16), bf16),
            pltpu.VMEM((groups, width + 16), bf16),
            dma((2 + rows,)),
            dma((cols,)),
            dma((cols,)),
            dma((cols,)),
            dma((cols,)),
            dma((2,)),
            dma((2,)),
            dma((3,)),
            dma((3,)),
            dma,
            dma,
            dma((rows,)),
            dma((rows,)),
        ],
        compiler_params=pltpu.CompilerParams(
            collective_id=0, has_side_effects=True, vmem_limit_bytes=48 << 20
        ),
        cost_estimate=pl.CostEstimate(
            flops=8 * full * full * chunk, bytes_accessed=16 << 20, transcendentals=0
        ),
    )(
        attended,
        residual,
        out_weight,
        merge_weight,
        far_weight,
        gain[:, None],
        dest_slots[None, :],
        dest_slots[:, None],
    )


def body(qkv, residual_in, out_weight, merge_weight, merge_gain, image_groups, dest_row):
    tok_rows = qkv.shape[2]
    rows = lax.axis_size("row")
    cols = lax.axis_size("col")
    row_id = lax.axis_index("row")
    col_id = lax.axis_index("col")
    all_tokens = tok_rows * rows
    reach = tok_rows // 2

    left = lax.ppermute(
        qkv[1:, :, tok_rows - reach :], "row", [(i, i + 1) for i in range(rows - 1)]
    )
    right = lax.ppermute(qkv[1:, :, :reach], "row", [(i + 1, i) for i in range(rows - 1)])
    residual = lax.all_to_all(residual_in, "col", 1, 0, tiled=True)

    lanes = merge_weight.shape[1]
    piece = -(-lanes // (128 * rows)) * 128
    piece_at = jnp.minimum(row_id * piece, lanes - piece)
    slice_here = lax.dynamic_slice_in_dim(merge_weight, piece_at, piece, 1)
    slice_far = lax.ppermute(slice_here, "col", [(i, (i + cols // 2) % cols) for i in range(cols)])
    far_weight = lax.all_gather(slice_far, "row", axis=0)

    chips = cols // 2
    chip = col_id // 2
    before, after, across = (chip + chips - 1) % chips, (chip + 1) % chips, (chip + 2) % chips
    met = jnp.stack(
        [
            2 * chip,
            2 * chip + 1,
            2 * before,
            2 * after + 1,
            2 * across,
            2 * across + 1,
            2 * after,
            2 * before + 1,
        ]
    )
    dest_slots = jnp.take(dest_row.reshape(cols, -1), met, axis=0).reshape(-1)

    attended = attention(qkv, left, right, image_groups, row_id, all_tokens)
    return tail(
        attended, residual, out_weight, merge_weight, far_weight, merge_gain, dest_slots, rows, cols
    )


def solution(mesh):
    return jax.shard_map(
        body,
        mesh=mesh,
        in_specs=(P(None, "col", "row"), P("col", "row"), P(), P("col", None), P(), P(), P("row")),
        out_specs=(P("col", "row"), P("col", "row")),
        check_vma=False,
    )
```

```python
import functools
import math

import jax
import jax.numpy as jnp
from jax import lax
from jax.experimental import pallas as pl
from jax.experimental.pallas import tpu as pltpu
from jax.sharding import PartitionSpec as P

HEAD_DIM = 88
QB = 256
KB = 256
NEAR = 2
NEG = -1e30
MESH = pl.DeviceIdType.MESH


def tile_step(kt, v0, v1, qcat, ok, coef, row, m_ref, l_ref, acc_ref):
    scores = lax.dot_general(
        kt, qcat, (((1,), (0,)), ((), ())), preferred_element_type=jnp.float32
    )
    width = qcat.shape[1] // 2
    for head in range(2):
        part = jnp.where(ok, scores[:, head * width : (head + 1) * width], NEG)
        old = m_ref[row + head]
        new = jnp.maximum(old, jnp.max(part, axis=0, keepdims=True))
        fade = jnp.exp2((old - new) * coef)
        expo = jnp.exp2(part * coef - new * coef)
        l_ref[row + head] = l_ref[row + head] * fade + jnp.sum(expo, axis=0, keepdims=True)
        m_ref[row + head] = new
        values = v1 if head else v0
        acc_ref[row + head] = acc_ref[row + head] * fade + lax.dot_general(
            values,
            expo.astype(jnp.bfloat16),
            (((1,), (0,)), ((), ())),
            preferred_element_type=jnp.float32,
        )


def split_heads(values):
    wide = values.astype(jnp.float32)
    return wide[:HEAD_DIM].astype(jnp.bfloat16), wide[HEAD_DIM:].astype(jnp.bfloat16)


def query_pair(block):
    feature = lax.broadcasted_iota(jnp.int32, block.shape, 0)
    zero = jnp.zeros_like(block)
    return jnp.concatenate(
        [jnp.where(feature < HEAD_DIM, block, zero), jnp.where(feature < HEAD_DIM, zero, block)],
        axis=1,
    )


def head_kernel(
    rows,
    cols,
    coef,
    qkv_hbm,
    residual_hbm,
    merge_weight_hbm,
    groups_line_ref,
    groups_column_ref,
    left_hbm,
    right_hbm,
    spread_hbm,
    far_hbm,
    m_ref,
    l_ref,
    acc_ref,
    kt,
    vt,
    bound_ref,
    qkv,
    load_sem,
    halo_send,
    halo_recv,
    res_send,
    res_recv,
    far_send,
    far_recv,
):
    row = lax.axis_index("row")
    me = lax.axis_index("col")
    _, width, tokens = qkv.shape
    reach = left_hbm.shape[2]
    blocks = tokens // QB
    chunk = tokens // cols
    full = spread_hbm.shape[0]
    barrier = pltpu.get_barrier_semaphore()
    after = (row + 1) % rows
    before = (row + rows - 1) % rows
    for other in (after, before):
        pl.semaphore_signal(barrier, inc=1, device_id={"row": other}, device_id_type=MESH)
    for k in range(1, cols):
        pl.semaphore_signal(
            barrier, inc=1, device_id={"col": (me + k) % cols}, device_id_type=MESH
        )
    loads = [
        pltpu.make_async_copy(qkv_hbm.at[i], qkv.at[i], load_sem.at[i]) for i in range(3)
    ]
    for load in loads:
        load.start()
    mine = pl.ds(pl.multiple_of(me * chunk, chunk), chunk)
    place = pl.ds(pl.multiple_of(me * width, 16), width)
    keep = pltpu.make_async_copy(residual_hbm.at[:, mine], spread_hbm.at[place], load_sem.at[3])
    keep.start()
    pl.semaphore_wait(barrier, cols + 1)

    sent = []
    for side, (other, target, at) in enumerate(
        ((after, left_hbm, tokens - reach), (before, right_hbm, 0))
    ):
        for i in range(2):
            sent.append(
                pltpu.make_async_remote_copy(
                    src_ref=qkv_hbm.at[1 + i, :, at : at + reach],
                    dst_ref=target.at[i],
                    send_sem=halo_send.at[2 * side + i],
                    recv_sem=halo_recv.at[2 * side + i],
                    device_id={"row": other},
                    device_id_type=MESH,
                )
            )
    for k in range(1, cols):
        to = (me + k) % cols
        sent.append(
            pltpu.make_async_remote_copy(
                src_ref=residual_hbm.at[:, pl.ds(pl.multiple_of(to * chunk, chunk), chunk)],
                dst_ref=spread_hbm.at[place],
                send_sem=res_send.at[k],
                recv_sem=res_recv.at[k],
                device_id={"col": to},
                device_id_type=MESH,
            )
        )
    part = row // (rows // 4)
    sent.append(
        pltpu.make_async_remote_copy(
            src_ref=merge_weight_hbm.at[:, pl.ds(pl.multiple_of(part * full, 128), full)],
            dst_ref=far_hbm,
            send_sem=far_send,
            recv_sem=far_recv,
            device_id={"col": (me + cols // 2) % cols},
            device_id_type=MESH,
        )
    )
    for copy in sent:
        copy.start()

    images = groups_line_ref.shape[1]
    first = lax.broadcasted_iota(jnp.int32, (images, images), 0)
    second = lax.broadcasted_iota(jnp.int32, (images, images), 1)
    size = groups_column_ref[...] * 4
    begin = (
        jnp.sum(
            jnp.where(second < first, groups_line_ref[...], 0), axis=1, keepdims=True
        )
        * 4
        - row * tokens
    )
    for load in loads:
        load.wait()

    def prepare(b, carry):
        at = pl.multiple_of(b * QB, QB)
        token = lax.broadcasted_iota(jnp.int32, (images, QB), 1) + at
        inside = (token >= begin) & (token < begin + size)
        bound_ref[0:1, pl.ds(at, QB)] = jnp.sum(jnp.where(inside, begin, 0), axis=0, keepdims=True)
        bound_ref[1:2, pl.ds(at, QB)] = jnp.sum(jnp.where(inside, size, 0), axis=0, keepdims=True)
        kt[pl.ds(at, QB), :] = jnp.transpose(qkv[1, :, pl.ds(at, QB)])
        v0, v1 = split_heads(qkv[2, :, pl.ds(at, QB)])
        vt[0, :, pl.ds(at, QB)] = v0
        vt[1, :, pl.ds(at, QB)] = v1
        return carry

    lax.fori_loop(0, blocks, prepare, 0)

    def per_block(b, carry):
        at = pl.multiple_of(b * QB, QB)
        qcat = query_pair(qkv[0, :, pl.ds(at, QB)])
        start = bound_ref[0:1, pl.ds(at, QB)]
        length = bound_ref[1:2, pl.ds(at, QB)]
        row_at = b * 2
        for head in range(2):
            m_ref[row_at + head] = jnp.full((1, QB), NEG, jnp.float32)
            l_ref[row_at + head] = jnp.zeros((1, QB), jnp.float32)
            acc_ref[row_at + head] = jnp.zeros((HEAD_DIM, QB), jnp.float32)

        def per_tile(t, inner):
            key = pl.multiple_of(t * KB, KB)
            spot = lax.broadcasted_iota(jnp.int32, (KB, QB), 0) + (key - start)
            ok = (spot >= 0) & (spot < length)
            tile_step(
                kt[pl.ds(key, KB), :],
                vt[0, :, pl.ds(key, KB)],
                vt[1, :, pl.ds(key, KB)],
                qcat,
                ok,
                coef,
                row_at,
                m_ref,
                l_ref,
                acc_ref,
            )
            return inner

        lax.fori_loop(
            jnp.maximum(b - NEAR, 0), jnp.minimum(b + NEAR + 1, blocks), per_tile, 0
        )
        return carry

    lax.fori_loop(0, blocks, per_block, 0)
    keep.wait()
    for copy in sent:
        copy.wait()


def far_kernel(
    coef,
    groups_ref,
    row_ref,
    q_ref,
    left_ref,
    right_ref,
    bound_ref,
    m_in,
    l_in,
    acc_in,
    kt_in,
    vt_in,
    out_ref,
    low_ref,
    high_ref,
    kt,
    vt,
    m_ref,
    l_ref,
    acc_ref,
    sem,
):
    reach = left_ref.shape[2]
    width, tokens = q_ref.shape
    blocks = tokens // QB
    base = row_ref[0] * tokens
    moves = [
        pltpu.make_async_copy(kt_in, kt.at[reach : reach + tokens], sem.at[0]),
        pltpu.make_async_copy(vt_in, vt.at[:, :, reach : reach + tokens], sem.at[1]),
    ]
    for move in moves:
        move.start()

    def find(b, state):
        image, begin = state
        token = base + b * QB

        def past(at):
            def more(s):
                return s[1] + groups_ref[s[0]] * 4 <= at

            def step(s):
                return s[0] + 1, s[1] + groups_ref[s[0]] * 4

            return more, step

        image, begin = lax.while_loop(*past(token), (image, begin))
        low_ref[b] = begin - base
        image, begin = lax.while_loop(*past(token + QB - 1), (image, begin))
        high_ref[b] = begin + groups_ref[image] * 4 - base
        return image, begin

    lax.fori_loop(0, blocks, find, (jnp.int32(0), jnp.int32(0)))
    for i in range(reach // KB):
        for needed, source, at in (
            (low_ref[0] < (i + 1) * KB - reach, left_ref, 0),
            (high_ref[blocks - 1] > tokens + i * KB, right_ref, reach + tokens),
        ):

            @pl.when(needed)
            def _():
                span = slice(i * KB, (i + 1) * KB)
                to = slice(at + i * KB, at + (i + 1) * KB)
                kt[to, :] = jnp.transpose(source[0, :, span])
                v0, v1 = split_heads(source[1, :, span])
                vt[0, :, to] = v0
                vt[1, :, to] = v1

    for move in moves:
        move.wait()

    def per_block(b, carry):
        at = pl.multiple_of(b * QB, QB)
        row_at = b * 2
        near_low = jnp.maximum(b - NEAR, 0) * QB
        near_high = jnp.minimum(b + NEAR + 1, blocks) * QB
        below = jnp.maximum((near_low - low_ref[b] + KB - 1) // KB, 0)
        above = jnp.maximum((high_ref[b] - near_high + KB - 1) // KB, 0)
        for head in range(2):
            m_ref[head] = m_in[row_at + head]
            l_ref[head] = l_in[row_at + head]
            acc_ref[head] = acc_in[row_at + head]

        @pl.when(below + above > 0)
        def _():
            qcat = query_pair(q_ref[:, pl.ds(at, QB)])
            start = bound_ref[0:1, pl.ds(at, QB)]
            length = bound_ref[1:2, pl.ds(at, QB)]

            def per_tile(t, inner):
                key = jnp.where(
                    t < below, near_low - (t + 1) * KB, near_high + (t - below) * KB
                )
                spot = lax.broadcasted_iota(jnp.int32, (KB, QB), 0) + (key - start)
                ok = (spot >= 0) & (spot < length)
                slot = pl.multiple_of(key + reach, KB)
                tile_step(
                    kt[pl.ds(slot, KB), :],
                    vt[0, :, pl.ds(slot, KB)],
                    vt[1, :, pl.ds(slot, KB)],
                    qcat,
                    ok,
                    coef,
                    0,
                    m_ref,
                    l_ref,
                    acc_ref,
                )
                return inner

            lax.fori_loop(0, below + above, per_tile, 0)

        both = [acc_ref[head] / l_ref[head] for head in range(2)]
        out_ref[:, pl.ds(at, QB)] = jnp.concatenate(both, axis=0).astype(jnp.bfloat16)
        return carry

    lax.fori_loop(0, blocks, per_block, 0)


def attention(qkv, residual, merge_weight, image_groups, row_id, full, rows, cols):
    _, width, tokens = qkv.shape
    reach = tokens // 2
    blocks = tokens // QB
    chunk = tokens // cols
    bf16, f32 = jnp.bfloat16, jnp.float32
    coef = math.log2(math.e) / math.sqrt(HEAD_DIM)
    smem = pl.BlockSpec(memory_space=pltpu.SMEM)
    vmem = pl.BlockSpec(memory_space=pltpu.VMEM)
    hbm = pl.BlockSpec(memory_space=pl.ANY)
    dma = pltpu.SemaphoreType.DMA
    halo = jax.ShapeDtypeStruct((2, width, reach), bf16)
    stat = jax.ShapeDtypeStruct((2 * blocks, 1, QB), f32)
    left, right, spread, far, m, l, acc, kt, vt, bound = pl.pallas_call(
        functools.partial(head_kernel, rows, cols, coef),
        out_shape=(
            halo,
            halo,
            jax.ShapeDtypeStruct((full, chunk), bf16),
            jax.ShapeDtypeStruct((width, full), bf16),
            stat,
            stat,
            jax.ShapeDtypeStruct((2 * blocks, HEAD_DIM, QB), f32),
            jax.ShapeDtypeStruct((tokens, width), bf16),
            jax.ShapeDtypeStruct((2, HEAD_DIM, tokens), bf16),
            jax.ShapeDtypeStruct((8, tokens), jnp.int32),
        ),
        in_specs=[hbm, hbm, hbm, vmem, vmem],
        out_specs=(hbm, hbm, hbm, hbm, vmem, vmem, vmem, vmem, vmem, vmem),
        scratch_shapes=[
            pltpu.VMEM((3, width, tokens), bf16),
            dma((4,)),
            dma((4,)),
            dma((4,)),
            dma((cols,)),
            dma((cols,)),
            dma,
            dma,
        ],
        compiler_params=pltpu.CompilerParams(
            collective_id=1, has_side_effects=True, vmem_limit_bytes=56 << 20
        ),
    )(qkv, residual, merge_weight, image_groups[None, :], image_groups[:, None])
    attended = pl.pallas_call(
        functools.partial(far_kernel, coef),
        out_shape=jax.ShapeDtypeStruct((width, tokens), bf16),
        in_specs=[smem, smem] + [vmem] * 7 + [hbm] * 2,
        out_specs=vmem,
        scratch_shapes=[
            pltpu.SMEM((blocks,), jnp.int32),
            pltpu.SMEM((blocks,), jnp.int32),
            pltpu.VMEM((2 * reach + tokens, width), bf16),
            pltpu.VMEM((2, HEAD_DIM, 2 * reach + tokens), bf16),
            pltpu.VMEM((2, 1, QB), f32),
            pltpu.VMEM((2, 1, QB), f32),
            pltpu.VMEM((2, HEAD_DIM, QB), f32),
            dma((2,)),
        ],
        compiler_params=pltpu.CompilerParams(vmem_limit_bytes=56 << 20),
    )(image_groups, row_id[None], qkv[0], left, right, bound, m, l, acc, kt, vt)
    return attended, spread, far


def tail_kernel(
    rows,
    cols,
    attended_ref,
    residual_ref,
    out_weight_hbm,
    merge_weight_hbm,
    far_weight_hbm,
    gain_ref,
    dest_line_ref,
    dest_column_ref,
    layer_ref,
    image_ref,
    att,
    weight,
    weight_t,
    merge_w,
    layer_rows,
    held,
    far_rows,
    merged,
    pick,
    sorted_rows,
    got_rows,
    load_sem,
    spread_send,
    spread_recv,
    back_send,
    back_recv,
    near_send,
    near_recv,
    sib_send,
    sib_recv,
    far_send,
    far_recv,
    row_send,
    row_recv,
    far_w_send,
    far_w_recv,
    gain_column,
):
    row = lax.axis_index("row")
    me = lax.axis_index("col")
    width, tokens = attended_ref.shape
    full = weight.shape[0]
    chunk = tokens // cols
    part = chunk // 4
    groups = tokens // 4
    share = groups // rows
    chips = cols // 2
    core = me % 2
    chip = me // 2
    sibling = me + 1 - 2 * core
    half = full // 2

    barrier = pltpu.get_barrier_semaphore()
    for k in range(1, cols):
        pl.semaphore_signal(
            barrier, inc=1, device_id={"col": (me + k) % cols}, device_id_type=MESH
        )
    for k in range(1, rows):
        pl.semaphore_signal(
            barrier, inc=1, device_id={"row": (row + k) % rows}, device_id_type=MESH
        )
    loads = [
        pltpu.make_async_copy(out_weight_hbm, weight, load_sem.at[0]),
        pltpu.make_async_copy(merge_weight_hbm, merge_w.at[0:width], load_sem.at[1]),
    ]
    line_up = rows // 4
    part_at = row // line_up
    far_at = pl.ds(pl.multiple_of(part_at * full, 128), full)
    far_place = merge_w.at[width : 2 * width, far_at]
    loads.append(pltpu.make_async_copy(far_weight_hbm, far_place, load_sem.at[2]))
    for load in loads:
        load.start()
    pl.semaphore_wait(barrier, rows + cols - 2)

    spread = []
    for k in range(1, cols):
        to = (me + k) % cols
        copy = pltpu.make_async_remote_copy(
            src_ref=attended_ref.at[:, pl.ds(pl.multiple_of(to * chunk, chunk), chunk)],
            dst_ref=att.at[pl.ds(pl.multiple_of(me * width, 16), width)],
            send_sem=spread_send.at[k],
            recv_sem=spread_recv.at[k],
            device_id={"col": to},
            device_id_type=MESH,
        )
        copy.start()
        spread.append(copy)
    gather = []
    for k in range(1, 4):
        copy = pltpu.make_async_remote_copy(
            src_ref=far_weight_hbm,
            dst_ref=far_place,
            send_sem=far_w_send.at[k],
            recv_sem=far_w_recv.at[k],
            device_id={"row": (row + k * line_up) % rows},
            device_id_type=MESH,
        )
        copy.start()
        gather.append(copy)
    mine = pl.ds(pl.multiple_of(me * chunk, chunk), chunk)
    att[pl.ds(pl.multiple_of(me * width, 16), width), :] = attended_ref[:, mine]

    line = dest_line_ref[...]
    owner_line = line // groups
    owner_column = dest_column_ref[...] // groups
    down = lax.broadcasted_iota(jnp.int32, (groups, groups), 0)
    across = lax.broadcasted_iota(jnp.int32, (groups, groups), 1)
    earlier = (owner_column == owner_line) & (down < across)
    rank = jnp.sum(earlier.astype(jnp.int32), axis=0, keepdims=True)
    spot = owner_line * share + rank
    pick[...] = jnp.where(down == spot, 1.0, 0.0).astype(jnp.bfloat16)
    slot = line % groups
    extra = merged.shape[0] - width
    which = lax.broadcasted_iota(jnp.int32, (extra, groups), 0)
    digits = jnp.where(which == 0, slot // 16, jnp.where(which == 1, slot % 16, 0))
    merged[width:, :] = digits.astype(jnp.float32).astype(jnp.bfloat16)

    loads[0].wait()

    def turn(i, carry):
        at = pl.multiple_of(i * 128, 128)
        weight_t[pl.ds(at, 128), :] = jnp.transpose(weight[:, pl.ds(at, 128)])
        return carry

    lax.fori_loop(0, full // 128, turn, 0)
    gain_wide = jnp.broadcast_to(gain_ref[...], (8, full))
    gain_column[...] = jnp.transpose(gain_wide)
    for load in loads[1:]:
        load.wait()

    for copy in spread:
        copy.wait()
    strip = full // 4
    for i in range(4):
        at = i * strip
        projected = jnp.dot(
            weight_t[at : at + strip, :], att[...], preferred_element_type=jnp.float32
        )
        layer_rows[at : at + strip, :] = (
            residual_ref[at : at + strip, :].astype(jnp.float32) + projected
        ).astype(jnp.bfloat16)

    values32 = layer_rows[...].astype(jnp.float32)
    centre = jnp.sum(values32, axis=0, keepdims=True) * (1.0 / full)
    spread_of = jnp.sum(jnp.square(values32 - centre), axis=0, keepdims=True) * (1.0 / full)
    scale = lax.rsqrt(spread_of + 1e-06)
    normed = ((values32 - centre) * scale * gain_column[:, 0:1]).astype(jnp.bfloat16)
    here = lax.broadcasted_iota(jnp.int32, (chunk, chunk), 0)
    there = lax.broadcasted_iota(jnp.int32, (chunk, chunk), 1)
    order = jnp.where((here % 4) * part + here // 4 == there, 1.0, 0.0).astype(jnp.bfloat16)
    held[core] = jnp.dot(normed, order, preferred_element_type=jnp.float32).astype(jnp.bfloat16)

    goal = (chip + 1 + 2 * core) % chips
    near = []
    for h in range(2):
        span = pl.ds(h * half, half)
        copy = pltpu.make_async_remote_copy(
            src_ref=held.at[core, span],
            dst_ref=held.at[2 + core, span],
            send_sem=near_send.at[h],
            recv_sem=near_recv.at[core],
            device_id={"col": goal * 2 + h},
            device_id_type=MESH,
        )
        copy.start()
        near.append(copy)
    own = pltpu.make_async_remote_copy(
        src_ref=held.at[core],
        dst_ref=held.at[core],
        send_sem=sib_send.at[0],
        recv_sem=sib_recv.at[0],
        device_id={"col": sibling},
        device_id_type=MESH,
    )
    own.start()

    passed = []
    my_half = pl.ds(pl.multiple_of(core * half, 16), half)
    for s in range(2):
        arrive = pltpu.make_async_remote_copy(
            src_ref=held.at[core, my_half],
            dst_ref=held.at[2 + s, my_half],
            send_sem=near_send.at[s],
            recv_sem=near_recv.at[s],
            device_id={"col": sibling},
            device_id_type=MESH,
        )
        arrive.wait_recv()
        copy = pltpu.make_async_remote_copy(
            src_ref=held.at[2 + s, my_half],
            dst_ref=held.at[2 + s, my_half],
            send_sem=sib_send.at[1 + s],
            recv_sem=sib_recv.at[1 + s],
            device_id={"col": sibling},
            device_id_type=MESH,
        )
        copy.start()
        passed.append(copy)
    for copy in near:
        copy.wait_send()
    own.wait()
    for copy in passed:
        copy.wait()

    back = []
    for k in range(1, cols):
        to = (me + k) % cols
        copy = pltpu.make_async_remote_copy(
            src_ref=layer_rows.at[pl.ds(pl.multiple_of(to * width, 16), width)],
            dst_ref=layer_ref.at[:, mine],
            send_sem=back_send.at[k],
            recv_sem=back_recv.at[k],
            device_id={"col": to},
            device_id_type=MESH,
        )
        copy.start()
        back.append(copy)
    layer_ref[:, mine] = layer_rows[pl.ds(pl.multiple_of(me * width, 16), width), :]
    for copy in gather:
        copy.wait()

    total = None
    for j in range(4):
        side = jnp.concatenate(
            [held[s, :, j * part : (j + 1) * part] for s in range(4)], axis=1
        )
        term = jnp.dot(
            merge_w[:, j * full : (j + 1) * full], side, preferred_element_type=jnp.float32
        )
        total = term if total is None else total + term
    far_rows[...] = total[width:].astype(jnp.bfloat16)
    across_y = pltpu.make_async_remote_copy(
        src_ref=far_rows,
        dst_ref=merged.at[0:width, chunk : 2 * chunk],
        send_sem=far_send,
        recv_sem=far_recv,
        device_id={"col": (me + cols // 2) % cols},
        device_id_type=MESH,
    )
    across_y.start()
    merged[0:width, 0:chunk] = total[:width].astype(jnp.bfloat16)
    across_y.wait()

    sorted_rows[...] = lax.dot_general(
        pick[...], merged[...], (((1,), (1,)), ((), ())), preferred_element_type=jnp.float32
    ).astype(jnp.bfloat16)
    moves = []
    for k in range(1, rows):
        to = (row + k) % rows
        copy = pltpu.make_async_remote_copy(
            src_ref=sorted_rows.at[pl.ds(pl.multiple_of(to * share, share), share)],
            dst_ref=got_rows.at[pl.ds(pl.multiple_of(row * share, share), share)],
            send_sem=row_send.at[k],
            recv_sem=row_recv.at[k],
            device_id={"row": to},
            device_id_type=MESH,
        )
        copy.start()
        moves.append(copy)
    keep = pl.ds(pl.multiple_of(row * share, share), share)
    got_rows[keep, :] = sorted_rows[keep, :]
    for copy in moves:
        copy.wait()
    got = got_rows[...]
    target = got[:, width : width + 1].astype(jnp.float32) * 16.0 + got[
        :, width + 1 : width + 2
    ].astype(jnp.float32)
    put = jnp.where(target == across.astype(jnp.float32), 1.0, 0.0).astype(jnp.bfloat16)
    image_ref[...] = lax.dot_general(
        got, put, (((0,), (0,)), ((), ())), preferred_element_type=jnp.float32
    )[:width].astype(jnp.bfloat16)
    for copy in back:
        copy.wait()


def tail(attended, residual, out_weight, merge_weight, far_weight, gain, dest_slots, rows, cols):
    width, tokens = attended.shape
    full = out_weight.shape[0]
    chunk = tokens // cols
    groups = tokens // 4
    bf16 = jnp.bfloat16
    vmem = pl.BlockSpec(memory_space=pltpu.VMEM)
    hbm = pl.BlockSpec(memory_space=pl.ANY)
    dma = pltpu.SemaphoreType.DMA
    return pl.pallas_call(
        functools.partial(tail_kernel, rows, cols),
        out_shape=(
            jax.ShapeDtypeStruct((width, tokens), bf16),
            jax.ShapeDtypeStruct((width, groups), bf16),
        ),
        in_specs=[vmem, vmem, hbm, hbm, hbm, vmem, vmem, vmem],
        out_specs=(vmem, vmem),
        scratch_shapes=[
            pltpu.VMEM((full, chunk), bf16),
            pltpu.VMEM((full, full), bf16),
            pltpu.VMEM((full, full), bf16),
            pltpu.VMEM((2 * width, merge_weight.shape[1]), bf16),
            pltpu.VMEM((full, chunk), bf16),
            pltpu.VMEM((4, full, chunk), bf16),
            pltpu.VMEM((width, chunk), bf16),
            pltpu.VMEM((width + 16, groups), bf16),
            pltpu.VMEM((groups, groups), bf16),
            pltpu.VMEM((groups, width + 16), bf16),
            pltpu.VMEM((groups, width + 16), bf16),
            dma((3,)),
            dma((cols,)),
            dma((cols,)),
            dma((cols,)),
            dma((cols,)),
            dma((2,)),
            dma((2,)),
            dma((3,)),
            dma((3,)),
            dma,
            dma,
            dma((rows,)),
            dma((rows,)),
            dma((4,)),
            dma((4,)),
            pltpu.VMEM((full, 8), jnp.float32),
        ],
        compiler_params=pltpu.CompilerParams(
            collective_id=0, has_side_effects=True, vmem_limit_bytes=60 << 20
        ),
        cost_estimate=pl.CostEstimate(
            flops=8 * full * full * chunk, bytes_accessed=16 << 20, transcendentals=0
        ),
    )(
        attended,
        residual,
        out_weight,
        merge_weight,
        far_weight,
        gain[None, :],
        dest_slots[None, :],
        dest_slots[:, None],
    )


def body(qkv, residual_in, out_weight, merge_weight, merge_gain, image_groups, dest_row):
    rows = lax.axis_size("row")
    cols = lax.axis_size("col")
    row_id = lax.axis_index("row")
    col_id = lax.axis_index("col")

    chips = cols // 2
    chip = col_id // 2
    before, after, across = (chip + chips - 1) % chips, (chip + 1) % chips, (chip + 2) % chips
    met = jnp.stack(
        [
            2 * chip,
            2 * chip + 1,
            2 * before,
            2 * after + 1,
            2 * across,
            2 * across + 1,
            2 * after,
            2 * before + 1,
        ]
    )
    dest_slots = jnp.take(dest_row.reshape(cols, -1), met, axis=0).reshape(-1)

    attended, residual, far_weight = attention(
        qkv, residual_in, merge_weight, image_groups, row_id, out_weight.shape[0], rows, cols
    )
    return tail(
        attended, residual, out_weight, merge_weight, far_weight, merge_gain, dest_slots, rows, cols
    )


def solution(mesh):
    return jax.shard_map(
        body,
        mesh=mesh,
        in_specs=(P(None, "col", "row"), P("col", "row"), P(), P("col", None), P(), P(), P("row")),
        out_specs=(P("col", "row"), P("col", "row")),
        check_vma=False,
    )
```

```python
import functools
import math

import jax
import jax.numpy as jnp
from jax import lax
from jax.experimental import pallas as pl
from jax.experimental.pallas import tpu as pltpu
from jax.sharding import PartitionSpec as P

HEAD_DIM = 88
QB = 256
KB = 256
NEAR = 2
NEG = -1e30
MESH = pl.DeviceIdType.MESH


def tile_step(kt, v0, v1, qcat, ok, coef, row, m_ref, l_ref, acc_ref):
    scores = lax.dot_general(
        kt, qcat, (((1,), (0,)), ((), ())), preferred_element_type=jnp.float32
    )
    width = qcat.shape[1] // 2
    for head in range(2):
        part = jnp.where(ok, scores[:, head * width : (head + 1) * width], NEG)
        old = m_ref[row + head]
        new = jnp.maximum(old, jnp.max(part, axis=0, keepdims=True))
        fade = jnp.exp2((old - new) * coef)
        expo = jnp.exp2(part * coef - new * coef)
        l_ref[row + head] = l_ref[row + head] * fade + jnp.sum(expo, axis=0, keepdims=True)
        m_ref[row + head] = new
        values = v1 if head else v0
        acc_ref[row + head] = acc_ref[row + head] * fade + lax.dot_general(
            values,
            expo.astype(jnp.bfloat16),
            (((1,), (0,)), ((), ())),
            preferred_element_type=jnp.float32,
        )


def split_heads(values):
    wide = values.astype(jnp.float32)
    return wide[:HEAD_DIM].astype(jnp.bfloat16), wide[HEAD_DIM:].astype(jnp.bfloat16)


def query_pair(block):
    feature = lax.broadcasted_iota(jnp.int32, block.shape, 0)
    zero = jnp.zeros_like(block)
    return jnp.concatenate(
        [jnp.where(feature < HEAD_DIM, block, zero), jnp.where(feature < HEAD_DIM, zero, block)],
        axis=1,
    )


def head_kernel(
    rows,
    cols,
    coef,
    qkv_hbm,
    residual_hbm,
    merge_weight_hbm,
    groups_line_ref,
    left_hbm,
    right_hbm,
    spread_hbm,
    far_hbm,
    m_ref,
    l_ref,
    acc_ref,
    kt,
    vt,
    bound_ref,
    qkv,
    load_sem,
    halo_send,
    halo_recv,
    res_send,
    res_recv,
    far_send,
    far_recv,
):
    row = lax.axis_index("row")
    me = lax.axis_index("col")
    _, width, tokens = qkv.shape
    reach = left_hbm.shape[2]
    blocks = tokens // QB
    chunk = tokens // cols
    full = spread_hbm.shape[0]
    barrier = pltpu.get_barrier_semaphore()
    after = (row + 1) % rows
    before = (row + rows - 1) % rows
    for other in (after, before):
        pl.semaphore_signal(barrier, inc=1, device_id={"row": other}, device_id_type=MESH)
    for k in range(1, cols):
        pl.semaphore_signal(
            barrier, inc=1, device_id={"col": (me + k) % cols}, device_id_type=MESH
        )
    loads = [
        pltpu.make_async_copy(qkv_hbm.at[i], qkv.at[i], load_sem.at[i]) for i in range(3)
    ]
    for load in loads:
        load.start()
    mine = pl.ds(pl.multiple_of(me * chunk, chunk), chunk)
    place = pl.ds(pl.multiple_of(me * width, 16), width)
    keep = pltpu.make_async_copy(residual_hbm.at[:, mine], spread_hbm.at[place], load_sem.at[3])
    keep.start()
    pl.semaphore_wait(barrier, cols + 1)

    sent = []
    for side, (other, target, at) in enumerate(
        ((after, left_hbm, tokens - reach), (before, right_hbm, 0))
    ):
        for i in range(2):
            sent.append(
                pltpu.make_async_remote_copy(
                    src_ref=qkv_hbm.at[1 + i, :, at : at + reach],
                    dst_ref=target.at[i],
                    send_sem=halo_send.at[2 * side + i],
                    recv_sem=halo_recv.at[2 * side + i],
                    device_id={"row": other},
                    device_id_type=MESH,
                )
            )
    for k in range(1, cols):
        to = (me + k) % cols
        sent.append(
            pltpu.make_async_remote_copy(
                src_ref=residual_hbm.at[:, pl.ds(pl.multiple_of(to * chunk, chunk), chunk)],
                dst_ref=spread_hbm.at[place],
                send_sem=res_send.at[k],
                recv_sem=res_recv.at[k],
                device_id={"col": to},
                device_id_type=MESH,
            )
        )
    part = row // (rows // 4)
    sent.append(
        pltpu.make_async_remote_copy(
            src_ref=merge_weight_hbm.at[:, pl.ds(pl.multiple_of(part * full, 128), full)],
            dst_ref=far_hbm,
            send_sem=far_send,
            recv_sem=far_recv,
            device_id={"col": (me + cols // 2) % cols},
            device_id_type=MESH,
        )
    )
    for copy in sent:
        copy.start()

    images = groups_line_ref.shape[1]
    first = lax.broadcasted_iota(jnp.int32, (images, images), 0)
    second = lax.broadcasted_iota(jnp.int32, (images, images), 1)
    size = (
        jnp.sum(jnp.where(second == first, groups_line_ref[...], 0), axis=1, keepdims=True) * 4
    )
    begin = (
        jnp.sum(
            jnp.where(second < first, groups_line_ref[...], 0), axis=1, keepdims=True
        )
        * 4
        - row * tokens
    )
    for load in loads:
        load.wait()

    def prepare(b, carry):
        at = pl.multiple_of(b * QB, QB)
        token = lax.broadcasted_iota(jnp.int32, (images, QB), 1) + at
        inside = (token >= begin) & (token < begin + size)
        bound_ref[0:1, pl.ds(at, QB)] = jnp.sum(jnp.where(inside, begin, 0), axis=0, keepdims=True)
        bound_ref[1:2, pl.ds(at, QB)] = jnp.sum(jnp.where(inside, size, 0), axis=0, keepdims=True)
        kt[pl.ds(at, QB), :] = jnp.transpose(qkv[1, :, pl.ds(at, QB)])
        v0, v1 = split_heads(qkv[2, :, pl.ds(at, QB)])
        vt[0, :, pl.ds(at, QB)] = v0
        vt[1, :, pl.ds(at, QB)] = v1
        return carry

    lax.fori_loop(0, blocks, prepare, 0)

    def per_block(b, carry):
        at = pl.multiple_of(b * QB, QB)
        qcat = query_pair(qkv[0, :, pl.ds(at, QB)])
        start = bound_ref[0:1, pl.ds(at, QB)]
        length = bound_ref[1:2, pl.ds(at, QB)]
        row_at = b * 2
        for head in range(2):
            m_ref[row_at + head] = jnp.full((1, QB), NEG, jnp.float32)
            l_ref[row_at + head] = jnp.zeros((1, QB), jnp.float32)
            acc_ref[row_at + head] = jnp.zeros((HEAD_DIM, QB), jnp.float32)

        def per_tile(t, inner):
            key = pl.multiple_of(t * KB, KB)
            spot = lax.broadcasted_iota(jnp.int32, (KB, QB), 0) + (key - start)
            ok = (spot >= 0) & (spot < length)
            tile_step(
                kt[pl.ds(key, KB), :],
                vt[0, :, pl.ds(key, KB)],
                vt[1, :, pl.ds(key, KB)],
                qcat,
                ok,
                coef,
                row_at,
                m_ref,
                l_ref,
                acc_ref,
            )
            return inner

        lax.fori_loop(
            jnp.maximum(b - NEAR, 0), jnp.minimum(b + NEAR + 1, blocks), per_tile, 0
        )
        return carry

    lax.fori_loop(0, blocks, per_block, 0)
    keep.wait()
    for copy in sent:
        copy.wait()


def far_kernel(
    coef,
    groups_ref,
    row_ref,
    qkv_hbm,
    left_ref,
    right_ref,
    bound_ref,
    m_in,
    l_in,
    acc_in,
    kt_in,
    vt_in,
    out_ref,
    low_ref,
    high_ref,
    kt,
    vt,
    m_ref,
    l_ref,
    acc_ref,
    q_ref,
    sem,
):
    reach = left_ref.shape[2]
    width, tokens = q_ref.shape
    blocks = tokens // QB
    base = row_ref[0] * tokens
    moves = [
        pltpu.make_async_copy(kt_in, kt.at[reach : reach + tokens], sem.at[0]),
        pltpu.make_async_copy(vt_in, vt.at[:, :, reach : reach + tokens], sem.at[1]),
        pltpu.make_async_copy(qkv_hbm.at[0], q_ref, sem.at[2]),
    ]
    for move in moves:
        move.start()

    def find(b, state):
        image, begin = state
        token = base + b * QB

        def past(at):
            def more(s):
                return s[1] + groups_ref[s[0]] * 4 <= at

            def step(s):
                return s[0] + 1, s[1] + groups_ref[s[0]] * 4

            return more, step

        image, begin = lax.while_loop(*past(token), (image, begin))
        low_ref[b] = begin - base
        image, begin = lax.while_loop(*past(token + QB - 1), (image, begin))
        high_ref[b] = begin + groups_ref[image] * 4 - base
        return image, begin

    lax.fori_loop(0, blocks, find, (jnp.int32(0), jnp.int32(0)))
    for i in range(reach // KB):
        for needed, source, at in (
            (low_ref[0] < (i + 1) * KB - reach, left_ref, 0),
            (high_ref[blocks - 1] > tokens + i * KB, right_ref, reach + tokens),
        ):

            @pl.when(needed)
            def _():
                span = slice(i * KB, (i + 1) * KB)
                to = slice(at + i * KB, at + (i + 1) * KB)
                kt[to, :] = jnp.transpose(source[0, :, span])
                v0, v1 = split_heads(source[1, :, span])
                vt[0, :, to] = v0
                vt[1, :, to] = v1

    for move in moves:
        move.wait()

    def per_block(b, carry):
        at = pl.multiple_of(b * QB, QB)
        row_at = b * 2
        near_low = jnp.maximum(b - NEAR, 0) * QB
        near_high = jnp.minimum(b + NEAR + 1, blocks) * QB
        below = jnp.maximum((near_low - low_ref[b] + KB - 1) // KB, 0)
        above = jnp.maximum((high_ref[b] - near_high + KB - 1) // KB, 0)
        for head in range(2):
            m_ref[head] = m_in[row_at + head]
            l_ref[head] = l_in[row_at + head]
            acc_ref[head] = acc_in[row_at + head]

        @pl.when(below + above > 0)
        def _():
            qcat = query_pair(q_ref[:, pl.ds(at, QB)])
            start = bound_ref[0:1, pl.ds(at, QB)]
            length = bound_ref[1:2, pl.ds(at, QB)]

            def per_tile(t, inner):
                key = jnp.where(
                    t < below, near_low - (t + 1) * KB, near_high + (t - below) * KB
                )
                spot = lax.broadcasted_iota(jnp.int32, (KB, QB), 0) + (key - start)
                ok = (spot >= 0) & (spot < length)
                slot = pl.multiple_of(key + reach, KB)
                tile_step(
                    kt[pl.ds(slot, KB), :],
                    vt[0, :, pl.ds(slot, KB)],
                    vt[1, :, pl.ds(slot, KB)],
                    qcat,
                    ok,
                    coef,
                    0,
                    m_ref,
                    l_ref,
                    acc_ref,
                )
                return inner

            lax.fori_loop(0, below + above, per_tile, 0)

        both = [acc_ref[head] / l_ref[head] for head in range(2)]
        out_ref[:, pl.ds(at, QB)] = jnp.concatenate(both, axis=0).astype(jnp.bfloat16)
        return carry

    lax.fori_loop(0, blocks, per_block, 0)


def attention(qkv, residual, merge_weight, image_groups, row_id, full, rows, cols):
    _, width, tokens = qkv.shape
    reach = tokens // 2
    blocks = tokens // QB
    chunk = tokens // cols
    bf16, f32 = jnp.bfloat16, jnp.float32
    coef = math.log2(math.e) / math.sqrt(HEAD_DIM)
    smem = pl.BlockSpec(memory_space=pltpu.SMEM)
    vmem = pl.BlockSpec(memory_space=pltpu.VMEM)
    hbm = pl.BlockSpec(memory_space=pl.ANY)
    dma = pltpu.SemaphoreType.DMA
    halo = jax.ShapeDtypeStruct((2, width, reach), bf16)
    stat = jax.ShapeDtypeStruct((2 * blocks, 1, QB), f32)
    left, right, spread, far, m, l, acc, kt, vt, bound = pl.pallas_call(
        functools.partial(head_kernel, rows, cols, coef),
        out_shape=(
            halo,
            halo,
            jax.ShapeDtypeStruct((full, chunk), bf16),
            jax.ShapeDtypeStruct((width, full), bf16),
            stat,
            stat,
            jax.ShapeDtypeStruct((2 * blocks, HEAD_DIM, QB), f32),
            jax.ShapeDtypeStruct((tokens, width), bf16),
            jax.ShapeDtypeStruct((2, HEAD_DIM, tokens), bf16),
            jax.ShapeDtypeStruct((8, tokens), jnp.int32),
        ),
        in_specs=[hbm, hbm, hbm, vmem],
        out_specs=(hbm, hbm, hbm, hbm, vmem, vmem, vmem, vmem, vmem, vmem),
        scratch_shapes=[
            pltpu.VMEM((3, width, tokens), bf16),
            dma((4,)),
            dma((4,)),
            dma((4,)),
            dma((cols,)),
            dma((cols,)),
            dma,
            dma,
        ],
        compiler_params=pltpu.CompilerParams(
            collective_id=1, has_side_effects=True, vmem_limit_bytes=56 << 20
        ),
    )(qkv, residual, merge_weight, image_groups[None, :])
    attended = pl.pallas_call(
        functools.partial(far_kernel, coef),
        out_shape=jax.ShapeDtypeStruct((width, tokens), bf16),
        in_specs=[smem, smem, hbm] + [vmem] * 6 + [hbm] * 2,
        out_specs=vmem,
        scratch_shapes=[
            pltpu.SMEM((blocks,), jnp.int32),
            pltpu.SMEM((blocks,), jnp.int32),
            pltpu.VMEM((2 * reach + tokens, width), bf16),
            pltpu.VMEM((2, HEAD_DIM, 2 * reach + tokens), bf16),
            pltpu.VMEM((2, 1, QB), f32),
            pltpu.VMEM((2, 1, QB), f32),
            pltpu.VMEM((2, HEAD_DIM, QB), f32),
            pltpu.VMEM((width, tokens), bf16),
            dma((3,)),
        ],
        compiler_params=pltpu.CompilerParams(vmem_limit_bytes=56 << 20),
    )(image_groups, row_id[None], qkv, left, right, bound, m, l, acc, kt, vt)
    return attended, spread, far


def tail_kernel(
    rows,
    cols,
    attended_ref,
    residual_ref,
    out_weight_hbm,
    merge_weight_hbm,
    far_weight_hbm,
    gain_ref,
    dest_ref,
    layer_ref,
    got_rows,
    att,
    weight,
    weight_t,
    merge_w,
    layer_rows,
    held,
    far_rows,
    merged,
    pick,
    sorted_rows,
    load_sem,
    spread_send,
    spread_recv,
    back_send,
    back_recv,
    near_send,
    near_recv,
    sib_send,
    sib_recv,
    far_send,
    far_recv,
    row_send,
    row_recv,
    far_w_send,
    far_w_recv,
    gain_column,
):
    row = lax.axis_index("row")
    me = lax.axis_index("col")
    width, tokens = attended_ref.shape
    full = weight.shape[0]
    chunk = tokens // cols
    part = chunk // 4
    groups = tokens // 4
    share = groups // rows
    chips = cols // 2
    core = me % 2
    chip = me // 2
    sibling = me + 1 - 2 * core
    half = full // 2

    barrier = pltpu.get_barrier_semaphore()
    for k in range(1, cols):
        pl.semaphore_signal(
            barrier, inc=1, device_id={"col": (me + k) % cols}, device_id_type=MESH
        )
    for k in range(1, rows):
        pl.semaphore_signal(
            barrier, inc=1, device_id={"row": (row + k) % rows}, device_id_type=MESH
        )
    loads = [
        pltpu.make_async_copy(out_weight_hbm, weight, load_sem.at[0]),
        pltpu.make_async_copy(merge_weight_hbm, merge_w.at[0:width], load_sem.at[1]),
    ]
    line_up = rows // 4
    part_at = row // line_up
    far_at = pl.ds(pl.multiple_of(part_at * full, 128), full)
    far_place = merge_w.at[width : 2 * width, far_at]
    loads.append(pltpu.make_async_copy(far_weight_hbm, far_place, load_sem.at[2]))
    for load in loads:
        load.start()
    pl.semaphore_wait(barrier, rows + cols - 2)

    spread = []
    for k in range(1, cols):
        to = (me + k) % cols
        copy = pltpu.make_async_remote_copy(
            src_ref=attended_ref.at[:, pl.ds(pl.multiple_of(to * chunk, chunk), chunk)],
            dst_ref=att.at[pl.ds(pl.multiple_of(me * width, 16), width)],
            send_sem=spread_send.at[k],
            recv_sem=spread_recv.at[k],
            device_id={"col": to},
            device_id_type=MESH,
        )
        copy.start()
        spread.append(copy)
    gather = []
    for k in range(1, 4):
        copy = pltpu.make_async_remote_copy(
            src_ref=far_weight_hbm,
            dst_ref=far_place,
            send_sem=far_w_send.at[k],
            recv_sem=far_w_recv.at[k],
            device_id={"row": (row + k * line_up) % rows},
            device_id_type=MESH,
        )
        copy.start()
        gather.append(copy)
    mine = pl.ds(pl.multiple_of(me * chunk, chunk), chunk)
    att[pl.ds(pl.multiple_of(me * width, 16), width), :] = attended_ref[:, mine]

    before, after, across_chip = (chip + 3) % chips, (chip + 1) % chips, (chip + 2) % chips
    tile = 2 * part
    lane = lax.broadcasted_iota(jnp.int32, (1, tile), 1)
    of_chip = [dest_ref[pl.ds(c, 1), :] for c in (chip, before, across_chip, after)]
    line = jnp.concatenate(
        [
            of_chip[0],
            jnp.where(lane < part, of_chip[1], of_chip[3]),
            of_chip[2],
            jnp.where(lane < part, of_chip[3], of_chip[1]),
        ],
        axis=1,
    )
    owner_line = line // groups
    owner_column = jnp.transpose(
        jnp.broadcast_to(owner_line.astype(jnp.float32), (8, groups))
    )[:, 0:1].astype(jnp.int32)
    down = lax.broadcasted_iota(jnp.int32, (groups, groups), 0)
    across = lax.broadcasted_iota(jnp.int32, (groups, groups), 1)
    earlier = (owner_column == owner_line) & (down < across)
    rank = jnp.sum(earlier.astype(jnp.int32), axis=0, keepdims=True)
    spot = owner_line * share + rank
    pick[...] = jnp.where(down == spot, 1.0, 0.0).astype(jnp.bfloat16)
    slot = line % groups
    extra = merged.shape[0] - width
    which = lax.broadcasted_iota(jnp.int32, (extra, groups), 0)
    digits = jnp.where(which == 0, slot // 16, jnp.where(which == 1, slot % 16, 0))
    merged[width:, :] = digits.astype(jnp.float32).astype(jnp.bfloat16)

    loads[0].wait()

    def turn(i, carry):
        at = pl.multiple_of(i * 128, 128)
        weight_t[pl.ds(at, 128), :] = jnp.transpose(weight[:, pl.ds(at, 128)])
        return carry

    lax.fori_loop(0, full // 128, turn, 0)
    for i in range(full // 128):
        gain_column[i * 128 : (i + 1) * 128, :] = jnp.transpose(
            jnp.broadcast_to(gain_ref[i : i + 1, :], (8, 128))
        )
    for load in loads[1:]:
        load.wait()

    for copy in spread:
        copy.wait()
    strip = full // 4
    for i in range(4):
        at = i * strip
        projected = jnp.dot(
            weight_t[at : at + strip, :], att[...], preferred_element_type=jnp.float32
        )
        layer_rows[at : at + strip, :] = (
            residual_ref[at : at + strip, :].astype(jnp.float32) + projected
        ).astype(jnp.bfloat16)

    values32 = layer_rows[...].astype(jnp.float32)
    centre = jnp.sum(values32, axis=0, keepdims=True) * (1.0 / full)
    spread_of = jnp.sum(jnp.square(values32 - centre), axis=0, keepdims=True) * (1.0 / full)
    scale = lax.rsqrt(spread_of + 1e-06)
    normed = ((values32 - centre) * scale * gain_column[:, 0:1]).astype(jnp.bfloat16)
    here = lax.broadcasted_iota(jnp.int32, (chunk, chunk), 0)
    there = lax.broadcasted_iota(jnp.int32, (chunk, chunk), 1)
    order = jnp.where((here % 4) * part + here // 4 == there, 1.0, 0.0).astype(jnp.bfloat16)
    held[core] = jnp.dot(normed, order, preferred_element_type=jnp.float32).astype(jnp.bfloat16)

    goal = (chip + 1 + 2 * core) % chips
    near = []
    for h in range(2):
        span = pl.ds(h * half, half)
        copy = pltpu.make_async_remote_copy(
            src_ref=held.at[core, span],
            dst_ref=held.at[2 + core, span],
            send_sem=near_send.at[h],
            recv_sem=near_recv.at[core],
            device_id={"col": goal * 2 + h},
            device_id_type=MESH,
        )
        copy.start()
        near.append(copy)
    own = pltpu.make_async_remote_copy(
        src_ref=held.at[core],
        dst_ref=held.at[core],
        send_sem=sib_send.at[0],
        recv_sem=sib_recv.at[0],
        device_id={"col": sibling},
        device_id_type=MESH,
    )
    own.start()

    passed = []
    my_half = pl.ds(pl.multiple_of(core * half, 16), half)
    for s in range(2):
        arrive = pltpu.make_async_remote_copy(
            src_ref=held.at[core, my_half],
            dst_ref=held.at[2 + s, my_half],
            send_sem=near_send.at[s],
            recv_sem=near_recv.at[s],
            device_id={"col": sibling},
            device_id_type=MESH,
        )
        arrive.wait_recv()
        copy = pltpu.make_async_remote_copy(
            src_ref=held.at[2 + s, my_half],
            dst_ref=held.at[2 + s, my_half],
            send_sem=sib_send.at[1 + s],
            recv_sem=sib_recv.at[1 + s],
            device_id={"col": sibling},
            device_id_type=MESH,
        )
        copy.start()
        passed.append(copy)
    for copy in near:
        copy.wait_send()
    own.wait()
    for copy in passed:
        copy.wait()

    for copy in gather:
        copy.wait()

    total = None
    for j in range(4):
        side = jnp.concatenate(
            [held[s, :, j * part : (j + 1) * part] for s in range(4)], axis=1
        )
        term = jnp.dot(
            merge_w[:, j * full : (j + 1) * full], side, preferred_element_type=jnp.float32
        )
        total = term if total is None else total + term
    far_rows[...] = total[width:].astype(jnp.bfloat16)
    across_y = pltpu.make_async_remote_copy(
        src_ref=far_rows,
        dst_ref=merged.at[0:width, chunk : 2 * chunk],
        send_sem=far_send,
        recv_sem=far_recv,
        device_id={"col": (me + cols // 2) % cols},
        device_id_type=MESH,
    )
    across_y.start()
    merged[0:width, 0:chunk] = total[:width].astype(jnp.bfloat16)
    back = []
    for k in range(1, cols):
        to = (me + k) % cols
        copy = pltpu.make_async_remote_copy(
            src_ref=layer_rows.at[pl.ds(pl.multiple_of(to * width, 16), width)],
            dst_ref=layer_ref.at[:, mine],
            send_sem=back_send.at[k],
            recv_sem=back_recv.at[k],
            device_id={"col": to},
            device_id_type=MESH,
        )
        copy.start()
        back.append(copy)
    layer_ref[:, mine] = layer_rows[pl.ds(pl.multiple_of(me * width, 16), width), :]
    across_y.wait()

    sorted_rows[...] = lax.dot_general(
        pick[...], merged[...], (((1,), (1,)), ((), ())), preferred_element_type=jnp.float32
    ).astype(jnp.bfloat16)
    moves = []
    for k in range(1, rows):
        to = (row + k) % rows
        copy = pltpu.make_async_remote_copy(
            src_ref=sorted_rows.at[pl.ds(pl.multiple_of(to * share, share), share)],
            dst_ref=got_rows.at[pl.ds(pl.multiple_of(row * share, share), share)],
            send_sem=row_send.at[k],
            recv_sem=row_recv.at[k],
            device_id={"row": to},
            device_id_type=MESH,
        )
        copy.start()
        moves.append(copy)
    keep = pl.ds(pl.multiple_of(row * share, share), share)
    got_rows[keep, :] = sorted_rows[keep, :]
    for copy in moves:
        copy.wait()
    for copy in back:
        copy.wait()


def place_kernel(layer_hbm, got_ref, layer_out, image_ref, sem):
    copy = pltpu.make_async_copy(layer_hbm, layer_out, sem)
    copy.start()
    width, groups = image_ref.shape
    got = got_ref[...]
    target = got[:, width : width + 1].astype(jnp.float32) * 16.0 + got[
        :, width + 1 : width + 2
    ].astype(jnp.float32)
    slot = lax.broadcasted_iota(jnp.int32, (groups, groups), 1).astype(jnp.float32)
    put = jnp.where(target == slot, 1.0, 0.0).astype(jnp.bfloat16)
    image_ref[...] = lax.dot_general(
        got, put, (((0,), (0,)), ((), ())), preferred_element_type=jnp.float32
    )[:width].astype(jnp.bfloat16)
    copy.wait()


def tail(attended, residual, out_weight, merge_weight, far_weight, gain, dest_row, rows, cols):
    width, tokens = attended.shape
    full = out_weight.shape[0]
    chunk = tokens // cols
    groups = tokens // 4
    bf16 = jnp.bfloat16
    vmem = pl.BlockSpec(memory_space=pltpu.VMEM)
    hbm = pl.BlockSpec(memory_space=pl.ANY)
    dma = pltpu.SemaphoreType.DMA
    layer, got = pl.pallas_call(
        functools.partial(tail_kernel, rows, cols),
        out_shape=(
            jax.ShapeDtypeStruct((width, tokens), bf16),
            jax.ShapeDtypeStruct((groups, width + 16), bf16),
        ),
        in_specs=[vmem, vmem, hbm, hbm, hbm, vmem, vmem],
        out_specs=(vmem, vmem),
        scratch_shapes=[
            pltpu.VMEM((full, chunk), bf16),
            pltpu.VMEM((full, full), bf16),
            pltpu.VMEM((full, full), bf16),
            pltpu.VMEM((2 * width, merge_weight.shape[1]), bf16),
            pltpu.VMEM((full, chunk), bf16),
            pltpu.VMEM((4, full, chunk), bf16),
            pltpu.VMEM((width, chunk), bf16),
            pltpu.VMEM((width + 16, groups), bf16),
            pltpu.VMEM((groups, groups), bf16),
            pltpu.VMEM((groups, width + 16), bf16),
            dma((3,)),
            dma((cols,)),
            dma((cols,)),
            dma((cols,)),
            dma((cols,)),
            dma((2,)),
            dma((2,)),
            dma((3,)),
            dma((3,)),
            dma,
            dma,
            dma((rows,)),
            dma((rows,)),
            dma((4,)),
            dma((4,)),
            pltpu.VMEM((full, 8), jnp.float32),
        ],
        compiler_params=pltpu.CompilerParams(
            collective_id=0, has_side_effects=True, vmem_limit_bytes=60 << 20
        ),
        cost_estimate=pl.CostEstimate(
            flops=8 * full * full * chunk, bytes_accessed=16 << 20, transcendentals=0
        ),
    )(
        attended,
        residual,
        out_weight,
        merge_weight,
        far_weight,
        gain.reshape(-1, 128),
        dest_row.reshape(cols // 2, -1),
    )
    return pl.pallas_call(
        place_kernel,
        out_shape=(
            jax.ShapeDtypeStruct((width, tokens), bf16),
            jax.ShapeDtypeStruct((width, groups), bf16),
        ),
        in_specs=[hbm, vmem],
        out_specs=(hbm, vmem),
        scratch_shapes=[dma],
        compiler_params=pltpu.CompilerParams(vmem_limit_bytes=60 << 20),
    )(layer, got)


def body(qkv, residual_in, out_weight, merge_weight, merge_gain, image_groups, dest_row):
    rows = lax.axis_size("row")
    cols = lax.axis_size("col")
    row_id = lax.axis_index("row")
    attended, residual, far_weight = attention(
        qkv, residual_in, merge_weight, image_groups, row_id, out_weight.shape[0], rows, cols
    )
    return tail(
        attended, residual, out_weight, merge_weight, far_weight, merge_gain, dest_row, rows, cols
    )


def solution(mesh):
    return jax.shard_map(
        body,
        mesh=mesh,
        in_specs=(P(None, "col", "row"), P("col", "row"), P(), P("col", None), P(), P(), P("row")),
        out_specs=(P("col", "row"), P("col", "row")),
        check_vma=False,
    )
```

```python
import functools
import math

import jax
import jax.numpy as jnp
from jax import lax
from jax.experimental import pallas as pl
from jax.experimental.pallas import tpu as pltpu
from jax.sharding import PartitionSpec as P

HEAD_DIM = 88
QB = 256
KB = 256
NEAR = 2
PIECES = 2
NEG = -1e30
MESH = pl.DeviceIdType.MESH


def tile_step(kt, v0, v1, qcat, ok, coef, row, m_ref, l_ref, acc_ref):
    scores = lax.dot_general(
        kt, qcat, (((1,), (0,)), ((), ())), preferred_element_type=jnp.float32
    )
    width = qcat.shape[1] // 2
    for head in range(2):
        part = jnp.where(ok, scores[:, head * width : (head + 1) * width], NEG)
        old = m_ref[row + head]
        new = jnp.maximum(old, jnp.max(part, axis=0, keepdims=True))
        fade = jnp.exp2((old - new) * coef)
        expo = jnp.exp2(part * coef - new * coef)
        l_ref[row + head] = l_ref[row + head] * fade + jnp.sum(expo, axis=0, keepdims=True)
        m_ref[row + head] = new
        values = v1 if head else v0
        acc_ref[row + head] = acc_ref[row + head] * fade + lax.dot_general(
            values,
            expo.astype(jnp.bfloat16),
            (((1,), (0,)), ((), ())),
            preferred_element_type=jnp.float32,
        )


def split_heads(values):
    wide = values.astype(jnp.float32)
    return wide[:HEAD_DIM].astype(jnp.bfloat16), wide[HEAD_DIM:].astype(jnp.bfloat16)


def query_pair(block):
    feature = lax.broadcasted_iota(jnp.int32, block.shape, 0)
    zero = jnp.zeros_like(block)
    return jnp.concatenate(
        [jnp.where(feature < HEAD_DIM, block, zero), jnp.where(feature < HEAD_DIM, zero, block)],
        axis=1,
    )


def head_kernel(
    rows,
    cols,
    coef,
    qkv,
    res,
    merge_weight_ref,
    groups_line_ref,
    left_hbm,
    right_hbm,
    spread_hbm,
    far_hbm,
    m_ref,
    l_ref,
    acc_ref,
    kt,
    vt,
    bound_ref,
    load_sem,
    halo_send,
    halo_recv,
    res_send,
    res_recv,
    far_send,
    far_recv,
):
    row = lax.axis_index("row")
    me = lax.axis_index("col")
    _, width, tokens = qkv.shape
    reach = left_hbm.shape[2]
    blocks = tokens // QB
    chunk = tokens // cols
    full = spread_hbm.shape[0]
    barrier = pltpu.get_barrier_semaphore()
    after = (row + 1) % rows
    before = (row + rows - 1) % rows
    for other in (after, before):
        pl.semaphore_signal(barrier, inc=1, device_id={"row": other}, device_id_type=MESH)
    for k in range(1, cols):
        pl.semaphore_signal(
            barrier, inc=1, device_id={"col": (me + k) % cols}, device_id_type=MESH
        )
    mine = pl.ds(pl.multiple_of(me * chunk, chunk), chunk)
    place = pl.ds(pl.multiple_of(me * width, 16), width)
    keep = pltpu.make_async_copy(res.at[:, mine], spread_hbm.at[place], load_sem)
    keep.start()
    pl.semaphore_wait(barrier, cols + 1)

    sent = []
    for side, (other, target, at) in enumerate(
        ((after, left_hbm, tokens - reach), (before, right_hbm, 0))
    ):
        for i in range(2):
            sent.append(
                pltpu.make_async_remote_copy(
                    src_ref=qkv.at[1 + i, :, at : at + reach],
                    dst_ref=target.at[i],
                    send_sem=halo_send.at[2 * side + i],
                    recv_sem=halo_recv.at[2 * side + i],
                    device_id={"row": other},
                    device_id_type=MESH,
                )
            )
    for k in range(1, cols):
        to = (me + k) % cols
        sent.append(
            pltpu.make_async_remote_copy(
                src_ref=res.at[:, pl.ds(pl.multiple_of(to * chunk, chunk), chunk)],
                dst_ref=spread_hbm.at[place],
                send_sem=res_send.at[k],
                recv_sem=res_recv.at[k],
                device_id={"col": to},
                device_id_type=MESH,
            )
        )
    part = row // (rows // 4)
    sent.append(
        pltpu.make_async_remote_copy(
            src_ref=merge_weight_ref.at[:, pl.ds(pl.multiple_of(part * full, 128), full)],
            dst_ref=far_hbm,
            send_sem=far_send,
            recv_sem=far_recv,
            device_id={"col": (me + cols // 2) % cols},
            device_id_type=MESH,
        )
    )
    for copy in sent:
        copy.start()

    images = groups_line_ref.shape[1]
    first = lax.broadcasted_iota(jnp.int32, (images, images), 0)
    second = lax.broadcasted_iota(jnp.int32, (images, images), 1)
    size = (
        jnp.sum(jnp.where(second == first, groups_line_ref[...], 0), axis=1, keepdims=True) * 4
    )
    begin = (
        jnp.sum(
            jnp.where(second < first, groups_line_ref[...], 0), axis=1, keepdims=True
        )
        * 4
        - row * tokens
    )

    def prepare(b, carry):
        at = pl.multiple_of(b * QB, QB)
        token = lax.broadcasted_iota(jnp.int32, (images, QB), 1) + at
        inside = (token >= begin) & (token < begin + size)
        bound_ref[0:1, pl.ds(at, QB)] = jnp.sum(jnp.where(inside, begin, 0), axis=0, keepdims=True)
        bound_ref[1:2, pl.ds(at, QB)] = jnp.sum(jnp.where(inside, size, 0), axis=0, keepdims=True)
        kt[pl.ds(at, QB), :] = jnp.transpose(qkv[1, :, pl.ds(at, QB)])
        v0, v1 = split_heads(qkv[2, :, pl.ds(at, QB)])
        vt[0, :, pl.ds(at, QB)] = v0
        vt[1, :, pl.ds(at, QB)] = v1
        return carry

    lax.fori_loop(0, blocks, prepare, 0)

    def per_block(b, carry):
        at = pl.multiple_of(b * QB, QB)
        qcat = query_pair(qkv[0, :, pl.ds(at, QB)])
        start = bound_ref[0:1, pl.ds(at, QB)]
        length = bound_ref[1:2, pl.ds(at, QB)]
        row_at = b * 2
        for head in range(2):
            m_ref[row_at + head] = jnp.full((1, QB), NEG, jnp.float32)
            l_ref[row_at + head] = jnp.zeros((1, QB), jnp.float32)
            acc_ref[row_at + head] = jnp.zeros((HEAD_DIM, QB), jnp.float32)

        def per_tile(t, inner):
            key = pl.multiple_of(t * KB, KB)
            spot = lax.broadcasted_iota(jnp.int32, (KB, QB), 0) + (key - start)
            ok = (spot >= 0) & (spot < length)
            tile_step(
                kt[pl.ds(key, KB), :],
                vt[0, :, pl.ds(key, KB)],
                vt[1, :, pl.ds(key, KB)],
                qcat,
                ok,
                coef,
                row_at,
                m_ref,
                l_ref,
                acc_ref,
            )
            return inner

        lax.fori_loop(
            jnp.maximum(b - NEAR, 0), jnp.minimum(b + NEAR + 1, blocks), per_tile, 0
        )
        return carry

    lax.fori_loop(0, blocks, per_block, 0)
    keep.wait()
    for copy in sent:
        copy.wait()


def far_kernel(
    coef,
    groups_ref,
    row_ref,
    qkv_ref,
    left_ref,
    right_ref,
    bound_ref,
    m_in,
    l_in,
    acc_in,
    kt_in,
    vt_in,
    out_ref,
    low_ref,
    high_ref,
    kt,
    vt,
    m_ref,
    l_ref,
    acc_ref,
):
    reach = left_ref.shape[2]
    tokens = qkv_ref.shape[2]
    blocks = tokens // QB
    base = row_ref[0] * tokens

    def find(b, state):
        token = base + b * QB

        def past(at, state):
            def more(s):
                return s[1] + groups_ref[s[0]] * 4 <= at

            def step(s):
                return s[0] + 1, s[1] + groups_ref[s[0]] * 4

            return lax.while_loop(more, step, state)

        state = past(token, state)
        low_ref[b] = state[1] - base
        state = past(token + QB - 1, state)
        high_ref[b] = state[1] + groups_ref[state[0]] * 4 - base
        return state

    lax.fori_loop(0, blocks, find, (jnp.int32(0), jnp.int32(0)))
    for i in range(reach // KB):
        for needed, source, at in (
            (low_ref[0] < (i + 1) * KB - reach, left_ref, 0),
            (high_ref[blocks - 1] > tokens + i * KB, right_ref, reach),
        ):

            @pl.when(needed)
            def _():
                span = slice(i * KB, (i + 1) * KB)
                to = slice(at + i * KB, at + (i + 1) * KB)
                kt[to, :] = jnp.transpose(source[0, :, span])
                v0, v1 = split_heads(source[1, :, span])
                vt[0, :, to] = v0
                vt[1, :, to] = v1

    def per_block(b, carry):
        at = pl.multiple_of(b * QB, QB)
        row_at = b * 2
        near_low = jnp.maximum(b - NEAR, 0) * QB
        near_high = jnp.minimum(b + NEAR + 1, blocks) * QB
        low, high = low_ref[b], high_ref[b]
        below = jnp.maximum((near_low - jnp.maximum(low, 0) + KB - 1) // KB, 0)
        above = jnp.maximum((jnp.minimum(high, tokens) - near_high + KB - 1) // KB, 0)
        before = jnp.maximum((KB - 1 - low) // KB, 0)
        after = jnp.maximum((high - tokens + KB - 1) // KB, 0)
        for head in range(2):
            m_ref[head] = m_in[row_at + head]
            l_ref[head] = l_in[row_at + head]
            acc_ref[head] = acc_in[row_at + head]

        @pl.when(below + above + before + after > 0)
        def _():
            qcat = query_pair(qkv_ref[0, :, pl.ds(at, QB)])
            start = bound_ref[0:1, pl.ds(at, QB)]
            length = bound_ref[1:2, pl.ds(at, QB)]

            def tile(key, slot, k_from, v_from):
                slot = pl.multiple_of(slot, KB)
                spot = lax.broadcasted_iota(jnp.int32, (KB, QB), 0) + (key - start)
                ok = (spot >= 0) & (spot < length)
                tile_step(
                    k_from[pl.ds(slot, KB), :],
                    v_from[0, :, pl.ds(slot, KB)],
                    v_from[1, :, pl.ds(slot, KB)],
                    qcat,
                    ok,
                    coef,
                    0,
                    m_ref,
                    l_ref,
                    acc_ref,
                )

            def own_tile(t, inner):
                key = jnp.where(
                    t < below, near_low - (t + 1) * KB, near_high + (t - below) * KB
                )
                tile(key, key, kt_in, vt_in)
                return inner

            def halo_tile(t, inner):
                key = jnp.where(t < before, -(t + 1) * KB, tokens + (t - before) * KB)
                slot = jnp.where(t < before, reach - (t + 1) * KB, reach + (t - before) * KB)
                tile(key, slot, kt, vt)
                return inner

            lax.fori_loop(0, below + above, own_tile, 0)
            lax.fori_loop(0, before + after, halo_tile, 0)

        both = [acc_ref[head] * (1.0 / l_ref[head]) for head in range(2)]
        out_ref[:, pl.ds(at, QB)] = jnp.concatenate(both, axis=0).astype(jnp.bfloat16)
        return carry

    lax.fori_loop(0, blocks, per_block, 0)


def attention(qkv, residual, merge_weight, image_groups, row_id, full, rows, cols):
    _, width, tokens = qkv.shape
    reach = tokens // 2
    blocks = tokens // QB
    chunk = tokens // cols
    bf16, f32 = jnp.bfloat16, jnp.float32
    coef = math.log2(math.e) / math.sqrt(HEAD_DIM)
    smem = pl.BlockSpec(memory_space=pltpu.SMEM)
    vmem = pl.BlockSpec(memory_space=pltpu.VMEM)
    hbm = pl.BlockSpec(memory_space=pl.ANY)
    dma = pltpu.SemaphoreType.DMA
    halo = jax.ShapeDtypeStruct((2, width, reach), bf16)
    stat = jax.ShapeDtypeStruct((2 * blocks, 1, QB), f32)
    left, right, spread, far, m, l, acc, kt, vt, bound = pl.pallas_call(
        functools.partial(head_kernel, rows, cols, coef),
        out_shape=(
            halo,
            halo,
            jax.ShapeDtypeStruct((full, chunk), bf16),
            jax.ShapeDtypeStruct((width, full), bf16),
            stat,
            stat,
            jax.ShapeDtypeStruct((2 * blocks, HEAD_DIM, QB), f32),
            jax.ShapeDtypeStruct((tokens, width), bf16),
            jax.ShapeDtypeStruct((2, HEAD_DIM, tokens), bf16),
            jax.ShapeDtypeStruct((8, tokens), jnp.int32),
        ),
        in_specs=[vmem, vmem, vmem, vmem],
        out_specs=(hbm, hbm, hbm, hbm, vmem, vmem, vmem, vmem, vmem, vmem),
        scratch_shapes=[
            dma,
            dma((4,)),
            dma((4,)),
            dma((cols,)),
            dma((cols,)),
            dma,
            dma,
        ],
        compiler_params=pltpu.CompilerParams(
            collective_id=1, has_side_effects=True, vmem_limit_bytes=20 << 20
        ),
    )(qkv, residual, merge_weight, image_groups[None, :])
    attended = pl.pallas_call(
        functools.partial(far_kernel, coef),
        out_shape=jax.ShapeDtypeStruct((width, tokens), bf16),
        in_specs=[smem, smem] + [vmem] * 9,
        out_specs=vmem,
        scratch_shapes=[
            pltpu.SMEM((blocks,), jnp.int32),
            pltpu.SMEM((blocks,), jnp.int32),
            pltpu.VMEM((2 * reach, width), bf16),
            pltpu.VMEM((2, HEAD_DIM, 2 * reach), bf16),
            pltpu.VMEM((2, 1, QB), f32),
            pltpu.VMEM((2, 1, QB), f32),
            pltpu.VMEM((2, HEAD_DIM, QB), f32),
        ],
        compiler_params=pltpu.CompilerParams(vmem_limit_bytes=20 << 20),
    )(image_groups, row_id[None], qkv, left, right, bound, m, l, acc, kt, vt)
    return attended, spread, far


def tail_kernel(
    rows,
    cols,
    attended_ref,
    residual_ref,
    weight,
    merge_weight_ref,
    far_weight_ref,
    gain_ref,
    dest_ref,
    layer_ref,
    got_rows,
    att,
    weight_t,
    merge_w,
    layer_rows,
    held,
    far_rows,
    merged,
    pick,
    sorted_rows,
    gain_column,
    load_sem,
    spread_send,
    spread_recv,
    back_send,
    back_recv,
    near_send,
    near_recv,
    own_send,
    own_recv,
    pass_send,
    pass_recv,
    far_send,
    far_recv,
    row_send,
    row_recv,
    far_w_send,
    far_w_recv,
):
    row = lax.axis_index("row")
    me = lax.axis_index("col")
    width, tokens = attended_ref.shape
    full = weight.shape[0]
    chunk = tokens // cols
    piece = chunk // PIECES
    part = piece // 4
    groups = tokens // 4
    share = groups // rows
    chips = cols // 2
    core = me % 2
    chip = me // 2
    sibling = me + 1 - 2 * core
    half = full // 2
    line_up = rows // 4

    barrier = pltpu.get_barrier_semaphore()
    for k in range(1, cols):
        pl.semaphore_signal(
            barrier, inc=1, device_id={"col": (me + k) % cols}, device_id_type=MESH
        )
    for k in range(1, rows):
        pl.semaphore_signal(
            barrier, inc=1, device_id={"row": (row + k) % rows}, device_id_type=MESH
        )
    far_at = pl.ds(pl.multiple_of(row // line_up * full, 128), full)
    far_place = merge_w.at[width : 2 * width, far_at]
    loads = [
        pltpu.make_async_copy(merge_weight_ref, merge_w.at[0:width], load_sem.at[0]),
        pltpu.make_async_copy(far_weight_ref, far_place, load_sem.at[1]),
    ]
    for load in loads:
        load.start()
    my_rows = pl.ds(pl.multiple_of(me * width, 16), width)
    pl.semaphore_wait(barrier, rows + cols - 2)

    def lanes(owner, p):
        return pl.ds(pl.multiple_of(owner * chunk + p * piece, 128), piece)

    spread = []
    for p in range(PIECES):
        for k in range(1, cols):
            to = (me + k) % cols
            copy = pltpu.make_async_remote_copy(
                src_ref=attended_ref.at[:, lanes(to, p)],
                dst_ref=att.at[p, my_rows],
                send_sem=spread_send.at[p, k],
                recv_sem=spread_recv.at[p, k],
                device_id={"col": to},
                device_id_type=MESH,
            )
            copy.start()
            spread.append(copy)
    gather = []
    for k in range(1, 4):
        copy = pltpu.make_async_remote_copy(
            src_ref=far_weight_ref,
            dst_ref=far_place,
            send_sem=far_w_send.at[k],
            recv_sem=far_w_recv.at[k],
            device_id={"row": (row + k * line_up) % rows},
            device_id_type=MESH,
        )
        copy.start()
        gather.append(copy)
    for p in range(PIECES):
        att[p, my_rows, :] = attended_ref[:, lanes(me, p)]

    def turn(i, carry):
        at = pl.multiple_of(i * 128, 128)
        weight_t[pl.ds(at, 128), :] = jnp.transpose(weight[:, pl.ds(at, 128)])
        return carry

    lax.fori_loop(0, full // 128, turn, 0)
    for i in range(full // 128):
        gain_column[i * 128 : (i + 1) * 128, :] = jnp.transpose(
            jnp.broadcast_to(gain_ref[i : i + 1, :], (8, 128))
        )

    before, after, across_chip = (chip + 3) % chips, (chip + 1) % chips, (chip + 2) % chips
    of = [dest_ref[pl.ds(c, 1), :] for c in (chip, before, across_chip, after)]
    span = chunk // 4
    line = jnp.concatenate(
        [
            of[c][:, k * span + p * part : k * span + (p + 1) * part]
            for order in (((0, 0), (0, 1), (1, 0), (3, 1)), ((2, 0), (2, 1), (3, 0), (1, 1)))
            for p in range(PIECES)
            for c, k in order
        ],
        axis=1,
    )
    owner_line = line // groups
    owner_column = jnp.transpose(
        jnp.broadcast_to(owner_line.astype(jnp.float32), (8, groups))
    )[:, 0:1].astype(jnp.int32)
    down = lax.broadcasted_iota(jnp.int32, (groups, groups), 0)
    across = lax.broadcasted_iota(jnp.int32, (groups, groups), 1)
    earlier = (owner_column == owner_line) & (down < across)
    rank = jnp.sum(earlier.astype(jnp.int32), axis=0, keepdims=True)
    pick[...] = jnp.where(down == owner_line * share + rank, 1.0, 0.0).astype(jnp.bfloat16)
    slot = line % groups
    which = lax.broadcasted_iota(jnp.int32, (merged.shape[0] - width, groups), 0)
    digits = jnp.where(which == 0, slot // 16, jnp.where(which == 1, slot % 16, 0))
    merged[width:, :] = digits.astype(jnp.float32).astype(jnp.bfloat16)

    here = lax.broadcasted_iota(jnp.int32, (piece, piece), 0)
    there = lax.broadcasted_iota(jnp.int32, (piece, piece), 1)
    order = jnp.where((here % 4) * part + here // 4 == there, 1.0, 0.0).astype(jnp.bfloat16)
    goal = (chip + 1 + 2 * core) % chips
    near, own, back = [], [], []
    for p in range(PIECES):
        for copy in spread[p * (cols - 1) : (p + 1) * (cols - 1)]:
            copy.wait()
        at = slice(p * piece, (p + 1) * piece)
        projected = jnp.dot(weight_t[...], att[p], preferred_element_type=jnp.float32)
        rounded = (residual_ref[:, at].astype(jnp.float32) + projected).astype(jnp.bfloat16)
        layer_rows[p] = rounded
        values32 = rounded.astype(jnp.float32)
        centre = jnp.sum(values32, axis=0, keepdims=True) * (1.0 / full)
        spread_of = jnp.sum(jnp.square(values32 - centre), axis=0, keepdims=True) * (1.0 / full)
        scale = lax.rsqrt(spread_of + 1e-06)
        normed = ((values32 - centre) * scale * gain_column[:, 0:1]).astype(jnp.bfloat16)
        held[p, core] = jnp.dot(normed, order, preferred_element_type=jnp.float32).astype(
            jnp.bfloat16
        )
        for h in range(2):
            rows_of = pl.ds(h * half, half)
            copy = pltpu.make_async_remote_copy(
                src_ref=held.at[p, core, rows_of],
                dst_ref=held.at[p, 2 + core, rows_of],
                send_sem=near_send.at[p, h],
                recv_sem=near_recv.at[p, core],
                device_id={"col": goal * 2 + h},
                device_id_type=MESH,
            )
            copy.start()
            near.append(copy)
        copy = pltpu.make_async_remote_copy(
            src_ref=held.at[p, core],
            dst_ref=held.at[p, core],
            send_sem=own_send.at[p],
            recv_sem=own_recv.at[p],
            device_id={"col": sibling},
            device_id_type=MESH,
        )
        copy.start()
        own.append(copy)
        layer_ref[:, lanes(me, p)] = layer_rows[p, my_rows, :]

    passed = []
    my_half = pl.ds(pl.multiple_of(core * half, 16), half)
    for p in range(PIECES):
        for s in range(2):
            arrive = pltpu.make_async_remote_copy(
                src_ref=held.at[p, core, my_half],
                dst_ref=held.at[p, 2 + s, my_half],
                send_sem=near_send.at[p, s],
                recv_sem=near_recv.at[p, s],
                device_id={"col": sibling},
                device_id_type=MESH,
            )
            arrive.wait_recv()
            copy = pltpu.make_async_remote_copy(
                src_ref=held.at[p, 2 + s, my_half],
                dst_ref=held.at[p, 2 + s, my_half],
                send_sem=pass_send.at[p, s],
                recv_sem=pass_recv.at[p, s],
                device_id={"col": sibling},
                device_id_type=MESH,
            )
            copy.start()
            passed.append(copy)
    for copy in near:
        copy.wait_send()

    def send_back(p):
        for k in range(1, cols):
            to = (me + k) % cols
            copy = pltpu.make_async_remote_copy(
                src_ref=layer_rows.at[p, pl.ds(pl.multiple_of(to * width, 16), width)],
                dst_ref=layer_ref.at[:, lanes(me, p)],
                send_sem=back_send.at[p, k],
                recv_sem=back_recv.at[p, k],
                device_id={"col": to},
                device_id_type=MESH,
            )
            copy.start()
            back.append(copy)

    for p in range(PIECES - 1):
        send_back(p)
    for load in loads:
        load.wait()
    for copy in gather:
        copy.wait()
    for copy in own + passed:
        copy.wait()

    total = None
    for j in range(4):
        side = jnp.concatenate(
            [
                held[p, s, :, j * part : (j + 1) * part]
                for p in range(PIECES)
                for s in range(4)
            ],
            axis=1,
        )
        term = jnp.dot(
            merge_w[:, j * full : (j + 1) * full], side, preferred_element_type=jnp.float32
        )
        total = term if total is None else total + term
    far_rows[...] = total[width:].astype(jnp.bfloat16)
    across_y = pltpu.make_async_remote_copy(
        src_ref=far_rows,
        dst_ref=merged.at[0:width, chunk : 2 * chunk],
        send_sem=far_send,
        recv_sem=far_recv,
        device_id={"col": (me + cols // 2) % cols},
        device_id_type=MESH,
    )
    across_y.start()
    send_back(PIECES - 1)
    merged[0:width, 0:chunk] = total[:width].astype(jnp.bfloat16)
    across_y.wait()

    sorted_rows[...] = lax.dot_general(
        pick[...], merged[...], (((1,), (1,)), ((), ())), preferred_element_type=jnp.float32
    ).astype(jnp.bfloat16)
    moves = []
    for k in range(1, rows):
        to = (row + k) % rows
        copy = pltpu.make_async_remote_copy(
            src_ref=sorted_rows.at[pl.ds(pl.multiple_of(to * share, share), share)],
            dst_ref=got_rows.at[pl.ds(pl.multiple_of(row * share, share), share)],
            send_sem=row_send.at[k],
            recv_sem=row_recv.at[k],
            device_id={"row": to},
            device_id_type=MESH,
        )
        copy.start()
        moves.append(copy)
    keep = pl.ds(pl.multiple_of(row * share, share), share)
    got_rows[keep, :] = sorted_rows[keep, :]
    for copy in moves + back:
        copy.wait()


def place_kernel(layer_ref, got_ref, layer_out, image_ref, sem):
    copy = pltpu.make_async_copy(layer_ref, layer_out, sem)
    copy.start()
    width, groups = image_ref.shape
    got = got_ref[...]
    target = got[:, width : width + 1].astype(jnp.float32) * 16.0 + got[
        :, width + 1 : width + 2
    ].astype(jnp.float32)
    slot = lax.broadcasted_iota(jnp.int32, (groups, groups), 1).astype(jnp.float32)
    put = jnp.where(target == slot, 1.0, 0.0).astype(jnp.bfloat16)
    image_ref[...] = lax.dot_general(
        got, put, (((0,), (0,)), ((), ())), preferred_element_type=jnp.float32
    )[:width].astype(jnp.bfloat16)
    copy.wait()


def tail(attended, residual, out_weight, merge_weight, far_weight, gain, dest_row, rows, cols):
    width, tokens = attended.shape
    full = out_weight.shape[0]
    chunk = tokens // cols
    piece = chunk // PIECES
    groups = tokens // 4
    bf16 = jnp.bfloat16
    vmem = pl.BlockSpec(memory_space=pltpu.VMEM)
    hbm = pl.BlockSpec(memory_space=pl.ANY)
    dma = pltpu.SemaphoreType.DMA
    layer, got = pl.pallas_call(
        functools.partial(tail_kernel, rows, cols),
        out_shape=(
            jax.ShapeDtypeStruct((width, tokens), bf16),
            jax.ShapeDtypeStruct((groups, width + 16), bf16),
        ),
        in_specs=[vmem] * 7,
        out_specs=(vmem, vmem),
        scratch_shapes=[
            pltpu.VMEM((PIECES, full, piece), bf16),
            pltpu.VMEM((full, full), bf16),
            pltpu.VMEM((2 * width, merge_weight.shape[1]), bf16),
            pltpu.VMEM((PIECES, full, piece), bf16),
            pltpu.VMEM((PIECES, 4, full, piece), bf16),
            pltpu.VMEM((width, chunk), bf16),
            pltpu.VMEM((width + 16, groups), bf16),
            pltpu.VMEM((groups, groups), bf16),
            pltpu.VMEM((groups, width + 16), bf16),
            pltpu.VMEM((full, 8), jnp.float32),
            dma((2,)),
            dma((PIECES, cols)),
            dma((PIECES, cols)),
            dma((PIECES, cols)),
            dma((PIECES, cols)),
            dma((PIECES, 2)),
            dma((PIECES, 2)),
            dma((PIECES,)),
            dma((PIECES,)),
            dma((PIECES, 2)),
            dma((PIECES, 2)),
            dma,
            dma,
            dma((rows,)),
            dma((rows,)),
            dma((4,)),
            dma((4,)),
        ],
        compiler_params=pltpu.CompilerParams(
            collective_id=0, has_side_effects=True, vmem_limit_bytes=40 << 20
        ),
    )(
        attended,
        residual,
        out_weight,
        merge_weight,
        far_weight,
        gain.reshape(-1, 128),
        dest_row.reshape(cols // 2, -1),
    )
    return pl.pallas_call(
        place_kernel,
        out_shape=(
            jax.ShapeDtypeStruct((width, tokens), bf16),
            jax.ShapeDtypeStruct((width, groups), bf16),
        ),
        in_specs=[vmem, vmem],
        out_specs=(hbm, vmem),
        scratch_shapes=[dma],
        compiler_params=pltpu.CompilerParams(vmem_limit_bytes=16 << 20),
    )(layer, got)


def body(qkv, residual_in, out_weight, merge_weight, merge_gain, image_groups, dest_row):
    rows = lax.axis_size("row")
    cols = lax.axis_size("col")
    row_id = lax.axis_index("row")
    attended, residual, far_weight = attention(
        qkv, residual_in, merge_weight, image_groups, row_id, out_weight.shape[0], rows, cols
    )
    return tail(
        attended, residual, out_weight, merge_weight, far_weight, merge_gain, dest_row, rows, cols
    )


def solution(mesh):
    return jax.shard_map(
        body,
        mesh=mesh,
        in_specs=(P(None, "col", "row"), P("col", "row"), P(), P("col", None), P(), P(), P("row")),
        out_specs=(P("col", "row"), P("col", "row")),
        check_vma=False,
    )
```

```python
import functools
import math

import jax
import jax.numpy as jnp
from jax import lax
from jax.experimental import pallas as pl
from jax.experimental.pallas import tpu as pltpu
from jax.sharding import PartitionSpec as P

HEAD_DIM = 88
QB = 256
KB = 256
PIECES = 2
NEG = -1e30
MESH = pl.DeviceIdType.MESH


def tile_step(kt, v0, v1, qcat, ok, coef, row, m_ref, l_ref, acc_ref):
    scores = lax.dot_general(
        kt, qcat, (((1,), (0,)), ((), ())), preferred_element_type=jnp.float32
    )
    width = qcat.shape[1] // 2
    for head in range(2):
        part = jnp.where(ok, scores[:, head * width : (head + 1) * width], NEG)
        old = m_ref[row + head]
        new = jnp.maximum(old, jnp.max(part, axis=0, keepdims=True))
        fade = jnp.exp2((old - new) * coef)
        expo = jnp.exp2(part * coef - new * coef)
        l_ref[row + head] = l_ref[row + head] * fade + jnp.sum(expo, axis=0, keepdims=True)
        m_ref[row + head] = new
        values = v1 if head else v0
        acc_ref[row + head] = acc_ref[row + head] * fade + lax.dot_general(
            values,
            expo.astype(jnp.bfloat16),
            (((1,), (0,)), ((), ())),
            preferred_element_type=jnp.float32,
        )


def split_heads(values):
    wide = values.astype(jnp.float32)
    return wide[:HEAD_DIM].astype(jnp.bfloat16), wide[HEAD_DIM:].astype(jnp.bfloat16)


def query_pair(block):
    feature = lax.broadcasted_iota(jnp.int32, block.shape, 0)
    zero = jnp.zeros_like(block)
    return jnp.concatenate(
        [jnp.where(feature < HEAD_DIM, block, zero), jnp.where(feature < HEAD_DIM, zero, block)],
        axis=1,
    )


def head_kernel(
    rows,
    cols,
    coef,
    qkv_hbm,
    res_hbm,
    merge_weight_hbm,
    groups_hbm,
    left_hbm,
    right_hbm,
    spread_hbm,
    far_hbm,
    m_ref,
    l_ref,
    acc_ref,
    bound_ref,
    q_ref,
    load_sem,
    halo_send,
    halo_recv,
    res_send,
    res_recv,
    far_send,
    far_recv,
    held_scores,
    kt,
    vt,
    kv,
    res,
    far,
    groups_line_ref,
):
    row = lax.axis_index("row")
    me = lax.axis_index("col")
    width, tokens = q_ref.shape
    reach = left_hbm.shape[2]
    blocks = tokens // QB
    chunk = tokens // cols
    full = spread_hbm.shape[0]
    barrier = pltpu.get_barrier_semaphore()
    after = (row + 1) % rows
    before = (row + rows - 1) % rows
    for other in (after, before):
        pl.semaphore_signal(barrier, inc=1, device_id={"row": other}, device_id_type=MESH)
    for k in range(1, cols):
        pl.semaphore_signal(
            barrier, inc=1, device_id={"col": (me + k) % cols}, device_id_type=MESH
        )
    mine = pl.ds(pl.multiple_of(me * chunk, chunk), chunk)
    place = pl.ds(pl.multiple_of(me * width, 16), width)
    part = row // (rows // 4)
    piece = merge_weight_hbm.at[:, pl.ds(pl.multiple_of(part * full, 128), full)]
    loads = [
        pltpu.make_async_copy(qkv_hbm.at[i], target, load_sem.at[i])
        for i, target in ((1, kv.at[0]), (2, kv.at[1]), (0, q_ref))
    ]
    loads.append(pltpu.make_async_copy(res_hbm, res, load_sem.at[3]))
    loads.append(pltpu.make_async_copy(piece, far, load_sem.at[4]))
    loads.append(pltpu.make_async_copy(groups_hbm, groups_line_ref, load_sem.at[6]))
    for load in loads:
        load.start()
    for load in loads:
        load.wait()
    keep = pltpu.make_async_copy(res.at[:, mine], spread_hbm.at[place], load_sem.at[5])
    keep.start()
    pl.semaphore_wait(barrier, cols + 1)

    sent = []
    for side, (other, target, at) in enumerate(
        ((after, left_hbm, tokens - reach), (before, right_hbm, 0))
    ):
        for i in range(2):
            sent.append(
                pltpu.make_async_remote_copy(
                    src_ref=kv.at[i, :, at : at + reach],
                    dst_ref=target.at[i],
                    send_sem=halo_send.at[2 * side + i],
                    recv_sem=halo_recv.at[2 * side + i],
                    device_id={"row": other},
                    device_id_type=MESH,
                )
            )
    for k in range(1, cols):
        to = (me + k) % cols
        sent.append(
            pltpu.make_async_remote_copy(
                src_ref=res.at[:, pl.ds(pl.multiple_of(to * chunk, chunk), chunk)],
                dst_ref=spread_hbm.at[place],
                send_sem=res_send.at[k],
                recv_sem=res_recv.at[k],
                device_id={"col": to},
                device_id_type=MESH,
            )
        )
    sent.append(
        pltpu.make_async_remote_copy(
            src_ref=far,
            dst_ref=far_hbm,
            send_sem=far_send,
            recv_sem=far_recv,
            device_id={"col": (me + cols // 2) % cols},
            device_id_type=MESH,
        )
    )
    for copy in sent:
        copy.start()

    images = groups_line_ref.shape[1]
    first = lax.broadcasted_iota(jnp.int32, (images, images), 0)
    second = lax.broadcasted_iota(jnp.int32, (images, images), 1)
    size = (
        jnp.sum(jnp.where(second == first, groups_line_ref[...], 0), axis=1, keepdims=True) * 4
    )
    begin = (
        jnp.sum(
            jnp.where(second < first, groups_line_ref[...], 0), axis=1, keepdims=True
        )
        * 4
        - row * tokens
    )

    def prepare(b, carry):
        at = pl.multiple_of(b * QB, QB)
        token = lax.broadcasted_iota(jnp.int32, (images, QB), 1) + at
        inside = (token >= begin) & (token < begin + size)
        bound_ref[0:1, pl.ds(at, QB)] = jnp.sum(jnp.where(inside, begin, 0), axis=0, keepdims=True)
        bound_ref[1:2, pl.ds(at, QB)] = jnp.sum(jnp.where(inside, size, 0), axis=0, keepdims=True)
        kt[pl.ds(at, QB), :] = jnp.transpose(kv[0, :, pl.ds(at, QB)])
        v0, v1 = split_heads(kv[1, :, pl.ds(at, QB)])
        vt[0, :, pl.ds(at, QB)] = v0
        vt[1, :, pl.ds(at, QB)] = v1
        return carry

    lax.fori_loop(0, blocks, prepare, 0)

    def per_block(b, carry):
        at = pl.multiple_of(b * QB, QB)
        qcat = query_pair(q_ref[:, pl.ds(at, QB)])
        start = bound_ref[0:1, pl.ds(at, QB)]
        length = bound_ref[1:2, pl.ds(at, QB)]
        spot = lax.broadcasted_iota(jnp.int32, (KB, QB), 0) - start
        tops = [jnp.full((1, QB), NEG, jnp.float32) for _ in range(2)]
        for t in range(blocks):
            key = t * KB
            scores = jnp.dot(kt[key : key + KB, :], qcat, preferred_element_type=jnp.float32)
            ok = (spot >= -key) & (spot < length - key)
            for head in range(2):
                part = jnp.where(ok, scores[:, head * QB : (head + 1) * QB], NEG)
                held_scores[head, t] = part
                tops[head] = jnp.maximum(tops[head], jnp.max(part, axis=0, keepdims=True))
        for head in range(2):
            peak = tops[head] * coef
            total = jnp.zeros((1, QB), jnp.float32)
            sums = jnp.zeros((HEAD_DIM, QB), jnp.float32)
            for t in range(blocks):
                expo = jnp.exp2(held_scores[head, t] * coef - peak)
                total = total + jnp.sum(expo, axis=0, keepdims=True)
                sums = sums + jnp.dot(
                    vt[head, :, t * KB : (t + 1) * KB],
                    expo.astype(jnp.bfloat16),
                    preferred_element_type=jnp.float32,
                )
            m_ref[b * 2 + head] = tops[head]
            l_ref[b * 2 + head] = total
            acc_ref[b * 2 + head] = sums
        return carry

    lax.fori_loop(0, blocks, per_block, 0)
    keep.wait()
    for copy in sent:
        copy.wait()


def far_kernel(
    coef,
    groups_ref,
    row_ref,
    q_ref,
    left_ref,
    right_ref,
    bound_ref,
    m_in,
    l_in,
    acc_in,
    out_ref,
    low_ref,
    high_ref,
    kt,
    vt,
    m_ref,
    l_ref,
    acc_ref,
):
    reach = left_ref.shape[2]
    tokens = q_ref.shape[1]
    blocks = tokens // QB
    base = row_ref[0] * tokens

    def find(b, state):
        token = base + b * QB

        def past(at, state):
            def more(s):
                return s[1] + groups_ref[s[0]] * 4 <= at

            def step(s):
                return s[0] + 1, s[1] + groups_ref[s[0]] * 4

            return lax.while_loop(more, step, state)

        state = past(token, state)
        low_ref[b] = state[1] - base
        state = past(token + QB - 1, state)
        high_ref[b] = state[1] + groups_ref[state[0]] * 4 - base
        return state

    lax.fori_loop(0, blocks, find, (jnp.int32(0), jnp.int32(0)))
    for i in range(reach // KB):
        for needed, source, at in (
            (low_ref[0] < (i + 1) * KB - reach, left_ref, 0),
            (high_ref[blocks - 1] > tokens + i * KB, right_ref, reach),
        ):

            @pl.when(needed)
            def _():
                span = slice(i * KB, (i + 1) * KB)
                to = slice(at + i * KB, at + (i + 1) * KB)
                kt[to, :] = jnp.transpose(source[0, :, span])
                v0, v1 = split_heads(source[1, :, span])
                vt[0, :, to] = v0
                vt[1, :, to] = v1

    def per_block(b, carry):
        at = pl.multiple_of(b * QB, QB)
        row_at = b * 2
        before = jnp.maximum((KB - 1 - low_ref[b]) // KB, 0)
        after = jnp.maximum((high_ref[b] - tokens + KB - 1) // KB, 0)
        for head in range(2):
            m_ref[head] = m_in[row_at + head]
            l_ref[head] = l_in[row_at + head]
            acc_ref[head] = acc_in[row_at + head]

        @pl.when(before + after > 0)
        def _():
            qcat = query_pair(q_ref[:, pl.ds(at, QB)])
            start = bound_ref[0:1, pl.ds(at, QB)]
            length = bound_ref[1:2, pl.ds(at, QB)]

            def halo_tile(t, inner):
                key = jnp.where(t < before, -(t + 1) * KB, tokens + (t - before) * KB)
                slot = jnp.where(t < before, reach - (t + 1) * KB, reach + (t - before) * KB)
                slot = pl.multiple_of(slot, KB)
                spot = lax.broadcasted_iota(jnp.int32, (KB, QB), 0) + (key - start)
                ok = (spot >= 0) & (spot < length)
                tile_step(
                    kt[pl.ds(slot, KB), :],
                    vt[0, :, pl.ds(slot, KB)],
                    vt[1, :, pl.ds(slot, KB)],
                    qcat,
                    ok,
                    coef,
                    0,
                    m_ref,
                    l_ref,
                    acc_ref,
                )
                return inner

            lax.fori_loop(0, before + after, halo_tile, 0)

        both = [acc_ref[head] * (1.0 / l_ref[head]) for head in range(2)]
        out_ref[:, pl.ds(at, QB)] = jnp.concatenate(both, axis=0).astype(jnp.bfloat16)
        return carry

    lax.fori_loop(0, blocks, per_block, 0)


def attention(qkv, residual, merge_weight, image_groups, row_id, full, rows, cols):
    _, width, tokens = qkv.shape
    reach = tokens // 2
    blocks = tokens // QB
    chunk = tokens // cols
    bf16, f32 = jnp.bfloat16, jnp.float32
    coef = math.log2(math.e) / math.sqrt(HEAD_DIM)
    smem = pl.BlockSpec(memory_space=pltpu.SMEM)
    vmem = pl.BlockSpec(memory_space=pltpu.VMEM)
    hbm = pl.BlockSpec(memory_space=pl.ANY)
    dma = pltpu.SemaphoreType.DMA
    halo = jax.ShapeDtypeStruct((2, width, reach), bf16)
    stat = jax.ShapeDtypeStruct((2 * blocks, 1, QB), f32)
    left, right, spread, far, m, l, acc, bound, q = pl.pallas_call(
        functools.partial(head_kernel, rows, cols, coef),
        out_shape=(
            halo,
            halo,
            jax.ShapeDtypeStruct((full, chunk), bf16),
            jax.ShapeDtypeStruct((width, full), bf16),
            stat,
            stat,
            jax.ShapeDtypeStruct((2 * blocks, HEAD_DIM, QB), f32),
            jax.ShapeDtypeStruct((8, tokens), jnp.int32),
            jax.ShapeDtypeStruct((width, tokens), bf16),
        ),
        in_specs=[hbm, hbm, hbm, hbm],
        out_specs=(hbm, hbm, hbm, hbm, vmem, vmem, vmem, vmem, vmem),
        scratch_shapes=[
            dma((7,)),
            dma((4,)),
            dma((4,)),
            dma((cols,)),
            dma((cols,)),
            dma,
            dma,
            pltpu.VMEM((2, blocks, KB, QB), f32),
            pltpu.VMEM((tokens, width), bf16),
            pltpu.VMEM((2, HEAD_DIM, tokens), bf16),
            pltpu.VMEM((2, width, tokens), bf16),
            pltpu.VMEM((width, tokens), bf16),
            pltpu.VMEM((width, full), bf16),
            pltpu.VMEM((1, image_groups.shape[0]), jnp.int32),
        ],
        compiler_params=pltpu.CompilerParams(
            collective_id=1, has_side_effects=True, vmem_limit_bytes=50331648
        ),
    )(qkv, residual, merge_weight, image_groups[None, :])
    attended = pl.pallas_call(
        functools.partial(far_kernel, coef),
        out_shape=jax.ShapeDtypeStruct((width, tokens), bf16),
        in_specs=[smem, smem] + [vmem] * 7,
        out_specs=vmem,
        scratch_shapes=[
            pltpu.SMEM((blocks,), jnp.int32),
            pltpu.SMEM((blocks,), jnp.int32),
            pltpu.VMEM((2 * reach, width), bf16),
            pltpu.VMEM((2, HEAD_DIM, 2 * reach), bf16),
            pltpu.VMEM((2, 1, QB), f32),
            pltpu.VMEM((2, 1, QB), f32),
            pltpu.VMEM((2, HEAD_DIM, QB), f32),
        ],
        compiler_params=pltpu.CompilerParams(vmem_limit_bytes=20 << 20),
    )(image_groups, row_id[None], q, left, right, bound, m, l, acc)
    return attended, spread, far


def tail_kernel(
    rows,
    cols,
    attended_ref,
    residual_ref,
    weight,
    merge_weight_ref,
    far_weight_ref,
    gain_ref,
    dest_ref,
    layer_ref,
    got_rows,
    att,
    weight_t,
    merge_w,
    layer_rows,
    held,
    far_rows,
    merged,
    pick,
    sorted_rows,
    gain_column,
    load_sem,
    spread_send,
    spread_recv,
    back_send,
    back_recv,
    near_send,
    near_recv,
    own_send,
    own_recv,
    pass_send,
    pass_recv,
    far_send,
    far_recv,
    row_send,
    row_recv,
    far_w_send,
    far_w_recv,
):
    row = lax.axis_index("row")
    me = lax.axis_index("col")
    width, tokens = attended_ref.shape
    full = weight.shape[0]
    chunk = tokens // cols
    piece = chunk // PIECES
    part = piece // 4
    groups = tokens // 4
    share = groups // rows
    chips = cols // 2
    core = me % 2
    chip = me // 2
    sibling = me + 1 - 2 * core
    half = full // 2
    line_up = rows // 4

    barrier = pltpu.get_barrier_semaphore()
    for k in range(1, cols):
        pl.semaphore_signal(
            barrier, inc=1, device_id={"col": (me + k) % cols}, device_id_type=MESH
        )
    for k in range(1, rows):
        pl.semaphore_signal(
            barrier, inc=1, device_id={"row": (row + k) % rows}, device_id_type=MESH
        )
    far_at = pl.ds(pl.multiple_of(row // line_up * full, 128), full)
    far_place = merge_w.at[width : 2 * width, far_at]
    loads = [
        pltpu.make_async_copy(merge_weight_ref, merge_w.at[0:width], load_sem.at[0]),
        pltpu.make_async_copy(far_weight_ref, far_place, load_sem.at[1]),
    ]
    for load in loads:
        load.start()
    my_rows = pl.ds(pl.multiple_of(me * width, 16), width)
    pl.semaphore_wait(barrier, rows + cols - 2)

    def lanes(owner, p):
        return pl.ds(pl.multiple_of(owner * chunk + p * piece, 128), piece)

    spread = []
    for p in range(PIECES):
        for k in range(1, cols):
            to = (me + k) % cols
            copy = pltpu.make_async_remote_copy(
                src_ref=attended_ref.at[:, lanes(to, p)],
                dst_ref=att.at[p, my_rows],
                send_sem=spread_send.at[p, k],
                recv_sem=spread_recv.at[p, k],
                device_id={"col": to},
                device_id_type=MESH,
            )
            copy.start()
            spread.append(copy)
    gather = []
    for k in range(1, 4):
        copy = pltpu.make_async_remote_copy(
            src_ref=far_weight_ref,
            dst_ref=far_place,
            send_sem=far_w_send.at[k],
            recv_sem=far_w_recv.at[k],
            device_id={"row": (row + k * line_up) % rows},
            device_id_type=MESH,
        )
        copy.start()
        gather.append(copy)
    for p in range(PIECES):
        att[p, my_rows, :] = attended_ref[:, lanes(me, p)]

    def turn(i, carry):
        at = pl.multiple_of(i * 128, 128)
        weight_t[pl.ds(at, 128), :] = jnp.transpose(weight[:, pl.ds(at, 128)])
        return carry

    lax.fori_loop(0, full // 128, turn, 0)
    for i in range(full // 128):
        gain_column[i * 128 : (i + 1) * 128, :] = jnp.transpose(
            jnp.broadcast_to(gain_ref[i : i + 1, :], (8, 128))
        )

    before, after, across_chip = (chip + 3) % chips, (chip + 1) % chips, (chip + 2) % chips
    of = [dest_ref[pl.ds(c, 1), :] for c in (chip, before, across_chip, after)]
    span = chunk // 4
    line = jnp.concatenate(
        [
            of[c][:, k * span + p * part : k * span + (p + 1) * part]
            for order in (((0, 0), (0, 1), (1, 0), (3, 1)), ((2, 0), (2, 1), (3, 0), (1, 1)))
            for p in range(PIECES)
            for c, k in order
        ],
        axis=1,
    )
    owner_line = line // groups
    owner_column = jnp.transpose(
        jnp.broadcast_to(owner_line.astype(jnp.float32), (8, groups))
    )[:, 0:1].astype(jnp.int32)
    down = lax.broadcasted_iota(jnp.int32, (groups, groups), 0)
    across = lax.broadcasted_iota(jnp.int32, (groups, groups), 1)
    earlier = (owner_column == owner_line) & (down < across)
    rank = jnp.sum(earlier.astype(jnp.int32), axis=0, keepdims=True)
    pick[...] = jnp.where(down == owner_line * share + rank, 1.0, 0.0).astype(jnp.bfloat16)
    slot = line % groups
    which = lax.broadcasted_iota(jnp.int32, (merged.shape[0] - width, groups), 0)
    digits = jnp.where(which == 0, slot // 16, jnp.where(which == 1, slot % 16, 0))
    merged[width:, :] = digits.astype(jnp.float32).astype(jnp.bfloat16)

    here = lax.broadcasted_iota(jnp.int32, (piece, piece), 0)
    there = lax.broadcasted_iota(jnp.int32, (piece, piece), 1)
    order = jnp.where((here % 4) * part + here // 4 == there, 1.0, 0.0).astype(jnp.bfloat16)
    goal = (chip + 1 + 2 * core) % chips
    near, own, back = [], [], []
    for p in range(PIECES):
        for copy in spread[p * (cols - 1) : (p + 1) * (cols - 1)]:
            copy.wait()
        at = slice(p * piece, (p + 1) * piece)
        projected = jnp.dot(weight_t[...], att[p], preferred_element_type=jnp.float32)
        rounded = (residual_ref[:, at].astype(jnp.float32) + projected).astype(jnp.bfloat16)
        layer_rows[p] = rounded
        values32 = rounded.astype(jnp.float32)
        centre = jnp.sum(values32, axis=0, keepdims=True) * (1.0 / full)
        spread_of = jnp.sum(jnp.square(values32 - centre), axis=0, keepdims=True) * (1.0 / full)
        scale = lax.rsqrt(spread_of + 1e-06)
        normed = ((values32 - centre) * scale * gain_column[:, 0:1]).astype(jnp.bfloat16)
        held[p, core] = jnp.dot(normed, order, preferred_element_type=jnp.float32).astype(
            jnp.bfloat16
        )
        for h in range(2):
            rows_of = pl.ds(h * half, half)
            copy = pltpu.make_async_remote_copy(
                src_ref=held.at[p, core, rows_of],
                dst_ref=held.at[p, 2 + core, rows_of],
                send_sem=near_send.at[p, h],
                recv_sem=near_recv.at[p, core],
                device_id={"col": goal * 2 + h},
                device_id_type=MESH,
            )
            copy.start()
            near.append(copy)
        copy = pltpu.make_async_remote_copy(
            src_ref=held.at[p, core],
            dst_ref=held.at[p, core],
            send_sem=own_send.at[p],
            recv_sem=own_recv.at[p],
            device_id={"col": sibling},
            device_id_type=MESH,
        )
        copy.start()
        own.append(copy)
        layer_ref[:, lanes(me, p)] = layer_rows[p, my_rows, :]

    passed = []
    my_half = pl.ds(pl.multiple_of(core * half, 16), half)
    for p in range(PIECES):
        for s in range(2):
            arrive = pltpu.make_async_remote_copy(
                src_ref=held.at[p, core, my_half],
                dst_ref=held.at[p, 2 + s, my_half],
                send_sem=near_send.at[p, s],
                recv_sem=near_recv.at[p, s],
                device_id={"col": sibling},
                device_id_type=MESH,
            )
            arrive.wait_recv()
            copy = pltpu.make_async_remote_copy(
                src_ref=held.at[p, 2 + s, my_half],
                dst_ref=held.at[p, 2 + s, my_half],
                send_sem=pass_send.at[p, s],
                recv_sem=pass_recv.at[p, s],
                device_id={"col": sibling},
                device_id_type=MESH,
            )
            copy.start()
            passed.append(copy)
    for copy in near:
        copy.wait_send()

    def send_back(p):
        for k in range(1, cols):
            to = (me + k) % cols
            copy = pltpu.make_async_remote_copy(
                src_ref=layer_rows.at[p, pl.ds(pl.multiple_of(to * width, 16), width)],
                dst_ref=layer_ref.at[:, lanes(me, p)],
                send_sem=back_send.at[p, k],
                recv_sem=back_recv.at[p, k],
                device_id={"col": to},
                device_id_type=MESH,
            )
            copy.start()
            back.append(copy)

    for p in range(PIECES - 1):
        send_back(p)
    for load in loads:
        load.wait()
    for copy in gather:
        copy.wait()
    for copy in own + passed:
        copy.wait()

    total = None
    for j in range(4):
        side = jnp.concatenate(
            [
                held[p, s, :, j * part : (j + 1) * part]
                for p in range(PIECES)
                for s in range(4)
            ],
            axis=1,
        )
        term = jnp.dot(
            merge_w[:, j * full : (j + 1) * full], side, preferred_element_type=jnp.float32
        )
        total = term if total is None else total + term
    far_rows[...] = total[width:].astype(jnp.bfloat16)
    across_y = pltpu.make_async_remote_copy(
        src_ref=far_rows,
        dst_ref=merged.at[0:width, chunk : 2 * chunk],
        send_sem=far_send,
        recv_sem=far_recv,
        device_id={"col": (me + cols // 2) % cols},
        device_id_type=MESH,
    )
    across_y.start()
    send_back(PIECES - 1)
    merged[0:width, 0:chunk] = total[:width].astype(jnp.bfloat16)
    across_y.wait()

    sorted_rows[...] = lax.dot_general(
        pick[...], merged[...], (((1,), (1,)), ((), ())), preferred_element_type=jnp.float32
    ).astype(jnp.bfloat16)
    moves = []
    for k in range(1, rows):
        to = (row + k) % rows
        copy = pltpu.make_async_remote_copy(
            src_ref=sorted_rows.at[pl.ds(pl.multiple_of(to * share, share), share)],
            dst_ref=got_rows.at[pl.ds(pl.multiple_of(row * share, share), share)],
            send_sem=row_send.at[k],
            recv_sem=row_recv.at[k],
            device_id={"row": to},
            device_id_type=MESH,
        )
        copy.start()
        moves.append(copy)
    keep = pl.ds(pl.multiple_of(row * share, share), share)
    got_rows[keep, :] = sorted_rows[keep, :]
    for copy in moves + back:
        copy.wait()


def place_kernel(layer_ref, got_ref, layer_out, image_ref, sem):
    copy = pltpu.make_async_copy(layer_ref, layer_out, sem)
    copy.start()
    width, groups = image_ref.shape
    got = got_ref[...]
    target = got[:, width : width + 1].astype(jnp.float32) * 16.0 + got[
        :, width + 1 : width + 2
    ].astype(jnp.float32)
    slot = lax.broadcasted_iota(jnp.int32, (groups, groups), 1).astype(jnp.float32)
    put = jnp.where(target == slot, 1.0, 0.0).astype(jnp.bfloat16)
    image_ref[...] = lax.dot_general(
        got, put, (((0,), (0,)), ((), ())), preferred_element_type=jnp.float32
    )[:width].astype(jnp.bfloat16)
    copy.wait()


def tail(attended, residual, out_weight, merge_weight, far_weight, gain, dest_row, rows, cols):
    width, tokens = attended.shape
    full = out_weight.shape[0]
    chunk = tokens // cols
    piece = chunk // PIECES
    groups = tokens // 4
    bf16 = jnp.bfloat16
    vmem = pl.BlockSpec(memory_space=pltpu.VMEM)
    hbm = pl.BlockSpec(memory_space=pl.ANY)
    dma = pltpu.SemaphoreType.DMA
    layer, got = pl.pallas_call(
        functools.partial(tail_kernel, rows, cols),
        out_shape=(
            jax.ShapeDtypeStruct((width, tokens), bf16),
            jax.ShapeDtypeStruct((groups, width + 16), bf16),
        ),
        in_specs=[vmem] * 7,
        out_specs=(vmem, vmem),
        scratch_shapes=[
            pltpu.VMEM((PIECES, full, piece), bf16),
            pltpu.VMEM((full, full), bf16),
            pltpu.VMEM((2 * width, merge_weight.shape[1]), bf16),
            pltpu.VMEM((PIECES, full, piece), bf16),
            pltpu.VMEM((PIECES, 4, full, piece), bf16),
            pltpu.VMEM((width, chunk), bf16),
            pltpu.VMEM((width + 16, groups), bf16),
            pltpu.VMEM((groups, groups), bf16),
            pltpu.VMEM((groups, width + 16), bf16),
            pltpu.VMEM((full, 8), jnp.float32),
            dma((2,)),
            dma((PIECES, cols)),
            dma((PIECES, cols)),
            dma((PIECES, cols)),
            dma((PIECES, cols)),
            dma((PIECES, 2)),
            dma((PIECES, 2)),
            dma((PIECES,)),
            dma((PIECES,)),
            dma((PIECES, 2)),
            dma((PIECES, 2)),
            dma,
            dma,
            dma((rows,)),
            dma((rows,)),
            dma((4,)),
            dma((4,)),
        ],
        compiler_params=pltpu.CompilerParams(
            collective_id=0, has_side_effects=True, vmem_limit_bytes=40 << 20
        ),
    )(
        attended,
        residual,
        out_weight,
        merge_weight,
        far_weight,
        gain.reshape(-1, 128),
        dest_row.reshape(cols // 2, -1),
    )
    return pl.pallas_call(
        place_kernel,
        out_shape=(
            jax.ShapeDtypeStruct((width, tokens), bf16),
            jax.ShapeDtypeStruct((width, groups), bf16),
        ),
        in_specs=[vmem, vmem],
        out_specs=(hbm, vmem),
        scratch_shapes=[dma],
        compiler_params=pltpu.CompilerParams(vmem_limit_bytes=16 << 20),
    )(layer, got)


def body(qkv, residual_in, out_weight, merge_weight, merge_gain, image_groups, dest_row):
    rows = lax.axis_size("row")
    cols = lax.axis_size("col")
    row_id = lax.axis_index("row")
    attended, residual, far_weight = attention(
        qkv, residual_in, merge_weight, image_groups, row_id, out_weight.shape[0], rows, cols
    )
    return tail(
        attended, residual, out_weight, merge_weight, far_weight, merge_gain, dest_row, rows, cols
    )


def solution(mesh):
    return jax.shard_map(
        body,
        mesh=mesh,
        in_specs=(P(None, "col", "row"), P("col", "row"), P(), P("col", None), P(), P(), P("row")),
        out_specs=(P("col", "row"), P("col", "row")),
        check_vma=False,
    )
```

```python
import functools
import math

import jax
import jax.numpy as jnp
from jax import lax
from jax.experimental import pallas as pl
from jax.experimental.pallas import tpu as pltpu
from jax.sharding import PartitionSpec as P

HEAD_DIM = 88
QB = 256
KB = 256
HB = 512
PIECES = 2
NEG = -1e30
MESH = pl.DeviceIdType.MESH


def halo_step(keys, values, qcat, ok, coef, m_ref, l_ref, acc_ref):
    width = qcat.shape[1] // 2
    scores = jnp.dot(keys, qcat, preferred_element_type=jnp.float32)
    for head in range(2):
        part = jnp.where(ok, scores[:, head * width : (head + 1) * width], NEG)
        old = m_ref[head]
        new = jnp.maximum(old, jnp.max(part, axis=0, keepdims=True))
        fade = jnp.exp2((old - new) * coef)
        expo = jnp.exp2(part * coef - new * coef)
        l_ref[head] = l_ref[head] * fade + jnp.sum(expo, axis=0, keepdims=True)
        m_ref[head] = new
        acc_ref[head] = acc_ref[head] * fade + jnp.dot(
            values[head], expo.astype(jnp.bfloat16), preferred_element_type=jnp.float32
        )


def split_heads(values):
    wide = values.astype(jnp.float32)
    return wide[:HEAD_DIM].astype(jnp.bfloat16), wide[HEAD_DIM:].astype(jnp.bfloat16)


def query_pair(block):
    feature = lax.broadcasted_iota(jnp.int32, block.shape, 0)
    zero = jnp.zeros_like(block)
    return jnp.concatenate(
        [jnp.where(feature < HEAD_DIM, block, zero), jnp.where(feature < HEAD_DIM, zero, block)],
        axis=1,
    )


def layer_kernel(
    rows,
    cols,
    coef,
    qkv_hbm,
    residual_hbm,
    out_weight_hbm,
    merge_weight_hbm,
    gain_hbm,
    groups_hbm,
    dest_hbm,
    layer_ref,
    got_rows,
    q_ref,
    kv,
    kt,
    vt,
    left,
    right,
    halo_kt,
    halo_vt,
    bound_ref,
    held_scores,
    m_ref,
    l_ref,
    acc_ref,
    attended,
    res,
    residual,
    att,
    weight,
    weight_t,
    merge_w,
    layer_rows,
    held,
    far_rows,
    merged,
    pick,
    sorted_rows,
    gain_column,
    gain_ref,
    groups_line_ref,
    dest_ref,
    load_sem,
    halo_send,
    halo_recv,
    res_send,
    res_recv,
    shift_send,
    shift_recv,
    gather_send,
    gather_recv,
    spread_send,
    spread_recv,
    back_send,
    back_recv,
    near_send,
    near_recv,
    own_send,
    own_recv,
    pass_send,
    pass_recv,
    far_send,
    far_recv,
    row_send,
    row_recv,
):
    row = lax.axis_index("row")
    me = lax.axis_index("col")
    width, tokens = q_ref.shape
    full = weight.shape[0]
    reach = left.shape[2]
    blocks = tokens // QB
    chunk = tokens // cols
    piece = chunk // PIECES
    part = piece // 4
    groups = tokens // 4
    share = groups // rows
    chips = cols // 2
    core = me % 2
    chip = me // 2
    sibling = me + 1 - 2 * core
    half = full // 2
    line_up = rows // 4
    x_at, z_at = row // line_up, row % line_up

    barrier = pltpu.get_barrier_semaphore()
    for k in range(1, cols):
        pl.semaphore_signal(
            barrier, inc=1, device_id={"col": (me + k) % cols}, device_id_type=MESH
        )
    for k in range(1, rows):
        pl.semaphore_signal(
            barrier, inc=1, device_id={"row": (row + k) % rows}, device_id_type=MESH
        )
    loads = [
        pltpu.make_async_copy(source, target, load_sem.at[i])
        for i, (source, target) in enumerate(
            (
                (qkv_hbm.at[1], kv.at[0]),
                (qkv_hbm.at[2], kv.at[1]),
                (merge_weight_hbm, merge_w.at[0:width]),
                (residual_hbm, res),
                (groups_hbm, groups_line_ref),
                (qkv_hbm.at[0], q_ref),
                (gain_hbm, gain_ref),
                (dest_hbm, dest_ref),
                (out_weight_hbm, weight),
            )
        )
    ]
    for load in loads:
        load.start()
    for load in loads[:4]:
        load.wait()
    pl.semaphore_wait(barrier, rows + cols - 2)

    after_row, before_row = (row + 1) % rows, (row + rows - 1) % rows
    mine = pl.ds(pl.multiple_of(me * chunk, chunk), chunk)
    my_rows = pl.ds(pl.multiple_of(me * width, 16), width)
    halo = []
    for side, (other, target, at) in enumerate(
        ((after_row, left, tokens - reach), (before_row, right, 0))
    ):
        for i in range(2):
            halo.append(
                pltpu.make_async_remote_copy(
                    src_ref=kv.at[i, :, at : at + reach],
                    dst_ref=target.at[i],
                    send_sem=halo_send.at[2 * side + i],
                    recv_sem=halo_recv.at[2 * side + i],
                    device_id={"row": other},
                    device_id_type=MESH,
                )
            )
    cut = width // 32 * 16 + 16
    spans = ((0, cut, x_at), (cut, width, z_at))
    shift, gather = [], []
    for s, (top, end, at) in enumerate(spans):
        across = pl.ds(pl.multiple_of(at * full, 128), full)
        place = merge_w.at[width + top : width + end, across]
        shift.append(
            pltpu.make_async_remote_copy(
                src_ref=merge_w.at[top:end, across],
                dst_ref=place,
                send_sem=shift_send.at[s],
                recv_sem=shift_recv.at[s],
                device_id={"col": (me + cols // 2) % cols},
                device_id_type=MESH,
            )
        )
        for k in range(1, 4):
            other = x_at * line_up + (z_at + k) % line_up if s else (row + k * line_up) % rows
            gather.append(
                pltpu.make_async_remote_copy(
                    src_ref=place,
                    dst_ref=place,
                    send_sem=gather_send.at[s, k],
                    recv_sem=gather_recv.at[s, k],
                    device_id={"row": other},
                    device_id_type=MESH,
                )
            )
    resident = []
    for k in range(1, cols):
        to = (me + k) % cols
        resident.append(
            pltpu.make_async_remote_copy(
                src_ref=res.at[:, pl.ds(pl.multiple_of(to * chunk, chunk), chunk)],
                dst_ref=residual.at[my_rows],
                send_sem=res_send.at[k],
                recv_sem=res_recv.at[k],
                device_id={"col": to},
                device_id_type=MESH,
            )
        )
    for copy in halo + shift + resident:
        copy.start()
    residual[my_rows, :] = res[:, mine]
    for load in loads[4:]:
        load.wait()

    images = groups_line_ref.shape[1]
    first = lax.broadcasted_iota(jnp.int32, (images, images), 0)
    second = lax.broadcasted_iota(jnp.int32, (images, images), 1)
    sizes = groups_line_ref[...]
    size = jnp.sum(jnp.where(second == first, sizes, 0), axis=1, keepdims=True) * 4
    begin = (
        jnp.sum(jnp.where(second < first, sizes, 0), axis=1, keepdims=True) * 4 - row * tokens
    )

    def prepare(b, carry):
        at = pl.multiple_of(b * QB, QB)
        token = lax.broadcasted_iota(jnp.int32, (images, QB), 1) + at
        inside = (token >= begin) & (token < begin + size)
        bound_ref[0:1, pl.ds(at, QB)] = jnp.sum(jnp.where(inside, begin, 0), axis=0, keepdims=True)
        bound_ref[1:2, pl.ds(at, QB)] = jnp.sum(jnp.where(inside, size, 0), axis=0, keepdims=True)
        kt[pl.ds(at, QB), :] = jnp.transpose(kv[0, :, pl.ds(at, QB)])
        v0, v1 = split_heads(kv[1, :, pl.ds(at, QB)])
        vt[0, :, pl.ds(at, QB)] = v0
        vt[1, :, pl.ds(at, QB)] = v1
        return carry

    lax.fori_loop(0, blocks, prepare, 0)

    def local_block(b, carry):
        at = pl.multiple_of(b * QB, QB)
        qcat = query_pair(q_ref[:, pl.ds(at, QB)])
        start = bound_ref[0:1, pl.ds(at, QB)]
        length = bound_ref[1:2, pl.ds(at, QB)]
        spot = lax.broadcasted_iota(jnp.int32, (KB, QB), 0) - start
        tops = [jnp.full((1, QB), NEG, jnp.float32) for _ in range(2)]
        for t in range(blocks):
            key = t * KB
            scores = jnp.dot(kt[key : key + KB, :], qcat, preferred_element_type=jnp.float32)
            ok = (spot >= -key) & (spot < length - key)
            for head in range(2):
                masked = jnp.where(ok, scores[:, head * QB : (head + 1) * QB], NEG)
                held_scores[head, t] = masked
                tops[head] = jnp.maximum(tops[head], jnp.max(masked, axis=0, keepdims=True))
        for head in range(2):
            peak = tops[head] * coef
            total = jnp.zeros((1, QB), jnp.float32)
            sums = jnp.zeros((HEAD_DIM, QB), jnp.float32)
            for t in range(blocks):
                expo = jnp.exp2(held_scores[head, t] * coef - peak)
                total = total + jnp.sum(expo, axis=0, keepdims=True)
                sums = sums + jnp.dot(
                    vt[head, :, t * KB : (t + 1) * KB],
                    expo.astype(jnp.bfloat16),
                    preferred_element_type=jnp.float32,
                )
            m_ref[b * 2 + head] = tops[head]
            l_ref[b * 2 + head] = total
            acc_ref[b * 2 + head] = sums
        return carry

    lax.fori_loop(0, blocks, local_block, 0)

    def turn(i, carry):
        at = pl.multiple_of(i * 128, 128)
        weight_t[pl.ds(at, 128), :] = jnp.transpose(weight[:, pl.ds(at, 128)])
        return carry

    lax.fori_loop(0, full // 128, turn, 0)
    for i in range(full // 128):
        gain_column[i * 128 : (i + 1) * 128, :] = jnp.transpose(
            jnp.broadcast_to(gain_ref[i : i + 1, :], (8, 128))
        )

    before, after, across_chip = (chip + 3) % chips, (chip + 1) % chips, (chip + 2) % chips
    of = [dest_ref[pl.ds(c, 1), :] for c in (chip, before, across_chip, after)]
    span = chunk // 4
    line = jnp.concatenate(
        [
            of[c][:, k * span + p * part : k * span + (p + 1) * part]
            for order in (((0, 0), (0, 1), (1, 0), (3, 1)), ((2, 0), (2, 1), (3, 0), (1, 1)))
            for p in range(PIECES)
            for c, k in order
        ],
        axis=1,
    )
    owner_line = line // groups
    owner_column = jnp.transpose(
        jnp.broadcast_to(owner_line.astype(jnp.float32), (8, groups))
    )[:, 0:1].astype(jnp.int32)
    down = lax.broadcasted_iota(jnp.int32, (groups, groups), 0)
    across = lax.broadcasted_iota(jnp.int32, (groups, groups), 1)
    earlier = (owner_column == owner_line) & (down < across)
    rank = jnp.sum(earlier.astype(jnp.int32), axis=0, keepdims=True)
    pick[...] = jnp.where(down == owner_line * share + rank, 1.0, 0.0).astype(jnp.bfloat16)
    slot = line % groups
    which = lax.broadcasted_iota(jnp.int32, (merged.shape[0] - width, groups), 0)
    digits = jnp.where(which == 0, slot // 16, jnp.where(which == 1, slot % 16, 0))
    merged[width:, :] = digits.astype(jnp.float32).astype(jnp.bfloat16)

    for copy in shift:
        copy.wait_recv()
    for copy in gather:
        copy.start()
    for copy in halo:
        copy.wait_recv()

    def prepare_halo(i, carry):
        at = pl.multiple_of(i * QB, QB)
        for source, base in ((left, 0), (right, reach)):
            to = pl.ds(pl.multiple_of(base + at, QB), QB)
            halo_kt[to, :] = jnp.transpose(source[0, :, pl.ds(at, QB)])
            v0, v1 = split_heads(source[1, :, pl.ds(at, QB)])
            halo_vt[0, :, to] = v0
            halo_vt[1, :, to] = v1
        return carry

    lax.fori_loop(0, reach // QB, prepare_halo, 0)

    def spread_copy(k):
        to = (me + k) % cols
        return pltpu.make_async_remote_copy(
            src_ref=attended.at[to],
            dst_ref=att.at[my_rows],
            send_sem=spread_send.at[k],
            recv_sem=spread_recv.at[k],
            device_id={"col": to},
            device_id_type=MESH,
        )

    def halo_block(b):
        at = pl.multiple_of(b * QB, QB)
        qcat = query_pair(q_ref[:, pl.ds(at, QB)])
        start = bound_ref[0:1, pl.ds(at, QB)]
        length = bound_ref[1:2, pl.ds(at, QB)]
        high = b // (blocks // 2)
        tiles = high * (b - blocks // 2 + 1) + (1 - high) * (blocks // 2 - b)

        def pair(t, inner):
            slot = high * (reach + t * HB) + (1 - high) * (reach - (t + 1) * HB)
            slot = pl.multiple_of(slot, HB)
            key = slot - reach + high * tokens
            spot = lax.broadcasted_iota(jnp.int32, (HB, QB), 0) + (key - start)
            ok = (spot >= 0) & (spot < length)
            halo_step(
                halo_kt[pl.ds(slot, HB), :],
                [halo_vt[head, :, pl.ds(slot, HB)] for head in range(2)],
                qcat,
                ok,
                coef,
                m_ref.at[pl.ds(b * 2, 2)],
                l_ref.at[pl.ds(b * 2, 2)],
                acc_ref.at[pl.ds(b * 2, 2)],
            )
            return inner

        lax.fori_loop(0, (tiles * KB + HB - 1) // HB, pair, 0)
        both = [acc_ref[b * 2 + head] * (1.0 / l_ref[b * 2 + head]) for head in range(2)]
        attended[b] = jnp.concatenate(both, axis=0).astype(jnp.bfloat16)

    def block_of(i, carry):
        halo_block((me + 1 + i) % cols)
        spread_copy(1 + i).start()
        return carry

    lax.fori_loop(0, cols - 1, block_of, 0)
    halo_block(me)
    att[my_rows, :] = attended[me]
    for copy in resident:
        copy.wait()
    for k in range(1, cols):
        spread_copy(k).wait_recv()

    def lanes(owner, p):
        return pl.ds(pl.multiple_of(owner * chunk + p * piece, 128), piece)

    here = lax.broadcasted_iota(jnp.int32, (piece, piece), 0)
    there = lax.broadcasted_iota(jnp.int32, (piece, piece), 1)
    order = jnp.where((here % 4) * part + here // 4 == there, 1.0, 0.0).astype(jnp.bfloat16)
    goal = (chip + 1 + 2 * core) % chips
    near, own, back = [], [], []
    for p in range(PIECES):
        at = slice(p * piece, (p + 1) * piece)
        projected = jnp.dot(weight_t[...], att[:, at], preferred_element_type=jnp.float32)
        rounded = (residual[:, at].astype(jnp.float32) + projected).astype(jnp.bfloat16)
        layer_rows[p] = rounded
        values32 = rounded.astype(jnp.float32)
        centre = jnp.sum(values32, axis=0, keepdims=True) * (1.0 / full)
        spread_of = jnp.sum(jnp.square(values32 - centre), axis=0, keepdims=True) * (1.0 / full)
        scale = lax.rsqrt(spread_of + 1e-06)
        normed = ((values32 - centre) * scale * gain_column[:, 0:1]).astype(jnp.bfloat16)
        held[p, core] = jnp.dot(normed, order, preferred_element_type=jnp.float32).astype(
            jnp.bfloat16
        )
        for h in range(2):
            rows_of = pl.ds(h * half, half)
            copy = pltpu.make_async_remote_copy(
                src_ref=held.at[p, core, rows_of],
                dst_ref=held.at[p, 2 + core, rows_of],
                send_sem=near_send.at[p, h],
                recv_sem=near_recv.at[p, core],
                device_id={"col": goal * 2 + h},
                device_id_type=MESH,
            )
            copy.start()
            near.append(copy)
        copy = pltpu.make_async_remote_copy(
            src_ref=held.at[p, core],
            dst_ref=held.at[p, core],
            send_sem=own_send.at[p],
            recv_sem=own_recv.at[p],
            device_id={"col": sibling},
            device_id_type=MESH,
        )
        copy.start()
        own.append(copy)
        layer_ref[:, lanes(me, p)] = layer_rows[p, my_rows, :]

    for k in range(1, cols):
        spread_copy(k).wait_send()
    passed = []
    my_half = pl.ds(pl.multiple_of(core * half, 16), half)
    for p in range(PIECES):
        for s in range(2):
            arrive = pltpu.make_async_remote_copy(
                src_ref=held.at[p, core, my_half],
                dst_ref=held.at[p, 2 + s, my_half],
                send_sem=near_send.at[p, s],
                recv_sem=near_recv.at[p, s],
                device_id={"col": sibling},
                device_id_type=MESH,
            )
            arrive.wait_recv()
            copy = pltpu.make_async_remote_copy(
                src_ref=held.at[p, 2 + s, my_half],
                dst_ref=held.at[p, 2 + s, my_half],
                send_sem=pass_send.at[p, s],
                recv_sem=pass_recv.at[p, s],
                device_id={"col": sibling},
                device_id_type=MESH,
            )
            copy.start()
            passed.append(copy)
    for copy in near:
        copy.wait_send()

    def send_back(p):
        for k in range(1, cols):
            to = (me + k) % cols
            copy = pltpu.make_async_remote_copy(
                src_ref=layer_rows.at[p, pl.ds(pl.multiple_of(to * width, 16), width)],
                dst_ref=layer_ref.at[:, lanes(me, p)],
                send_sem=back_send.at[p, k],
                recv_sem=back_recv.at[p, k],
                device_id={"col": to},
                device_id_type=MESH,
            )
            copy.start()
            back.append(copy)

    for p in range(PIECES - 1):
        send_back(p)
    for copy in gather:
        copy.wait()
    for copy in own + passed:
        copy.wait()

    total = None
    for j in range(4):
        side = jnp.concatenate(
            [
                held[p, s, :, j * part : (j + 1) * part]
                for p in range(PIECES)
                for s in range(4)
            ],
            axis=1,
        )
        term = jnp.dot(
            merge_w[:, j * full : (j + 1) * full], side, preferred_element_type=jnp.float32
        )
        total = term if total is None else total + term
    far_rows[...] = total[width:].astype(jnp.bfloat16)
    across_y = pltpu.make_async_remote_copy(
        src_ref=far_rows,
        dst_ref=merged.at[0:width, chunk : 2 * chunk],
        send_sem=far_send,
        recv_sem=far_recv,
        device_id={"col": (me + cols // 2) % cols},
        device_id_type=MESH,
    )
    across_y.start()
    send_back(PIECES - 1)
    merged[0:width, 0:chunk] = total[:width].astype(jnp.bfloat16)
    across_y.wait()

    sorted_rows[...] = lax.dot_general(
        pick[...], merged[...], (((1,), (1,)), ((), ())), preferred_element_type=jnp.float32
    ).astype(jnp.bfloat16)
    moves = []
    for k in range(1, rows):
        to = (row + k) % rows
        copy = pltpu.make_async_remote_copy(
            src_ref=sorted_rows.at[pl.ds(pl.multiple_of(to * share, share), share)],
            dst_ref=got_rows.at[pl.ds(pl.multiple_of(row * share, share), share)],
            send_sem=row_send.at[k],
            recv_sem=row_recv.at[k],
            device_id={"row": to},
            device_id_type=MESH,
        )
        copy.start()
        moves.append(copy)
    keep = pl.ds(pl.multiple_of(row * share, share), share)
    got_rows[keep, :] = sorted_rows[keep, :]
    for copy in moves + back:
        copy.wait()
    for copy in halo + shift:
        copy.wait_send()


def place_kernel(layer_ref, got_ref, layer_out, image_ref, sem):
    copy = pltpu.make_async_copy(layer_ref, layer_out, sem)
    copy.start()
    width, groups = image_ref.shape
    got = got_ref[...]
    target = got[:, width : width + 1].astype(jnp.float32) * 16.0 + got[
        :, width + 1 : width + 2
    ].astype(jnp.float32)
    slot = lax.broadcasted_iota(jnp.int32, (groups, groups), 1).astype(jnp.float32)
    put = jnp.where(target == slot, 1.0, 0.0).astype(jnp.bfloat16)
    image_ref[...] = lax.dot_general(
        got, put, (((0,), (0,)), ((), ())), preferred_element_type=jnp.float32
    )[:width].astype(jnp.bfloat16)
    copy.wait()


def body(qkv, residual_in, out_weight, merge_weight, merge_gain, image_groups, dest_row):
    rows = lax.axis_size("row")
    cols = lax.axis_size("col")
    _, width, tokens = qkv.shape
    full = out_weight.shape[0]
    reach = tokens // 2
    blocks = tokens // QB
    chunk = tokens // cols
    piece = chunk // PIECES
    groups = tokens // 4
    bf16, f32, i32 = jnp.bfloat16, jnp.float32, jnp.int32
    coef = math.log2(math.e) / math.sqrt(HEAD_DIM)
    vmem = pl.BlockSpec(memory_space=pltpu.VMEM)
    hbm = pl.BlockSpec(memory_space=pl.ANY)
    dma = pltpu.SemaphoreType.DMA
    gain = merge_gain.reshape(-1, 128)
    dest = dest_row.reshape(cols // 2, -1)
    sizes = image_groups[None, :]
    layer, got = pl.pallas_call(
        functools.partial(layer_kernel, rows, cols, coef),
        out_shape=(
            jax.ShapeDtypeStruct((width, tokens), bf16),
            jax.ShapeDtypeStruct((groups, width + 16), bf16),
        ),
        in_specs=[hbm] * 7,
        out_specs=(vmem, vmem),
        scratch_shapes=[
            pltpu.VMEM((width, tokens), bf16),
            pltpu.VMEM((2, width, tokens), bf16),
            pltpu.VMEM((tokens, width), bf16),
            pltpu.VMEM((2, HEAD_DIM, tokens), bf16),
            pltpu.VMEM((2, width, reach), bf16),
            pltpu.VMEM((2, width, reach), bf16),
            pltpu.VMEM((2 * reach, width), bf16),
            pltpu.VMEM((2, HEAD_DIM, 2 * reach), bf16),
            pltpu.VMEM((8, tokens), i32),
            pltpu.VMEM((2, blocks, KB, QB), f32),
            pltpu.VMEM((2 * blocks, 1, QB), f32),
            pltpu.VMEM((2 * blocks, 1, QB), f32),
            pltpu.VMEM((2 * blocks, HEAD_DIM, QB), f32),
            pltpu.VMEM((blocks, width, QB), bf16),
            pltpu.VMEM((width, tokens), bf16),
            pltpu.VMEM((full, chunk), bf16),
            pltpu.VMEM((full, chunk), bf16),
            pltpu.VMEM((full, full), bf16),
            pltpu.VMEM((full, full), bf16),
            pltpu.VMEM((2 * width, merge_weight.shape[1]), bf16),
            pltpu.VMEM((PIECES, full, piece), bf16),
            pltpu.VMEM((PIECES, 4, full, piece), bf16),
            pltpu.VMEM((width, chunk), bf16),
            pltpu.VMEM((width + 16, groups), bf16),
            pltpu.VMEM((groups, groups), bf16),
            pltpu.VMEM((groups, width + 16), bf16),
            pltpu.VMEM((full, 8), f32),
            pltpu.VMEM(gain.shape, f32),
            pltpu.VMEM(sizes.shape, i32),
            pltpu.VMEM(dest.shape, i32),
            dma((9,)),
            dma((4,)),
            dma((4,)),
            dma((cols,)),
            dma((cols,)),
            dma((2,)),
            dma((2,)),
            dma((2, 4)),
            dma((2, 4)),
            dma((cols,)),
            dma((cols,)),
            dma((PIECES, cols)),
            dma((PIECES, cols)),
            dma((PIECES, 2)),
            dma((PIECES, 2)),
            dma((PIECES,)),
            dma((PIECES,)),
            dma((PIECES, 2)),
            dma((PIECES, 2)),
            dma,
            dma,
            dma((rows,)),
            dma((rows,)),
        ],
        compiler_params=pltpu.CompilerParams(
            collective_id=0, has_side_effects=True, vmem_limit_bytes=int(60 * 2**20)
        ),
    )(qkv, residual_in, out_weight, merge_weight, gain, sizes, dest)
    return pl.pallas_call(
        place_kernel,
        out_shape=(
            jax.ShapeDtypeStruct((width, tokens), bf16),
            jax.ShapeDtypeStruct((width, groups), bf16),
        ),
        in_specs=[vmem, vmem],
        out_specs=(hbm, vmem),
        scratch_shapes=[dma],
        compiler_params=pltpu.CompilerParams(vmem_limit_bytes=16 << 20),
    )(layer, got)


def solution(mesh):
    return jax.shard_map(
        body,
        mesh=mesh,
        in_specs=(P(None, "col", "row"), P("col", "row"), P(), P("col", None), P(), P(), P("row")),
        out_specs=(P("col", "row"), P("col", "row")),
        check_vma=False,
    )
```

```python
import functools
import math

import jax
import jax.numpy as jnp
from jax import lax
from jax.experimental import pallas as pl
from jax.experimental.pallas import tpu as pltpu
from jax.sharding import PartitionSpec as P

HEAD_DIM = 88
QB = 256
KB = 256
HB = 512
PIECES = 2
NEG = -1e30
MESH = pl.DeviceIdType.MESH


def halo_step(keys, values, qcat, ok, coef, m_ref, l_ref, acc_ref):
    width = qcat.shape[1] // 2
    scores = jnp.dot(keys, qcat, preferred_element_type=jnp.float32)
    for head in range(2):
        part = jnp.where(ok, scores[:, head * width : (head + 1) * width], NEG)
        old = m_ref[head]
        new = jnp.maximum(old, jnp.max(part, axis=0, keepdims=True))
        fade = jnp.exp2((old - new) * coef)
        expo = jnp.exp2(part * coef - new * coef)
        l_ref[head] = l_ref[head] * fade + jnp.sum(expo, axis=0, keepdims=True)
        m_ref[head] = new
        acc_ref[head] = acc_ref[head] * fade + jnp.dot(
            values[head], expo.astype(jnp.bfloat16), preferred_element_type=jnp.float32
        )


def split_heads(values):
    wide = values.astype(jnp.float32)
    return wide[:HEAD_DIM].astype(jnp.bfloat16), wide[HEAD_DIM:].astype(jnp.bfloat16)


def query_pair(block):
    feature = lax.broadcasted_iota(jnp.int32, block.shape, 0)
    zero = jnp.zeros_like(block)
    return jnp.concatenate(
        [jnp.where(feature < HEAD_DIM, block, zero), jnp.where(feature < HEAD_DIM, zero, block)],
        axis=1,
    )


def layer_kernel(
    rows,
    cols,
    coef,
    qkv_hbm,
    residual_hbm,
    out_weight_hbm,
    merge_weight_hbm,
    gain_hbm,
    groups_hbm,
    dest_hbm,
    layer_ref,
    got_rows,
    q_ref,
    kv,
    kt,
    vt,
    left,
    right,
    halo_kt,
    halo_vt,
    bound_ref,
    held_scores,
    m_ref,
    l_ref,
    acc_ref,
    attended,
    res,
    residual,
    att,
    weight,
    weight_t,
    merge_w,
    layer_rows,
    held,
    far_rows,
    merged,
    pick,
    sorted_rows,
    gain_column,
    gain_ref,
    groups_line_ref,
    dest_ref,
    load_sem,
    halo_send,
    halo_recv,
    res_send,
    res_recv,
    shift_send,
    shift_recv,
    gather_send,
    gather_recv,
    spread_send,
    spread_recv,
    back_send,
    back_recv,
    near_send,
    near_recv,
    own_send,
    own_recv,
    pass_send,
    pass_recv,
    far_send,
    far_recv,
    row_send,
    row_recv,
):
    row = lax.axis_index("row")
    me = lax.axis_index("col")
    width, tokens = q_ref.shape
    full = weight.shape[0]
    reach = left.shape[2]
    blocks = tokens // QB
    chunk = tokens // cols
    piece = chunk // PIECES
    part = piece // 4
    groups = tokens // 4
    share = groups // rows
    chips = cols // 2
    core = me % 2
    chip = me // 2
    sibling = me + 1 - 2 * core
    half = full // 2
    line_up = rows // 4
    x_at, z_at = row // line_up, row % line_up

    barrier = pltpu.get_barrier_semaphore()
    for k in range(1, cols):
        pl.semaphore_signal(
            barrier, inc=1, device_id={"col": (me + k) % cols}, device_id_type=MESH
        )
    for k in range(1, rows):
        pl.semaphore_signal(
            barrier, inc=1, device_id={"row": (row + k) % rows}, device_id_type=MESH
        )
    loads = [
        pltpu.make_async_copy(source, target, load_sem.at[i])
        for i, (source, target) in enumerate(
            (
                (qkv_hbm.at[1], kv.at[0]),
                (qkv_hbm.at[2], kv.at[1]),
                (merge_weight_hbm, merge_w.at[0:width]),
                (residual_hbm, res),
                (groups_hbm, groups_line_ref),
                (qkv_hbm.at[0], q_ref),
                (gain_hbm, gain_ref),
                (dest_hbm, dest_ref),
                (out_weight_hbm, weight),
            )
        )
    ]
    for load in loads:
        load.start()
    for load in loads[:4]:
        load.wait()
    pl.semaphore_wait(barrier, rows + cols - 2)

    after_row, before_row = (row + 1) % rows, (row + rows - 1) % rows
    mine = pl.ds(pl.multiple_of(me * chunk, chunk), chunk)
    my_rows = pl.ds(pl.multiple_of(me * width, 16), width)
    halo = []
    for side, (other, target, at) in enumerate(
        ((after_row, left, tokens - reach), (before_row, right, 0))
    ):
        for i in range(2):
            halo.append(
                pltpu.make_async_remote_copy(
                    src_ref=kv.at[i, :, at : at + reach],
                    dst_ref=target.at[i],
                    send_sem=halo_send.at[2 * side + i],
                    recv_sem=halo_recv.at[2 * side + i],
                    device_id={"row": other},
                    device_id_type=MESH,
                )
            )
    cut = width // 32 * 16 + 16
    spans = ((0, cut, x_at), (cut, width, z_at))
    shift, gather = [], []
    for s, (top, end, at) in enumerate(spans):
        across = pl.ds(pl.multiple_of(at * full, 128), full)
        place = merge_w.at[width + top : width + end, across]
        shift.append(
            pltpu.make_async_remote_copy(
                src_ref=merge_w.at[top:end, across],
                dst_ref=place,
                send_sem=shift_send.at[s],
                recv_sem=shift_recv.at[s],
                device_id={"col": (me + cols // 2) % cols},
                device_id_type=MESH,
            )
        )
        for k in range(1, 4):
            other = x_at * line_up + (z_at + k) % line_up if s else (row + k * line_up) % rows
            gather.append(
                pltpu.make_async_remote_copy(
                    src_ref=place,
                    dst_ref=place,
                    send_sem=gather_send.at[s, k],
                    recv_sem=gather_recv.at[s, k],
                    device_id={"row": other},
                    device_id_type=MESH,
                )
            )
    resident = []
    for k in range(1, cols):
        to = (me + k) % cols
        resident.append(
            pltpu.make_async_remote_copy(
                src_ref=res.at[:, pl.ds(pl.multiple_of(to * chunk, chunk), chunk)],
                dst_ref=residual.at[my_rows],
                send_sem=res_send.at[k],
                recv_sem=res_recv.at[k],
                device_id={"col": to},
                device_id_type=MESH,
            )
        )
    for copy in halo + shift:
        copy.start()
    residual[my_rows, :] = res[:, mine]
    for load in loads[4:]:
        load.wait()

    images = groups_line_ref.shape[1]
    first = lax.broadcasted_iota(jnp.int32, (images, images), 0)
    second = lax.broadcasted_iota(jnp.int32, (images, images), 1)
    sizes = groups_line_ref[...]
    size = jnp.sum(jnp.where(second == first, sizes, 0), axis=1, keepdims=True) * 4
    begin = (
        jnp.sum(jnp.where(second < first, sizes, 0), axis=1, keepdims=True) * 4 - row * tokens
    )

    def prepare(b, carry):
        at = pl.multiple_of(b * QB, QB)
        token = lax.broadcasted_iota(jnp.int32, (images, QB), 1) + at
        inside = (token >= begin) & (token < begin + size)
        bound_ref[0:1, pl.ds(at, QB)] = jnp.sum(jnp.where(inside, begin, 0), axis=0, keepdims=True)
        bound_ref[1:2, pl.ds(at, QB)] = jnp.sum(jnp.where(inside, size, 0), axis=0, keepdims=True)
        kt[pl.ds(at, QB), :] = jnp.transpose(kv[0, :, pl.ds(at, QB)])
        v0, v1 = split_heads(kv[1, :, pl.ds(at, QB)])
        vt[0, :, pl.ds(at, QB)] = v0
        vt[1, :, pl.ds(at, QB)] = v1
        return carry

    lax.fori_loop(0, blocks, prepare, 0)

    def local_block(b, carry):
        at = pl.multiple_of(b * QB, QB)
        qcat = query_pair(q_ref[:, pl.ds(at, QB)])
        start = bound_ref[0:1, pl.ds(at, QB)]
        length = bound_ref[1:2, pl.ds(at, QB)]
        spot = lax.broadcasted_iota(jnp.int32, (KB, QB), 0) - start
        tops = [jnp.full((1, QB), NEG, jnp.float32) for _ in range(2)]
        for t in range(blocks):
            key = t * KB
            scores = jnp.dot(kt[key : key + KB, :], qcat, preferred_element_type=jnp.float32)
            ok = (spot >= -key) & (spot < length - key)
            for head in range(2):
                masked = jnp.where(ok, scores[:, head * QB : (head + 1) * QB], NEG)
                held_scores[head, t] = masked
                tops[head] = jnp.maximum(tops[head], jnp.max(masked, axis=0, keepdims=True))
        for head in range(2):
            peak = tops[head] * coef
            total = jnp.zeros((1, QB), jnp.float32)
            sums = jnp.zeros((HEAD_DIM, QB), jnp.float32)
            for t in range(blocks):
                expo = jnp.exp2(held_scores[head, t] * coef - peak)
                total = total + jnp.sum(expo, axis=0, keepdims=True)
                sums = sums + jnp.dot(
                    vt[head, :, t * KB : (t + 1) * KB],
                    expo.astype(jnp.bfloat16),
                    preferred_element_type=jnp.float32,
                )
            m_ref[b * 2 + head] = tops[head]
            l_ref[b * 2 + head] = total
            acc_ref[b * 2 + head] = sums
        return carry

    lax.fori_loop(0, blocks // 2, local_block, 0)
    for copy in resident:
        copy.start()
    lax.fori_loop(blocks // 2, blocks, local_block, 0)

    def turn(i, carry):
        at = pl.multiple_of(i * 128, 128)
        weight_t[pl.ds(at, 128), :] = jnp.transpose(weight[:, pl.ds(at, 128)])
        return carry

    lax.fori_loop(0, full // 128, turn, 0)
    for i in range(full // 128):
        gain_column[i * 128 : (i + 1) * 128, :] = jnp.transpose(
            jnp.broadcast_to(gain_ref[i : i + 1, :], (8, 128))
        )

    before, after, across_chip = (chip + 3) % chips, (chip + 1) % chips, (chip + 2) % chips
    of = [dest_ref[pl.ds(c, 1), :] for c in (chip, before, across_chip, after)]
    span = chunk // 4
    line = jnp.concatenate(
        [
            of[c][:, k * span + p * part : k * span + (p + 1) * part]
            for order in (((0, 0), (0, 1), (1, 0), (3, 1)), ((2, 0), (2, 1), (3, 0), (1, 1)))
            for p in range(PIECES)
            for c, k in order
        ],
        axis=1,
    )
    owner_line = line // groups
    owner_column = jnp.transpose(
        jnp.broadcast_to(owner_line.astype(jnp.float32), (8, groups))
    )[:, 0:1].astype(jnp.int32)
    down = lax.broadcasted_iota(jnp.int32, (groups, groups), 0)
    across = lax.broadcasted_iota(jnp.int32, (groups, groups), 1)
    earlier = (owner_column == owner_line) & (down < across)
    rank = jnp.sum(earlier.astype(jnp.int32), axis=0, keepdims=True)
    pick[...] = jnp.where(down == owner_line * share + rank, 1.0, 0.0).astype(jnp.bfloat16)
    slot = line % groups
    which = lax.broadcasted_iota(jnp.int32, (merged.shape[0] - width, groups), 0)
    digits = jnp.where(which == 0, slot // 16, jnp.where(which == 1, slot % 16, 0))
    merged[width:, :] = digits.astype(jnp.float32).astype(jnp.bfloat16)

    for copy in shift:
        copy.wait_recv()
    for copy in gather:
        copy.start()
    for copy in halo:
        copy.wait_recv()

    def prepare_halo(i, carry):
        at = pl.multiple_of(i * QB, QB)
        for source, base in ((left, 0), (right, reach)):
            to = pl.ds(pl.multiple_of(base + at, QB), QB)
            halo_kt[to, :] = jnp.transpose(source[0, :, pl.ds(at, QB)])
            v0, v1 = split_heads(source[1, :, pl.ds(at, QB)])
            halo_vt[0, :, to] = v0
            halo_vt[1, :, to] = v1
        return carry

    lax.fori_loop(0, reach // QB, prepare_halo, 0)

    def spread_copy(k):
        to = (me + k) % cols
        return pltpu.make_async_remote_copy(
            src_ref=attended.at[to],
            dst_ref=att.at[my_rows],
            send_sem=spread_send.at[k],
            recv_sem=spread_recv.at[k],
            device_id={"col": to},
            device_id_type=MESH,
        )

    def halo_block(b):
        at = pl.multiple_of(b * QB, QB)
        qcat = query_pair(q_ref[:, pl.ds(at, QB)])
        start = bound_ref[0:1, pl.ds(at, QB)]
        length = bound_ref[1:2, pl.ds(at, QB)]
        high = b // (blocks // 2)
        tiles = high * (b - blocks // 2 + 1) + (1 - high) * (blocks // 2 - b)

        def pair(t, inner):
            slot = high * (reach + t * HB) + (1 - high) * (reach - (t + 1) * HB)
            slot = pl.multiple_of(slot, HB)
            key = slot - reach + high * tokens
            spot = lax.broadcasted_iota(jnp.int32, (HB, QB), 0) + (key - start)
            ok = (spot >= 0) & (spot < length)
            halo_step(
                halo_kt[pl.ds(slot, HB), :],
                [halo_vt[head, :, pl.ds(slot, HB)] for head in range(2)],
                qcat,
                ok,
                coef,
                m_ref.at[pl.ds(b * 2, 2)],
                l_ref.at[pl.ds(b * 2, 2)],
                acc_ref.at[pl.ds(b * 2, 2)],
            )
            return inner

        lax.fori_loop(0, (tiles * KB + HB - 1) // HB, pair, 0)
        both = [acc_ref[b * 2 + head] * (1.0 / l_ref[b * 2 + head]) for head in range(2)]
        attended[b] = jnp.concatenate(both, axis=0).astype(jnp.bfloat16)

    def block_of(i, carry):
        halo_block((me + 1 + i) % cols)
        spread_copy(1 + i).start()
        return carry

    lax.fori_loop(0, cols - 1, block_of, 0)
    halo_block(me)
    att[my_rows, :] = attended[me]
    for copy in resident:
        copy.wait()
    for k in range(1, cols):
        spread_copy(k).wait_recv()

    def lanes(owner, p):
        return pl.ds(pl.multiple_of(owner * chunk + p * piece, 128), piece)

    here = lax.broadcasted_iota(jnp.int32, (piece, piece), 0)
    there = lax.broadcasted_iota(jnp.int32, (piece, piece), 1)
    order = jnp.where((here % 4) * part + here // 4 == there, 1.0, 0.0).astype(jnp.bfloat16)
    goal = (chip + 1 + 2 * core) % chips
    near, own, back = [], [], []
    for p in range(PIECES):
        at = slice(p * piece, (p + 1) * piece)
        projected = jnp.dot(weight_t[...], att[:, at], preferred_element_type=jnp.float32)
        rounded = (residual[:, at].astype(jnp.float32) + projected).astype(jnp.bfloat16)
        layer_rows[p] = rounded
        values32 = rounded.astype(jnp.float32)
        centre = jnp.sum(values32, axis=0, keepdims=True) * (1.0 / full)
        spread_of = jnp.sum(jnp.square(values32 - centre), axis=0, keepdims=True) * (1.0 / full)
        scale = lax.rsqrt(spread_of + 1e-06)
        normed = ((values32 - centre) * scale * gain_column[:, 0:1]).astype(jnp.bfloat16)
        held[p, core] = jnp.dot(normed, order, preferred_element_type=jnp.float32).astype(
            jnp.bfloat16
        )
        for h in range(2):
            rows_of = pl.ds(h * half, half)
            copy = pltpu.make_async_remote_copy(
                src_ref=held.at[p, core, rows_of],
                dst_ref=held.at[p, 2 + core, rows_of],
                send_sem=near_send.at[p, h],
                recv_sem=near_recv.at[p, core],
                device_id={"col": goal * 2 + h},
                device_id_type=MESH,
            )
            copy.start()
            near.append(copy)
        copy = pltpu.make_async_remote_copy(
            src_ref=held.at[p, core],
            dst_ref=held.at[p, core],
            send_sem=own_send.at[p],
            recv_sem=own_recv.at[p],
            device_id={"col": sibling},
            device_id_type=MESH,
        )
        copy.start()
        own.append(copy)
        layer_ref[:, lanes(me, p)] = layer_rows[p, my_rows, :]

    for k in range(1, cols):
        spread_copy(k).wait_send()
    passed = []
    my_half = pl.ds(pl.multiple_of(core * half, 16), half)
    for p in range(PIECES):
        for s in range(2):
            arrive = pltpu.make_async_remote_copy(
                src_ref=held.at[p, core, my_half],
                dst_ref=held.at[p, 2 + s, my_half],
                send_sem=near_send.at[p, s],
                recv_sem=near_recv.at[p, s],
                device_id={"col": sibling},
                device_id_type=MESH,
            )
            arrive.wait_recv()
            copy = pltpu.make_async_remote_copy(
                src_ref=held.at[p, 2 + s, my_half],
                dst_ref=held.at[p, 2 + s, my_half],
                send_sem=pass_send.at[p, s],
                recv_sem=pass_recv.at[p, s],
                device_id={"col": sibling},
                device_id_type=MESH,
            )
            copy.start()
            passed.append(copy)
    for copy in near:
        copy.wait_send()

    def send_back(p):
        for k in range(1, cols):
            to = (me + k) % cols
            copy = pltpu.make_async_remote_copy(
                src_ref=layer_rows.at[p, pl.ds(pl.multiple_of(to * width, 16), width)],
                dst_ref=layer_ref.at[:, lanes(me, p)],
                send_sem=back_send.at[p, k],
                recv_sem=back_recv.at[p, k],
                device_id={"col": to},
                device_id_type=MESH,
            )
            copy.start()
            back.append(copy)

    for p in range(PIECES - 1):
        send_back(p)
    for copy in gather:
        copy.wait()
    for copy in own + passed:
        copy.wait()

    total = None
    for j in range(4):
        side = jnp.concatenate(
            [
                held[p, s, :, j * part : (j + 1) * part]
                for p in range(PIECES)
                for s in range(4)
            ],
            axis=1,
        )
        term = jnp.dot(
            merge_w[:, j * full : (j + 1) * full], side, preferred_element_type=jnp.float32
        )
        total = term if total is None else total + term
    far_rows[...] = total[width:].astype(jnp.bfloat16)
    across_y = pltpu.make_async_remote_copy(
        src_ref=far_rows,
        dst_ref=merged.at[0:width, chunk : 2 * chunk],
        send_sem=far_send,
        recv_sem=far_recv,
        device_id={"col": (me + cols // 2) % cols},
        device_id_type=MESH,
    )
    across_y.start()
    merged[0:width, 0:chunk] = total[:width].astype(jnp.bfloat16)
    across_y.wait()
    send_back(PIECES - 1)

    sorted_rows[...] = lax.dot_general(
        pick[...], merged[...], (((1,), (1,)), ((), ())), preferred_element_type=jnp.float32
    ).astype(jnp.bfloat16)
    moves = []
    for k in range(1, rows):
        to = (row + k) % rows
        copy = pltpu.make_async_remote_copy(
            src_ref=sorted_rows.at[pl.ds(pl.multiple_of(to * share, share), share)],
            dst_ref=got_rows.at[pl.ds(pl.multiple_of(row * share, share), share)],
            send_sem=row_send.at[k],
            recv_sem=row_recv.at[k],
            device_id={"row": to},
            device_id_type=MESH,
        )
        copy.start()
        moves.append(copy)
    keep = pl.ds(pl.multiple_of(row * share, share), share)
    got_rows[keep, :] = sorted_rows[keep, :]
    for copy in moves + back:
        copy.wait()
    for copy in halo + shift:
        copy.wait_send()


def place_kernel(layer_hbm, got_hbm, layer_out, image_ref, layer, got_ref, sem):
    load = pltpu.make_async_copy(got_hbm, got_ref, sem.at[0])
    copies = [
        pltpu.make_async_copy(layer_hbm, layer, sem.at[1]),
        pltpu.make_async_copy(layer, layer_out, sem.at[2]),
    ]
    load.start()
    copies[0].start()
    load.wait()
    width, groups = image_ref.shape
    got = got_ref[...]
    target = got[:, width : width + 1].astype(jnp.float32) * 16.0 + got[
        :, width + 1 : width + 2
    ].astype(jnp.float32)
    slot = lax.broadcasted_iota(jnp.int32, (groups, groups), 1).astype(jnp.float32)
    put = jnp.where(target == slot, 1.0, 0.0).astype(jnp.bfloat16)
    copies[0].wait()
    copies[1].start()
    image_ref[...] = lax.dot_general(
        got, put, (((0,), (0,)), ((), ())), preferred_element_type=jnp.float32
    )[:width].astype(jnp.bfloat16)
    copies[1].wait()


def body(qkv, residual_in, out_weight, merge_weight, merge_gain, image_groups, dest_row):
    rows = lax.axis_size("row")
    cols = lax.axis_size("col")
    _, width, tokens = qkv.shape
    full = out_weight.shape[0]
    reach = tokens // 2
    blocks = tokens // QB
    chunk = tokens // cols
    piece = chunk // PIECES
    groups = tokens // 4
    bf16, f32, i32 = jnp.bfloat16, jnp.float32, jnp.int32
    coef = math.log2(math.e) / math.sqrt(HEAD_DIM)
    vmem = pl.BlockSpec(memory_space=pltpu.VMEM)
    hbm = pl.BlockSpec(memory_space=pl.ANY)
    dma = pltpu.SemaphoreType.DMA
    gain = merge_gain.reshape(-1, 128)
    dest = dest_row.reshape(cols // 2, -1)
    sizes = image_groups[None, :]
    layer, got = pl.pallas_call(
        functools.partial(layer_kernel, rows, cols, coef),
        out_shape=(
            jax.ShapeDtypeStruct((width, tokens), bf16),
            jax.ShapeDtypeStruct((groups, width + 16), bf16),
        ),
        in_specs=[hbm] * 7,
        out_specs=(vmem, vmem),
        scratch_shapes=[
            pltpu.VMEM((width, tokens), bf16),
            pltpu.VMEM((2, width, tokens), bf16),
            pltpu.VMEM((tokens, width), bf16),
            pltpu.VMEM((2, HEAD_DIM, tokens), bf16),
            pltpu.VMEM((2, width, reach), bf16),
            pltpu.VMEM((2, width, reach), bf16),
            pltpu.VMEM((2 * reach, width), bf16),
            pltpu.VMEM((2, HEAD_DIM, 2 * reach), bf16),
            pltpu.VMEM((8, tokens), i32),
            pltpu.VMEM((2, blocks, KB, QB), f32),
            pltpu.VMEM((2 * blocks, 1, QB), f32),
            pltpu.VMEM((2 * blocks, 1, QB), f32),
            pltpu.VMEM((2 * blocks, HEAD_DIM, QB), f32),
            pltpu.VMEM((blocks, width, QB), bf16),
            pltpu.VMEM((width, tokens), bf16),
            pltpu.VMEM((full, chunk), bf16),
            pltpu.VMEM((full, chunk), bf16),
            pltpu.VMEM((full, full), bf16),
            pltpu.VMEM((full, full), bf16),
            pltpu.VMEM((2 * width, merge_weight.shape[1]), bf16),
            pltpu.VMEM((PIECES, full, piece), bf16),
            pltpu.VMEM((PIECES, 4, full, piece), bf16),
            pltpu.VMEM((width, chunk), bf16),
            pltpu.VMEM((width + 16, groups), bf16),
            pltpu.VMEM((groups, groups), bf16),
            pltpu.VMEM((groups, width + 16), bf16),
            pltpu.VMEM((full, 8), f32),
            pltpu.VMEM(gain.shape, f32),
            pltpu.VMEM(sizes.shape, i32),
            pltpu.VMEM(dest.shape, i32),
            dma((9,)),
            dma((4,)),
            dma((4,)),
            dma((cols,)),
            dma((cols,)),
            dma((2,)),
            dma((2,)),
            dma((2, 4)),
            dma((2, 4)),
            dma((cols,)),
            dma((cols,)),
            dma((PIECES, cols)),
            dma((PIECES, cols)),
            dma((PIECES, 2)),
            dma((PIECES, 2)),
            dma((PIECES,)),
            dma((PIECES,)),
            dma((PIECES, 2)),
            dma((PIECES, 2)),
            dma,
            dma,
            dma((rows,)),
            dma((rows,)),
        ],
        compiler_params=pltpu.CompilerParams(
            collective_id=0, has_side_effects=True, vmem_limit_bytes=int(60 * 2**20)
        ),
    )(qkv, residual_in, out_weight, merge_weight, gain, sizes, dest)
    return pl.pallas_call(
        place_kernel,
        out_shape=(
            jax.ShapeDtypeStruct((width, tokens), bf16),
            jax.ShapeDtypeStruct((width, groups), bf16),
        ),
        in_specs=[hbm, hbm],
        out_specs=(hbm, vmem),
        scratch_shapes=[
            pltpu.VMEM((width, tokens), bf16),
            pltpu.VMEM((groups, width + 16), bf16),
            dma((3,)),
        ],
        compiler_params=pltpu.CompilerParams(vmem_limit_bytes=60 << 20),
    )(layer, got)


def solution(mesh):
    return jax.shard_map(
        body,
        mesh=mesh,
        in_specs=(P(None, "col", "row"), P("col", "row"), P(), P("col", None), P(), P(), P("row")),
        out_specs=(P("col", "row"), P("col", "row")),
        check_vma=False,
    )
```

```python
import functools
import math

import jax
import jax.numpy as jnp
from jax import lax
from jax.experimental import pallas as pl
from jax.experimental.pallas import tpu as pltpu
from jax.sharding import PartitionSpec as P

HEAD_DIM = 88
QB = 256
KB = 256
HB = 512
PIECES = 2
NEG = -1e30
MESH = pl.DeviceIdType.MESH


def halo_step(keys, values, qcat, ok, coef, m_ref, l_ref, acc_ref):
    width = qcat.shape[1] // 2
    scores = jnp.dot(keys, qcat, preferred_element_type=jnp.float32)
    for head in range(2):
        part = jnp.where(ok, scores[:, head * width : (head + 1) * width], NEG)
        old = m_ref[head]
        new = jnp.maximum(old, jnp.max(part, axis=0, keepdims=True))
        fade = jnp.exp2((old - new) * coef)
        expo = jnp.exp2(part * coef - new * coef)
        l_ref[head] = l_ref[head] * fade + jnp.sum(expo, axis=0, keepdims=True)
        m_ref[head] = new
        acc_ref[head] = acc_ref[head] * fade + jnp.dot(
            values[head], expo.astype(jnp.bfloat16), preferred_element_type=jnp.float32
        )


def split_heads(values):
    wide = values.astype(jnp.float32)
    return wide[:HEAD_DIM].astype(jnp.bfloat16), wide[HEAD_DIM:].astype(jnp.bfloat16)


def query_pair(block):
    feature = lax.broadcasted_iota(jnp.int32, block.shape, 0)
    zero = jnp.zeros_like(block)
    return jnp.concatenate(
        [jnp.where(feature < HEAD_DIM, block, zero), jnp.where(feature < HEAD_DIM, zero, block)],
        axis=1,
    )


def layer_kernel(
    rows,
    cols,
    coef,
    qkv_hbm,
    residual_hbm,
    out_weight_hbm,
    merge_weight_hbm,
    gain_hbm,
    groups_hbm,
    dest_hbm,
    layer_ref,
    got_rows,
    q_ref,
    kv,
    kt,
    vt,
    left,
    right,
    halo_kt,
    halo_vt,
    bound_ref,
    held_scores,
    m_ref,
    l_ref,
    acc_ref,
    attended,
    res,
    residual,
    att,
    weight,
    weight_t,
    merge_w,
    layer_rows,
    held,
    far_rows,
    merged,
    pick,
    sorted_rows,
    gain_column,
    gain_ref,
    groups_line_ref,
    dest_ref,
    load_sem,
    halo_send,
    halo_recv,
    res_send,
    res_recv,
    shift_send,
    shift_recv,
    gather_send,
    gather_recv,
    spread_send,
    spread_recv,
    back_send,
    back_recv,
    near_send,
    near_recv,
    own_send,
    own_recv,
    pass_send,
    pass_recv,
    far_send,
    far_recv,
    row_send,
    row_recv,
):
    row = lax.axis_index("row")
    me = lax.axis_index("col")
    width, tokens = q_ref.shape
    full = weight.shape[0]
    reach = left.shape[2]
    blocks = tokens // QB
    chunk = tokens // cols
    piece = chunk // PIECES
    part = piece // 4
    groups = tokens // 4
    share = groups // rows
    chips = cols // 2
    core = me % 2
    chip = me // 2
    sibling = me + 1 - 2 * core
    half = full // 2
    line_up = rows // 4
    x_at, z_at = row // line_up, row % line_up

    barrier = pltpu.get_barrier_semaphore()
    for k in range(1, cols):
        pl.semaphore_signal(
            barrier, inc=1, device_id={"col": (me + k) % cols}, device_id_type=MESH
        )
    for k in range(1, rows):
        pl.semaphore_signal(
            barrier, inc=1, device_id={"row": (row + k) % rows}, device_id_type=MESH
        )
    loads = [
        pltpu.make_async_copy(source, target, load_sem.at[i])
        for i, (source, target) in enumerate(
            (
                (qkv_hbm.at[1], kv.at[0]),
                (qkv_hbm.at[2], kv.at[1]),
                (merge_weight_hbm, merge_w.at[0:width]),
                (residual_hbm, res),
                (groups_hbm, groups_line_ref),
                (qkv_hbm.at[0], q_ref),
                (gain_hbm, gain_ref),
                (dest_hbm, dest_ref),
                (out_weight_hbm, weight),
            )
        )
    ]
    for load in loads:
        load.start()
    for load in loads[:4]:
        load.wait()
    pl.semaphore_wait(barrier, rows + cols - 2)

    after_row, before_row = (row + 1) % rows, (row + rows - 1) % rows
    mine = pl.ds(pl.multiple_of(me * chunk, chunk), chunk)
    my_rows = pl.ds(pl.multiple_of(me * width, 16), width)
    near_halo, far_halo = [], []
    for side, (other, target, at) in enumerate(
        ((after_row, left, tokens - reach), (before_row, right, 0))
    ):
        for i in range(2):
            for h in range(2):
                to = (h if side else 1 - h) * HB
                copy = pltpu.make_async_remote_copy(
                    src_ref=kv.at[i, :, at + to : at + to + HB],
                    dst_ref=target.at[i, :, to : to + HB],
                    send_sem=halo_send.at[side, i, h],
                    recv_sem=halo_recv.at[side, i, h],
                    device_id={"row": other},
                    device_id_type=MESH,
                )
                (far_halo if h else near_halo).append(copy)
    strip = width // 64 * 16
    top = 4 * strip
    x_lanes = pl.ds(pl.multiple_of(x_at * full, 128), full)
    z_lanes = pl.ds(pl.multiple_of(z_at * full, 128), full)
    my_strip = pl.ds(pl.multiple_of(x_at * strip, 16), strip)
    far_strip = pl.ds(pl.multiple_of(width + x_at * strip, 16), strip)
    strip_place = merge_w.at[far_strip, z_lanes]
    top_place = merge_w.at[width : width + top, z_lanes]
    low_place = merge_w.at[width + top : 2 * width, x_lanes]
    shift = [
        pltpu.make_async_remote_copy(
            src_ref=source,
            dst_ref=place,
            send_sem=shift_send.at[s],
            recv_sem=shift_recv.at[s],
            device_id={"col": (me + cols // 2) % cols},
            device_id_type=MESH,
        )
        for s, (source, place) in enumerate(
            ((merge_w.at[my_strip, z_lanes], strip_place), (merge_w.at[top:width, x_lanes], low_place))
        )
    ]
    by_x, by_z = [], []
    for k in range(1, 4):
        for s, (place, other, group) in enumerate(
            (
                (strip_place, (row + k * line_up) % rows, by_x),
                (low_place, (row + k * line_up) % rows, by_x),
                (top_place, x_at * line_up + (z_at + k) % line_up, by_z),
            )
        ):
            group.append(
                pltpu.make_async_remote_copy(
                    src_ref=place,
                    dst_ref=place,
                    send_sem=gather_send.at[s, k],
                    recv_sem=gather_recv.at[s, k],
                    device_id={"row": other},
                    device_id_type=MESH,
                )
            )
    resident = []
    for k in range(1, cols):
        to = (me + k) % cols
        resident.append(
            pltpu.make_async_remote_copy(
                src_ref=res.at[:, pl.ds(pl.multiple_of(to * chunk, chunk), chunk)],
                dst_ref=residual.at[my_rows],
                send_sem=res_send.at[k],
                recv_sem=res_recv.at[k],
                device_id={"col": to},
                device_id_type=MESH,
            )
        )
    for copy in near_halo + shift:
        copy.start()
    residual[my_rows, :] = res[:, mine]
    for load in loads[4:]:
        load.wait()

    images = groups_line_ref.shape[1]
    first = lax.broadcasted_iota(jnp.int32, (images, images), 0)
    second = lax.broadcasted_iota(jnp.int32, (images, images), 1)
    sizes = groups_line_ref[...]
    size = jnp.sum(jnp.where(second == first, sizes, 0), axis=1, keepdims=True) * 4
    begin = (
        jnp.sum(jnp.where(second < first, sizes, 0), axis=1, keepdims=True) * 4 - row * tokens
    )

    def prepare(b, carry):
        at = pl.multiple_of(b * QB, QB)
        token = lax.broadcasted_iota(jnp.int32, (images, QB), 1) + at
        inside = (token >= begin) & (token < begin + size)
        bound_ref[0:1, pl.ds(at, QB)] = jnp.sum(jnp.where(inside, begin, 0), axis=0, keepdims=True)
        bound_ref[1:2, pl.ds(at, QB)] = jnp.sum(jnp.where(inside, size, 0), axis=0, keepdims=True)
        kt[pl.ds(at, QB), :] = jnp.transpose(kv[0, :, pl.ds(at, QB)])
        v0, v1 = split_heads(kv[1, :, pl.ds(at, QB)])
        vt[0, :, pl.ds(at, QB)] = v0
        vt[1, :, pl.ds(at, QB)] = v1
        return carry

    lax.fori_loop(0, blocks, prepare, 0)

    def local_block(b, carry):
        at = pl.multiple_of(b * QB, QB)
        qcat = query_pair(q_ref[:, pl.ds(at, QB)])
        start = bound_ref[0:1, pl.ds(at, QB)]
        length = bound_ref[1:2, pl.ds(at, QB)]
        spot = lax.broadcasted_iota(jnp.int32, (KB, QB), 0) - start
        tops = [jnp.full((1, QB), NEG, jnp.float32) for _ in range(2)]
        for t in range(blocks):
            key = t * KB
            scores = jnp.dot(kt[key : key + KB, :], qcat, preferred_element_type=jnp.float32)
            ok = (spot >= -key) & (spot < length - key)
            for head in range(2):
                masked = jnp.where(ok, scores[:, head * QB : (head + 1) * QB], NEG)
                held_scores[head, t] = masked
                tops[head] = jnp.maximum(tops[head], jnp.max(masked, axis=0, keepdims=True))
        for head in range(2):
            peak = tops[head] * coef
            total = jnp.zeros((1, QB), jnp.float32)
            sums = jnp.zeros((HEAD_DIM, QB), jnp.float32)
            for t in range(blocks):
                expo = jnp.exp2(held_scores[head, t] * coef - peak)
                total = total + jnp.sum(expo, axis=0, keepdims=True)
                sums = sums + jnp.dot(
                    vt[head, :, t * KB : (t + 1) * KB],
                    expo.astype(jnp.bfloat16),
                    preferred_element_type=jnp.float32,
                )
            m_ref[b * 2 + head] = tops[head]
            l_ref[b * 2 + head] = total
            acc_ref[b * 2 + head] = sums
        return carry

    lax.fori_loop(0, 2, local_block, 0)
    for copy in shift:
        copy.wait_recv()
    for copy in by_x + resident:
        copy.start()
    lax.fori_loop(2, 4, local_block, 0)
    for copy in near_halo:
        copy.wait_send()
    for copy in far_halo:
        copy.start()
    lax.fori_loop(4, blocks, local_block, 0)

    def turn(i, carry):
        at = pl.multiple_of(i * 128, 128)
        weight_t[pl.ds(at, 128), :] = jnp.transpose(weight[:, pl.ds(at, 128)])
        return carry

    lax.fori_loop(0, full // 128, turn, 0)
    for i in range(full // 128):
        gain_column[i * 128 : (i + 1) * 128, :] = jnp.transpose(
            jnp.broadcast_to(gain_ref[i : i + 1, :], (8, 128))
        )

    before, after, across_chip = (chip + 3) % chips, (chip + 1) % chips, (chip + 2) % chips
    of = [dest_ref[pl.ds(c, 1), :] for c in (chip, before, across_chip, after)]
    span = chunk // 4
    line = jnp.concatenate(
        [
            of[c][:, k * span + p * part : k * span + (p + 1) * part]
            for order in (((0, 0), (0, 1), (1, 0), (3, 1)), ((2, 0), (2, 1), (3, 0), (1, 1)))
            for p in range(PIECES)
            for c, k in order
        ],
        axis=1,
    )
    owner_line = line // groups
    owner_column = jnp.transpose(
        jnp.broadcast_to(owner_line.astype(jnp.float32), (8, groups))
    )[:, 0:1].astype(jnp.int32)
    down = lax.broadcasted_iota(jnp.int32, (groups, groups), 0)
    across = lax.broadcasted_iota(jnp.int32, (groups, groups), 1)
    earlier = (owner_column == owner_line) & (down < across)
    rank = jnp.sum(earlier.astype(jnp.int32), axis=0, keepdims=True)
    pick[...] = jnp.where(down == owner_line * share + rank, 1.0, 0.0).astype(jnp.bfloat16)
    slot = line % groups
    which = lax.broadcasted_iota(jnp.int32, (merged.shape[0] - width, groups), 0)
    digits = jnp.where(which == 0, slot // 16, jnp.where(which == 1, slot % 16, 0))
    merged[width:, :] = digits.astype(jnp.float32).astype(jnp.bfloat16)

    def prepare_halo(at, to):
        for source, base in ((left, 0), (right, reach)):
            here = (reach - HB - at if base == 0 else at) + to
            span = slice(here, here + QB)
            slot = slice(base + here, base + here + QB)
            halo_kt[slot, :] = jnp.transpose(source[0, :, span])
            v0, v1 = split_heads(source[1, :, span])
            halo_vt[0, :, slot] = v0
            halo_vt[1, :, slot] = v1

    def spread_copy(k):
        to = (me + k) % cols
        return pltpu.make_async_remote_copy(
            src_ref=attended.at[to],
            dst_ref=att.at[my_rows],
            send_sem=spread_send.at[k],
            recv_sem=spread_recv.at[k],
            device_id={"col": to},
            device_id_type=MESH,
        )

    def halo_block(b, t):
        at = pl.multiple_of(b * QB, QB)
        qcat = query_pair(q_ref[:, pl.ds(at, QB)])
        start = bound_ref[0:1, pl.ds(at, QB)]
        length = bound_ref[1:2, pl.ds(at, QB)]
        high = b // (blocks // 2)
        slot = high * (reach + t * HB) + (1 - high) * (reach - (t + 1) * HB)
        slot = pl.multiple_of(slot, HB)
        key = slot - reach + high * tokens
        spot = lax.broadcasted_iota(jnp.int32, (HB, QB), 0) + (key - start)
        ok = (spot >= 0) & (spot < length)
        halo_step(
            halo_kt[pl.ds(slot, HB), :],
            [halo_vt[head, :, pl.ds(slot, HB)] for head in range(2)],
            qcat,
            ok,
            coef,
            m_ref.at[pl.ds(b * 2, 2)],
            l_ref.at[pl.ds(b * 2, 2)],
            acc_ref.at[pl.ds(b * 2, 2)],
        )

    def finish(b, k):
        both = [acc_ref[b * 2 + head] * (1.0 / l_ref[b * 2 + head]) for head in range(2)]
        attended[b] = jnp.concatenate(both, axis=0).astype(jnp.bfloat16)

        @pl.when(k < cols)
        def _():
            spread_copy(k).start()

    def is_middle(b):
        return (b >= blocks // 4) & (b < blocks - blocks // 4)

    def near_pass(i, carry):
        b = (me + 1 + i) % cols
        halo_block(b, 0)

        @pl.when(is_middle(b))
        def _():
            finish(b, i + 1)

        return carry

    def far_pass(i, carry):
        b = (me + 1 + i) % cols

        @pl.when(jnp.logical_not(is_middle(b)))
        def _():
            halo_block(b, 1)
            finish(b, i + 1)

        return carry

    for copy in near_halo:
        copy.wait_recv()
    for to in range(0, HB, QB):
        prepare_halo(0, to)
    lax.fori_loop(0, cols, near_pass, 0)
    for copy in far_halo:
        copy.wait_recv()
    for copy in by_x:
        copy.wait()
    for copy in by_z:
        copy.start()
    for to in range(0, HB, QB):
        prepare_halo(HB, to)
    lax.fori_loop(0, cols, far_pass, 0)
    att[my_rows, :] = attended[me]
    for copy in resident:
        copy.wait()
    for k in range(1, cols):
        spread_copy(k).wait_recv()

    def lanes(owner, p):
        return pl.ds(pl.multiple_of(owner * chunk + p * piece, 128), piece)

    here = lax.broadcasted_iota(jnp.int32, (piece, piece), 0)
    there = lax.broadcasted_iota(jnp.int32, (piece, piece), 1)
    order = jnp.where((here % 4) * part + here // 4 == there, 1.0, 0.0).astype(jnp.bfloat16)
    goal = (chip + 1 + 2 * core) % chips
    near, own, back = [], [], []
    for p in range(PIECES):
        at = slice(p * piece, (p + 1) * piece)
        projected = jnp.dot(weight_t[...], att[:, at], preferred_element_type=jnp.float32)
        rounded = (residual[:, at].astype(jnp.float32) + projected).astype(jnp.bfloat16)
        layer_rows[p] = rounded
        values32 = rounded.astype(jnp.float32)
        centre = jnp.sum(values32, axis=0, keepdims=True) * (1.0 / full)
        spread_of = jnp.sum(jnp.square(values32 - centre), axis=0, keepdims=True) * (1.0 / full)
        scale = lax.rsqrt(spread_of + 1e-06)
        normed = ((values32 - centre) * scale * gain_column[:, 0:1]).astype(jnp.bfloat16)
        held[p, core] = jnp.dot(normed, order, preferred_element_type=jnp.float32).astype(
            jnp.bfloat16
        )
        for h in range(2):
            rows_of = pl.ds(h * half, half)
            copy = pltpu.make_async_remote_copy(
                src_ref=held.at[p, core, rows_of],
                dst_ref=held.at[p, 2 + core, rows_of],
                send_sem=near_send.at[p, h],
                recv_sem=near_recv.at[p, core],
                device_id={"col": goal * 2 + h},
                device_id_type=MESH,
            )
            copy.start()
            near.append(copy)
        copy = pltpu.make_async_remote_copy(
            src_ref=held.at[p, core],
            dst_ref=held.at[p, core],
            send_sem=own_send.at[p],
            recv_sem=own_recv.at[p],
            device_id={"col": sibling},
            device_id_type=MESH,
        )
        copy.start()
        own.append(copy)
        layer_ref[:, lanes(me, p)] = layer_rows[p, my_rows, :]

    for k in range(1, cols):
        spread_copy(k).wait_send()
    passed = []
    my_half = pl.ds(pl.multiple_of(core * half, 16), half)
    for p in range(PIECES):
        for s in range(2):
            arrive = pltpu.make_async_remote_copy(
                src_ref=held.at[p, core, my_half],
                dst_ref=held.at[p, 2 + s, my_half],
                send_sem=near_send.at[p, s],
                recv_sem=near_recv.at[p, s],
                device_id={"col": sibling},
                device_id_type=MESH,
            )
            arrive.wait_recv()
            copy = pltpu.make_async_remote_copy(
                src_ref=held.at[p, 2 + s, my_half],
                dst_ref=held.at[p, 2 + s, my_half],
                send_sem=pass_send.at[p, s],
                recv_sem=pass_recv.at[p, s],
                device_id={"col": sibling},
                device_id_type=MESH,
            )
            copy.start()
            passed.append(copy)
    for copy in near:
        copy.wait_send()

    def send_back(p):
        for k in range(1, cols):
            to = (me + k) % cols
            copy = pltpu.make_async_remote_copy(
                src_ref=layer_rows.at[p, pl.ds(pl.multiple_of(to * width, 16), width)],
                dst_ref=layer_ref.at[:, lanes(me, p)],
                send_sem=back_send.at[p, k],
                recv_sem=back_recv.at[p, k],
                device_id={"col": to},
                device_id_type=MESH,
            )
            copy.start()
            back.append(copy)

    for p in range(PIECES - 1):
        send_back(p)
    for copy in by_z:
        copy.wait()
    for copy in own + passed:
        copy.wait()

    total = None
    for j in range(4):
        side = jnp.concatenate(
            [
                held[p, s, :, j * part : (j + 1) * part]
                for p in range(PIECES)
                for s in range(4)
            ],
            axis=1,
        )
        term = jnp.dot(
            merge_w[:, j * full : (j + 1) * full], side, preferred_element_type=jnp.float32
        )
        total = term if total is None else total + term
    far_rows[...] = total[width:].astype(jnp.bfloat16)
    across_y = pltpu.make_async_remote_copy(
        src_ref=far_rows,
        dst_ref=merged.at[0:width, chunk : 2 * chunk],
        send_sem=far_send,
        recv_sem=far_recv,
        device_id={"col": (me + cols // 2) % cols},
        device_id_type=MESH,
    )
    across_y.start()
    merged[0:width, 0:chunk] = total[:width].astype(jnp.bfloat16)
    across_y.wait()
    send_back(PIECES - 1)

    sorted_rows[...] = lax.dot_general(
        pick[...], merged[...], (((1,), (1,)), ((), ())), preferred_element_type=jnp.float32
    ).astype(jnp.bfloat16)
    moves = []
    for k in range(1, rows):
        to = (row + k) % rows
        copy = pltpu.make_async_remote_copy(
            src_ref=sorted_rows.at[pl.ds(pl.multiple_of(to * share, share), share)],
            dst_ref=got_rows.at[pl.ds(pl.multiple_of(row * share, share), share)],
            send_sem=row_send.at[k],
            recv_sem=row_recv.at[k],
            device_id={"row": to},
            device_id_type=MESH,
        )
        copy.start()
        moves.append(copy)
    keep = pl.ds(pl.multiple_of(row * share, share), share)
    got_rows[keep, :] = sorted_rows[keep, :]
    for copy in moves + back:
        copy.wait()
    for copy in far_halo + shift:
        copy.wait_send()


def place_kernel(layer_hbm, got_hbm, layer_out, image_ref, layer, got_ref, sem):
    load = pltpu.make_async_copy(got_hbm, got_ref, sem.at[0])
    copies = [
        pltpu.make_async_copy(layer_hbm, layer, sem.at[1]),
        pltpu.make_async_copy(layer, layer_out, sem.at[2]),
    ]
    load.start()
    copies[0].start()
    load.wait()
    width, groups = image_ref.shape
    got = got_ref[...]
    target = got[:, width : width + 1].astype(jnp.float32) * 16.0 + got[
        :, width + 1 : width + 2
    ].astype(jnp.float32)
    slot = lax.broadcasted_iota(jnp.int32, (groups, groups), 1).astype(jnp.float32)
    put = jnp.where(target == slot, 1.0, 0.0).astype(jnp.bfloat16)
    copies[0].wait()
    copies[1].start()
    image_ref[...] = lax.dot_general(
        got, put, (((0,), (0,)), ((), ())), preferred_element_type=jnp.float32
    )[:width].astype(jnp.bfloat16)
    copies[1].wait()


def body(qkv, residual_in, out_weight, merge_weight, merge_gain, image_groups, dest_row):
    rows = lax.axis_size("row")
    cols = lax.axis_size("col")
    _, width, tokens = qkv.shape
    full = out_weight.shape[0]
    reach = tokens // 2
    blocks = tokens // QB
    chunk = tokens // cols
    piece = chunk // PIECES
    groups = tokens // 4
    bf16, f32, i32 = jnp.bfloat16, jnp.float32, jnp.int32
    coef = math.log2(math.e) / math.sqrt(HEAD_DIM)
    vmem = pl.BlockSpec(memory_space=pltpu.VMEM)
    hbm = pl.BlockSpec(memory_space=pl.ANY)
    dma = pltpu.SemaphoreType.DMA
    gain = merge_gain.reshape(-1, 128)
    dest = dest_row.reshape(cols // 2, -1)
    sizes = image_groups[None, :]
    layer, got = pl.pallas_call(
        functools.partial(layer_kernel, rows, cols, coef),
        out_shape=(
            jax.ShapeDtypeStruct((width, tokens), bf16),
            jax.ShapeDtypeStruct((groups, width + 16), bf16),
        ),
        in_specs=[hbm] * 7,
        out_specs=(vmem, vmem),
        scratch_shapes=[
            pltpu.VMEM((width, tokens), bf16),
            pltpu.VMEM((2, width, tokens), bf16),
            pltpu.VMEM((tokens, width), bf16),
            pltpu.VMEM((2, HEAD_DIM, tokens), bf16),
            pltpu.VMEM((2, width, reach), bf16),
            pltpu.VMEM((2, width, reach), bf16),
            pltpu.VMEM((2 * reach, width), bf16),
            pltpu.VMEM((2, HEAD_DIM, 2 * reach), bf16),
            pltpu.VMEM((8, tokens), i32),
            pltpu.VMEM((2, blocks, KB, QB), f32),
            pltpu.VMEM((2 * blocks, 1, QB), f32),
            pltpu.VMEM((2 * blocks, 1, QB), f32),
            pltpu.VMEM((2 * blocks, HEAD_DIM, QB), f32),
            pltpu.VMEM((blocks, width, QB), bf16),
            pltpu.VMEM((width, tokens), bf16),
            pltpu.VMEM((full, chunk), bf16),
            pltpu.VMEM((full, chunk), bf16),
            pltpu.VMEM((full, full), bf16),
            pltpu.VMEM((full, full), bf16),
            pltpu.VMEM((2 * width, merge_weight.shape[1]), bf16),
            pltpu.VMEM((PIECES, full, piece), bf16),
            pltpu.VMEM((PIECES, 4, full, piece), bf16),
            pltpu.VMEM((width, chunk), bf16),
            pltpu.VMEM((width + 16, groups), bf16),
            pltpu.VMEM((groups, groups), bf16),
            pltpu.VMEM((groups, width + 16), bf16),
            pltpu.VMEM((full, 8), f32),
            pltpu.VMEM(gain.shape, f32),
            pltpu.VMEM(sizes.shape, i32),
            pltpu.VMEM(dest.shape, i32),
            dma((9,)),
            dma((2, 2, 2)),
            dma((2, 2, 2)),
            dma((cols,)),
            dma((cols,)),
            dma((2,)),
            dma((2,)),
            dma((3, 4)),
            dma((3, 4)),
            dma((cols,)),
            dma((cols,)),
            dma((PIECES, cols)),
            dma((PIECES, cols)),
            dma((PIECES, 2)),
            dma((PIECES, 2)),
            dma((PIECES,)),
            dma((PIECES,)),
            dma((PIECES, 2)),
            dma((PIECES, 2)),
            dma,
            dma,
            dma((rows,)),
            dma((rows,)),
        ],
        compiler_params=pltpu.CompilerParams(
            collective_id=0, has_side_effects=True, vmem_limit_bytes=int(60 * 2**20)
        ),
    )(qkv, residual_in, out_weight, merge_weight, gain, sizes, dest)
    return pl.pallas_call(
        place_kernel,
        out_shape=(
            jax.ShapeDtypeStruct((width, tokens), bf16),
            jax.ShapeDtypeStruct((width, groups), bf16),
        ),
        in_specs=[hbm, hbm],
        out_specs=(hbm, vmem),
        scratch_shapes=[
            pltpu.VMEM((width, tokens), bf16),
            pltpu.VMEM((groups, width + 16), bf16),
            dma((3,)),
        ],
        compiler_params=pltpu.CompilerParams(vmem_limit_bytes=60 << 20),
    )(layer, got)


def solution(mesh):
    return jax.shard_map(
        body,
        mesh=mesh,
        in_specs=(P(None, "col", "row"), P("col", "row"), P(), P("col", None), P(), P(), P("row")),
        out_specs=(P("col", "row"), P("col", "row")),
        check_vma=False,
    )
```

```python
import functools
import math

import jax
import jax.numpy as jnp
from jax import lax
from jax.experimental import pallas as pl
from jax.experimental.pallas import tpu as pltpu
from jax.sharding import PartitionSpec as P

HEAD_DIM = 88
QB = 256
KB = 256
HB = 512
PIECES = 2
NEG = -1e30
MESH = pl.DeviceIdType.MESH


def halo_step(keys, values, qcat, ok, coef, m_ref, l_ref, acc_ref):
    width = qcat.shape[1] // 2
    scores = jnp.dot(keys, qcat, preferred_element_type=jnp.float32)
    for head in range(2):
        part = jnp.where(ok, scores[:, head * width : (head + 1) * width], NEG)
        old = m_ref[head]
        new = jnp.maximum(old, jnp.max(part, axis=0, keepdims=True))
        fade = jnp.exp2((old - new) * coef)
        expo = jnp.exp2(part * coef - new * coef)
        l_ref[head] = l_ref[head] * fade + jnp.sum(expo, axis=0, keepdims=True)
        m_ref[head] = new
        acc_ref[head] = acc_ref[head] * fade + jnp.dot(
            values[head], expo.astype(jnp.bfloat16), preferred_element_type=jnp.float32
        )


def split_heads(values):
    wide = values.astype(jnp.float32)
    return wide[:HEAD_DIM].astype(jnp.bfloat16), wide[HEAD_DIM:].astype(jnp.bfloat16)


def query_pair(block):
    feature = lax.broadcasted_iota(jnp.int32, block.shape, 0)
    zero = jnp.zeros_like(block)
    return jnp.concatenate(
        [jnp.where(feature < HEAD_DIM, block, zero), jnp.where(feature < HEAD_DIM, zero, block)],
        axis=1,
    )


def layer_kernel(
    rows,
    cols,
    coef,
    qkv_hbm,
    residual_hbm,
    out_weight_hbm,
    merge_weight_hbm,
    gain_hbm,
    groups_hbm,
    dest_hbm,
    layer_ref,
    got_rows,
    q_ref,
    kv,
    kt,
    vt,
    left,
    right,
    halo_kt,
    halo_vt,
    bound_ref,
    held_scores,
    m_ref,
    l_ref,
    acc_ref,
    attended,
    res,
    residual,
    att,
    weight,
    weight_t,
    merge_w,
    layer_rows,
    held,
    far_rows,
    merged,
    pick,
    sorted_rows,
    gain_column,
    gain_ref,
    groups_line_ref,
    dest_ref,
    load_sem,
    halo_send,
    halo_recv,
    res_send,
    res_recv,
    shift_send,
    shift_recv,
    gather_send,
    gather_recv,
    spread_send,
    spread_recv,
    back_send,
    back_recv,
    near_send,
    near_recv,
    own_send,
    own_recv,
    pass_send,
    pass_recv,
    far_send,
    far_recv,
    row_send,
    row_recv,
):
    row = lax.axis_index("row")
    me = lax.axis_index("col")
    width, tokens = q_ref.shape
    full = weight.shape[0]
    reach = left.shape[2]
    blocks = tokens // QB
    chunk = tokens // cols
    piece = chunk // PIECES
    part = piece // 4
    groups = tokens // 4
    share = groups // rows
    chips = cols // 2
    core = me % 2
    chip = me // 2
    sibling = me + 1 - 2 * core
    half = full // 2
    line_up = rows // 4
    x_at, z_at = row // line_up, row % line_up

    barrier = pltpu.get_barrier_semaphore()
    for k in range(1, cols):
        pl.semaphore_signal(
            barrier, inc=1, device_id={"col": (me + k) % cols}, device_id_type=MESH
        )
    for k in range(1, rows):
        pl.semaphore_signal(
            barrier, inc=1, device_id={"row": (row + k) % rows}, device_id_type=MESH
        )
    loads = [
        pltpu.make_async_copy(source, target, load_sem.at[i])
        for i, (source, target) in enumerate(
            (
                (qkv_hbm.at[1], kv.at[0]),
                (qkv_hbm.at[2], kv.at[1]),
                (merge_weight_hbm, merge_w.at[0:width]),
                (residual_hbm, res),
                (groups_hbm, groups_line_ref),
                (qkv_hbm.at[0], q_ref),
                (gain_hbm, gain_ref),
                (dest_hbm, dest_ref),
                (out_weight_hbm, weight),
            )
        )
    ]
    for load in loads:
        load.start()
    for load in loads[:4]:
        load.wait()
    pl.semaphore_wait(barrier, rows + cols - 2)

    after_row, before_row = (row + 1) % rows, (row + rows - 1) % rows
    mine = pl.ds(pl.multiple_of(me * chunk, chunk), chunk)
    my_rows = pl.ds(pl.multiple_of(me * width, 16), width)
    near_halo, far_halo = [], []
    for side, (other, target, at) in enumerate(
        ((after_row, left, tokens - reach), (before_row, right, 0))
    ):
        for i in range(2):
            for h in range(2):
                to = (h if side else 1 - h) * HB
                copy = pltpu.make_async_remote_copy(
                    src_ref=kv.at[i, :, at + to : at + to + HB],
                    dst_ref=target.at[i, :, to : to + HB],
                    send_sem=halo_send.at[side, i, h],
                    recv_sem=halo_recv.at[side, i, h],
                    device_id={"row": other},
                    device_id_type=MESH,
                )
                (far_halo if h else near_halo).append(copy)
    strip = width // 64 * 16
    top = 4 * strip
    x_lanes = pl.ds(pl.multiple_of(x_at * full, 128), full)
    z_lanes = pl.ds(pl.multiple_of(z_at * full, 128), full)
    my_strip = pl.ds(pl.multiple_of(x_at * strip, 16), strip)
    far_strip = pl.ds(pl.multiple_of(width + x_at * strip, 16), strip)
    strip_place = merge_w.at[far_strip, z_lanes]
    top_place = merge_w.at[width : width + top, z_lanes]
    low_place = merge_w.at[width + top : 2 * width, x_lanes]
    shift = [
        pltpu.make_async_remote_copy(
            src_ref=source,
            dst_ref=place,
            send_sem=shift_send.at[s],
            recv_sem=shift_recv.at[s],
            device_id={"col": (me + cols // 2) % cols},
            device_id_type=MESH,
        )
        for s, (source, place) in enumerate(
            ((merge_w.at[my_strip, z_lanes], strip_place), (merge_w.at[top:width, x_lanes], low_place))
        )
    ]
    by_x, by_z = [], []
    for k in range(1, 4):
        for s, (place, other, group) in enumerate(
            (
                (strip_place, (row + k * line_up) % rows, by_x),
                (low_place, (row + k * line_up) % rows, by_x),
                (top_place, x_at * line_up + (z_at + k) % line_up, by_z),
            )
        ):
            group.append(
                pltpu.make_async_remote_copy(
                    src_ref=place,
                    dst_ref=place,
                    send_sem=gather_send.at[s, k],
                    recv_sem=gather_recv.at[s, k],
                    device_id={"row": other},
                    device_id_type=MESH,
                )
            )
    resident = []
    for k in range(1, cols):
        to = (me + k) % cols
        resident.append(
            pltpu.make_async_remote_copy(
                src_ref=res.at[:, pl.ds(pl.multiple_of(to * chunk, chunk), chunk)],
                dst_ref=residual.at[my_rows],
                send_sem=res_send.at[k],
                recv_sem=res_recv.at[k],
                device_id={"col": to},
                device_id_type=MESH,
            )
        )
    for copy in near_halo + shift + far_halo:
        copy.start()
    residual[my_rows, :] = res[:, mine]
    for load in loads[4:]:
        load.wait()

    images = groups_line_ref.shape[1]
    first = lax.broadcasted_iota(jnp.int32, (images, images), 0)
    second = lax.broadcasted_iota(jnp.int32, (images, images), 1)
    sizes = groups_line_ref[...]
    size = jnp.sum(jnp.where(second == first, sizes, 0), axis=1, keepdims=True) * 4
    begin = (
        jnp.sum(jnp.where(second < first, sizes, 0), axis=1, keepdims=True) * 4 - row * tokens
    )

    def prepare(b, carry):
        at = pl.multiple_of(b * QB, QB)
        token = lax.broadcasted_iota(jnp.int32, (images, QB), 1) + at
        inside = (token >= begin) & (token < begin + size)
        bound_ref[0:1, pl.ds(at, QB)] = jnp.sum(jnp.where(inside, begin, 0), axis=0, keepdims=True)
        bound_ref[1:2, pl.ds(at, QB)] = jnp.sum(jnp.where(inside, size, 0), axis=0, keepdims=True)
        kt[pl.ds(at, QB), :] = jnp.transpose(kv[0, :, pl.ds(at, QB)])
        v0, v1 = split_heads(kv[1, :, pl.ds(at, QB)])
        vt[0, :, pl.ds(at, QB)] = v0
        vt[1, :, pl.ds(at, QB)] = v1
        return carry

    lax.fori_loop(0, blocks, prepare, 0)

    def local_block(b, carry):
        at = pl.multiple_of(b * QB, QB)
        qcat = query_pair(q_ref[:, pl.ds(at, QB)])
        start = bound_ref[0:1, pl.ds(at, QB)]
        length = bound_ref[1:2, pl.ds(at, QB)]
        spot = lax.broadcasted_iota(jnp.int32, (KB, QB), 0) - start
        tops = [jnp.full((1, QB), NEG, jnp.float32) for _ in range(2)]
        for t in range(blocks):
            key = t * KB
            scores = jnp.dot(kt[key : key + KB, :], qcat, preferred_element_type=jnp.float32)
            ok = (spot >= -key) & (spot < length - key)
            for head in range(2):
                masked = jnp.where(ok, scores[:, head * QB : (head + 1) * QB], NEG)
                held_scores[head, t] = masked
                tops[head] = jnp.maximum(tops[head], jnp.max(masked, axis=0, keepdims=True))
        for head in range(2):
            peak = tops[head] * coef
            total = jnp.zeros((1, QB), jnp.float32)
            sums = jnp.zeros((HEAD_DIM, QB), jnp.float32)
            for t in range(blocks):
                expo = jnp.exp2(held_scores[head, t] * coef - peak)
                total = total + jnp.sum(expo, axis=0, keepdims=True)
                sums = sums + jnp.dot(
                    vt[head, :, t * KB : (t + 1) * KB],
                    expo.astype(jnp.bfloat16),
                    preferred_element_type=jnp.float32,
                )
            m_ref[b * 2 + head] = tops[head]
            l_ref[b * 2 + head] = total
            acc_ref[b * 2 + head] = sums
        return carry

    lax.fori_loop(0, 2, local_block, 0)
    for copy in shift:
        copy.wait_recv()
    for copy in by_x + resident:
        copy.start()
    lax.fori_loop(2, blocks, local_block, 0)

    def turn(i, carry):
        at = pl.multiple_of(i * 128, 128)
        weight_t[pl.ds(at, 128), :] = jnp.transpose(weight[:, pl.ds(at, 128)])
        return carry

    lax.fori_loop(0, full // 128, turn, 0)
    for i in range(full // 128):
        gain_column[i * 128 : (i + 1) * 128, :] = jnp.transpose(
            jnp.broadcast_to(gain_ref[i : i + 1, :], (8, 128))
        )

    before, after, across_chip = (chip + 3) % chips, (chip + 1) % chips, (chip + 2) % chips
    of = [dest_ref[pl.ds(c, 1), :] for c in (chip, before, across_chip, after)]
    span = chunk // 4
    line = jnp.concatenate(
        [
            of[c][:, k * span + p * part : k * span + (p + 1) * part]
            for order in (((0, 0), (0, 1), (1, 0), (3, 1)), ((2, 0), (2, 1), (3, 0), (1, 1)))
            for p in range(PIECES)
            for c, k in order
        ],
        axis=1,
    )
    owner_line = line // groups
    owner_column = jnp.transpose(
        jnp.broadcast_to(owner_line.astype(jnp.float32), (8, groups))
    )[:, 0:1].astype(jnp.int32)
    down = lax.broadcasted_iota(jnp.int32, (groups, groups), 0)
    across = lax.broadcasted_iota(jnp.int32, (groups, groups), 1)
    earlier = (owner_column == owner_line) & (down < across)
    rank = jnp.sum(earlier.astype(jnp.int32), axis=0, keepdims=True)
    pick[...] = jnp.where(down == owner_line * share + rank, 1.0, 0.0).astype(jnp.bfloat16)
    slot = line % groups
    which = lax.broadcasted_iota(jnp.int32, (merged.shape[0] - width, groups), 0)
    digits = jnp.where(which == 0, slot // 16, jnp.where(which == 1, slot % 16, 0))
    merged[width:, :] = digits.astype(jnp.float32).astype(jnp.bfloat16)

    def prepare_halo(at, to):
        for source, base in ((left, 0), (right, reach)):
            here = (reach - HB - at if base == 0 else at) + to
            span = slice(here, here + QB)
            slot = slice(base + here, base + here + QB)
            halo_kt[slot, :] = jnp.transpose(source[0, :, span])
            v0, v1 = split_heads(source[1, :, span])
            halo_vt[0, :, slot] = v0
            halo_vt[1, :, slot] = v1

    def spread_copy(k):
        to = (me + k) % cols
        return pltpu.make_async_remote_copy(
            src_ref=attended.at[to],
            dst_ref=att.at[my_rows],
            send_sem=spread_send.at[k],
            recv_sem=spread_recv.at[k],
            device_id={"col": to},
            device_id_type=MESH,
        )

    def halo_block(b, t):
        at = pl.multiple_of(b * QB, QB)
        qcat = query_pair(q_ref[:, pl.ds(at, QB)])
        start = bound_ref[0:1, pl.ds(at, QB)]
        length = bound_ref[1:2, pl.ds(at, QB)]
        high = b // (blocks // 2)
        slot = high * (reach + t * HB) + (1 - high) * (reach - (t + 1) * HB)
        slot = pl.multiple_of(slot, HB)
        key = slot - reach + high * tokens
        spot = lax.broadcasted_iota(jnp.int32, (HB, QB), 0) + (key - start)
        ok = (spot >= 0) & (spot < length)
        halo_step(
            halo_kt[pl.ds(slot, HB), :],
            [halo_vt[head, :, pl.ds(slot, HB)] for head in range(2)],
            qcat,
            ok,
            coef,
            m_ref.at[pl.ds(b * 2, 2)],
            l_ref.at[pl.ds(b * 2, 2)],
            acc_ref.at[pl.ds(b * 2, 2)],
        )

    def finish(b, k):
        both = [acc_ref[b * 2 + head] * (1.0 / l_ref[b * 2 + head]) for head in range(2)]
        attended[b] = jnp.concatenate(both, axis=0).astype(jnp.bfloat16)

        @pl.when(k < cols)
        def _():
            spread_copy(k).start()

    def is_middle(b):
        return (b >= blocks // 4) & (b < blocks - blocks // 4)

    def near_pass(i, carry):
        b = (me + 1 + i) % cols
        halo_block(b, 0)

        @pl.when(is_middle(b))
        def _():
            finish(b, i + 1)

        return carry

    def far_pass(i, carry):
        b = (me + 1 + i) % cols

        @pl.when(jnp.logical_not(is_middle(b)))
        def _():
            halo_block(b, 1)
            finish(b, i + 1)

        return carry

    for copy in near_halo:
        copy.wait_recv()
    for to in range(0, HB, QB):
        prepare_halo(0, to)
    lax.fori_loop(0, cols, near_pass, 0)
    for copy in far_halo:
        copy.wait_recv()
    for copy in by_x:
        copy.wait()
    for copy in by_z:
        copy.start()
    for to in range(0, HB, QB):
        prepare_halo(HB, to)
    lax.fori_loop(0, cols, far_pass, 0)
    att[my_rows, :] = attended[me]
    for copy in resident:
        copy.wait()
    for k in range(1, cols):
        spread_copy(k).wait_recv()

    def lanes(owner, p):
        return pl.ds(pl.multiple_of(owner * chunk + p * piece, 128), piece)

    here = lax.broadcasted_iota(jnp.int32, (piece, piece), 0)
    there = lax.broadcasted_iota(jnp.int32, (piece, piece), 1)
    order = jnp.where((here % 4) * part + here // 4 == there, 1.0, 0.0).astype(jnp.bfloat16)
    goal = (chip + 1 + 2 * core) % chips
    near, own, back = [], [], []
    for p in range(PIECES):
        at = slice(p * piece, (p + 1) * piece)
        projected = jnp.dot(weight_t[...], att[:, at], preferred_element_type=jnp.float32)
        rounded = (residual[:, at].astype(jnp.float32) + projected).astype(jnp.bfloat16)
        layer_rows[p] = rounded
        values32 = rounded.astype(jnp.float32)
        centre = jnp.sum(values32, axis=0, keepdims=True) * (1.0 / full)
        spread_of = jnp.sum(jnp.square(values32 - centre), axis=0, keepdims=True) * (1.0 / full)
        scale = lax.rsqrt(spread_of + 1e-06)
        normed = ((values32 - centre) * scale * gain_column[:, 0:1]).astype(jnp.bfloat16)
        held[p, core] = jnp.dot(normed, order, preferred_element_type=jnp.float32).astype(
            jnp.bfloat16
        )
        for h in range(2):
            rows_of = pl.ds(h * half, half)
            copy = pltpu.make_async_remote_copy(
                src_ref=held.at[p, core, rows_of],
                dst_ref=held.at[p, 2 + core, rows_of],
                send_sem=near_send.at[p, h],
                recv_sem=near_recv.at[p, core],
                device_id={"col": goal * 2 + h},
                device_id_type=MESH,
            )
            copy.start()
            near.append(copy)
        copy = pltpu.make_async_remote_copy(
            src_ref=held.at[p, core],
            dst_ref=held.at[p, core],
            send_sem=own_send.at[p],
            recv_sem=own_recv.at[p],
            device_id={"col": sibling},
            device_id_type=MESH,
        )
        copy.start()
        own.append(copy)
        layer_ref[:, lanes(me, p)] = layer_rows[p, my_rows, :]

    for k in range(1, cols):
        spread_copy(k).wait_send()
    passed = []
    my_half = pl.ds(pl.multiple_of(core * half, 16), half)
    for p in range(PIECES):
        for s in range(2):
            arrive = pltpu.make_async_remote_copy(
                src_ref=held.at[p, core, my_half],
                dst_ref=held.at[p, 2 + s, my_half],
                send_sem=near_send.at[p, s],
                recv_sem=near_recv.at[p, s],
                device_id={"col": sibling},
                device_id_type=MESH,
            )
            arrive.wait_recv()
            copy = pltpu.make_async_remote_copy(
                src_ref=held.at[p, 2 + s, my_half],
                dst_ref=held.at[p, 2 + s, my_half],
                send_sem=pass_send.at[p, s],
                recv_sem=pass_recv.at[p, s],
                device_id={"col": sibling},
                device_id_type=MESH,
            )
            copy.start()
            passed.append(copy)
    for copy in near:
        copy.wait_send()

    def send_back(p):
        for k in range(1, cols):
            to = (me + k) % cols
            copy = pltpu.make_async_remote_copy(
                src_ref=layer_rows.at[p, pl.ds(pl.multiple_of(to * width, 16), width)],
                dst_ref=layer_ref.at[:, lanes(me, p)],
                send_sem=back_send.at[p, k],
                recv_sem=back_recv.at[p, k],
                device_id={"col": to},
                device_id_type=MESH,
            )
            copy.start()
            back.append(copy)

    for p in range(PIECES - 1):
        send_back(p)
    for copy in by_z:
        copy.wait()
    for copy in own + passed:
        copy.wait()

    total = None
    for j in range(4):
        side = jnp.concatenate(
            [
                held[p, s, :, j * part : (j + 1) * part]
                for p in range(PIECES)
                for s in range(4)
            ],
            axis=1,
        )
        term = jnp.dot(
            merge_w[:, j * full : (j + 1) * full], side, preferred_element_type=jnp.float32
        )
        total = term if total is None else total + term
    far_rows[...] = total[width:].astype(jnp.bfloat16)
    across_y = pltpu.make_async_remote_copy(
        src_ref=far_rows,
        dst_ref=merged.at[0:width, chunk : 2 * chunk],
        send_sem=far_send,
        recv_sem=far_recv,
        device_id={"col": (me + cols // 2) % cols},
        device_id_type=MESH,
    )
    across_y.start()
    merged[0:width, 0:chunk] = total[:width].astype(jnp.bfloat16)
    across_y.wait()
    send_back(PIECES - 1)

    sorted_rows[...] = lax.dot_general(
        pick[...], merged[...], (((1,), (1,)), ((), ())), preferred_element_type=jnp.float32
    ).astype(jnp.bfloat16)
    moves = []
    for k in range(1, rows):
        to = (row + k) % rows
        copy = pltpu.make_async_remote_copy(
            src_ref=sorted_rows.at[pl.ds(pl.multiple_of(to * share, share), share)],
            dst_ref=got_rows.at[pl.ds(pl.multiple_of(row * share, share), share)],
            send_sem=row_send.at[k],
            recv_sem=row_recv.at[k],
            device_id={"row": to},
            device_id_type=MESH,
        )
        copy.start()
        moves.append(copy)
    keep = pl.ds(pl.multiple_of(row * share, share), share)
    got_rows[keep, :] = sorted_rows[keep, :]
    for copy in moves + back:
        copy.wait()
    for copy in near_halo + far_halo + shift:
        copy.wait_send()


def place_kernel(layer_hbm, got_hbm, layer_out, image_ref, layer, got_ref, sem):
    load = pltpu.make_async_copy(got_hbm, got_ref, sem.at[0])
    copies = [
        pltpu.make_async_copy(layer_hbm, layer, sem.at[1]),
        pltpu.make_async_copy(layer, layer_out, sem.at[2]),
    ]
    load.start()
    copies[0].start()
    load.wait()
    width, groups = image_ref.shape
    got = got_ref[...]
    target = got[:, width : width + 1].astype(jnp.float32) * 16.0 + got[
        :, width + 1 : width + 2
    ].astype(jnp.float32)
    slot = lax.broadcasted_iota(jnp.int32, (groups, groups), 1).astype(jnp.float32)
    put = jnp.where(target == slot, 1.0, 0.0).astype(jnp.bfloat16)
    copies[0].wait()
    copies[1].start()
    image_ref[...] = lax.dot_general(
        got, put, (((0,), (0,)), ((), ())), preferred_element_type=jnp.float32
    )[:width].astype(jnp.bfloat16)
    copies[1].wait()


def body(qkv, residual_in, out_weight, merge_weight, merge_gain, image_groups, dest_row):
    rows = lax.axis_size("row")
    cols = lax.axis_size("col")
    _, width, tokens = qkv.shape
    full = out_weight.shape[0]
    reach = tokens // 2
    blocks = tokens // QB
    chunk = tokens // cols
    piece = chunk // PIECES
    groups = tokens // 4
    bf16, f32, i32 = jnp.bfloat16, jnp.float32, jnp.int32
    coef = math.log2(math.e) / math.sqrt(HEAD_DIM)
    vmem = pl.BlockSpec(memory_space=pltpu.VMEM)
    hbm = pl.BlockSpec(memory_space=pl.ANY)
    dma = pltpu.SemaphoreType.DMA
    gain = merge_gain.reshape(-1, 128)
    dest = dest_row.reshape(cols // 2, -1)
    sizes = image_groups[None, :]
    layer, got = pl.pallas_call(
        functools.partial(layer_kernel, rows, cols, coef),
        out_shape=(
            jax.ShapeDtypeStruct((width, tokens), bf16),
            jax.ShapeDtypeStruct((groups, width + 16), bf16),
        ),
        in_specs=[hbm] * 7,
        out_specs=(vmem, vmem),
        scratch_shapes=[
            pltpu.VMEM((width, tokens), bf16),
            pltpu.VMEM((2, width, tokens), bf16),
            pltpu.VMEM((tokens, width), bf16),
            pltpu.VMEM((2, HEAD_DIM, tokens), bf16),
            pltpu.VMEM((2, width, reach), bf16),
            pltpu.VMEM((2, width, reach), bf16),
            pltpu.VMEM((2 * reach, width), bf16),
            pltpu.VMEM((2, HEAD_DIM, 2 * reach), bf16),
            pltpu.VMEM((8, tokens), i32),
            pltpu.VMEM((2, blocks, KB, QB), f32),
            pltpu.VMEM((2 * blocks, 1, QB), f32),
            pltpu.VMEM((2 * blocks, 1, QB), f32),
            pltpu.VMEM((2 * blocks, HEAD_DIM, QB), f32),
            pltpu.VMEM((blocks, width, QB), bf16),
            pltpu.VMEM((width, tokens), bf16),
            pltpu.VMEM((full, chunk), bf16),
            pltpu.VMEM((full, chunk), bf16),
            pltpu.VMEM((full, full), bf16),
            pltpu.VMEM((full, full), bf16),
            pltpu.VMEM((2 * width, merge_weight.shape[1]), bf16),
            pltpu.VMEM((PIECES, full, piece), bf16),
            pltpu.VMEM((PIECES, 4, full, piece), bf16),
            pltpu.VMEM((width, chunk), bf16),
            pltpu.VMEM((width + 16, groups), bf16),
            pltpu.VMEM((groups, groups), bf16),
            pltpu.VMEM((groups, width + 16), bf16),
            pltpu.VMEM((full, 8), f32),
            pltpu.VMEM(gain.shape, f32),
            pltpu.VMEM(sizes.shape, i32),
            pltpu.VMEM(dest.shape, i32),
            dma((9,)),
            dma((2, 2, 2)),
            dma((2, 2, 2)),
            dma((cols,)),
            dma((cols,)),
            dma((2,)),
            dma((2,)),
            dma((3, 4)),
            dma((3, 4)),
            dma((cols,)),
            dma((cols,)),
            dma((PIECES, cols)),
            dma((PIECES, cols)),
            dma((PIECES, 2)),
            dma((PIECES, 2)),
            dma((PIECES,)),
            dma((PIECES,)),
            dma((PIECES, 2)),
            dma((PIECES, 2)),
            dma,
            dma,
            dma((rows,)),
            dma((rows,)),
        ],
        compiler_params=pltpu.CompilerParams(
            collective_id=0, has_side_effects=True, vmem_limit_bytes=int(60 * 2**20)
        ),
    )(qkv, residual_in, out_weight, merge_weight, gain, sizes, dest)
    return pl.pallas_call(
        place_kernel,
        out_shape=(
            jax.ShapeDtypeStruct((width, tokens), bf16),
            jax.ShapeDtypeStruct((width, groups), bf16),
        ),
        in_specs=[hbm, hbm],
        out_specs=(hbm, vmem),
        scratch_shapes=[
            pltpu.VMEM((width, tokens), bf16),
            pltpu.VMEM((groups, width + 16), bf16),
            dma((3,)),
        ],
        compiler_params=pltpu.CompilerParams(vmem_limit_bytes=60 << 20),
    )(layer, got)


def solution(mesh):
    return jax.shard_map(
        body,
        mesh=mesh,
        in_specs=(P(None, "col", "row"), P("col", "row"), P(), P("col", None), P(), P(), P("row")),
        out_specs=(P("col", "row"), P("col", "row")),
        check_vma=False,
    )
```

```python
import functools
import math

import jax
import jax.numpy as jnp
from jax import lax
from jax.experimental import pallas as pl
from jax.experimental.pallas import tpu as pltpu
from jax.sharding import PartitionSpec as P

HEAD_DIM = 88
QB = 256
KB = 256
HB = 512
PIECES = 2
NEG = -1e30
MESH = pl.DeviceIdType.MESH


def halo_step(keys, values, qcat, ok, coef, m_ref, l_ref, acc_ref):
    width = qcat.shape[1] // 2
    scores = jnp.dot(keys, qcat, preferred_element_type=jnp.float32)
    for head in range(2):
        part = jnp.where(ok, scores[:, head * width : (head + 1) * width], NEG)
        old = m_ref[head]
        new = jnp.maximum(old, jnp.max(part, axis=0, keepdims=True))
        fade = jnp.exp2((old - new) * coef)
        expo = jnp.exp2(part * coef - new * coef)
        l_ref[head] = l_ref[head] * fade + jnp.sum(expo, axis=0, keepdims=True)
        m_ref[head] = new
        acc_ref[head] = acc_ref[head] * fade + jnp.dot(
            values[head], expo.astype(jnp.bfloat16), preferred_element_type=jnp.float32
        )


def split_heads(values):
    wide = values.astype(jnp.float32)
    return wide[:HEAD_DIM].astype(jnp.bfloat16), wide[HEAD_DIM:].astype(jnp.bfloat16)


def query_pair(block):
    feature = lax.broadcasted_iota(jnp.int32, block.shape, 0)
    zero = jnp.zeros_like(block)
    return jnp.concatenate(
        [jnp.where(feature < HEAD_DIM, block, zero), jnp.where(feature < HEAD_DIM, zero, block)],
        axis=1,
    )


def layer_kernel(
    rows,
    cols,
    coef,
    qkv_hbm,
    residual_hbm,
    out_weight_hbm,
    merge_weight_hbm,
    gain_hbm,
    groups_hbm,
    dest_hbm,
    layer_ref,
    got_rows,
    q_ref,
    kv,
    kt,
    vt,
    left,
    right,
    halo_kt,
    halo_vt,
    bound_ref,
    held_scores,
    m_ref,
    l_ref,
    acc_ref,
    attended,
    res,
    residual,
    att,
    weight,
    weight_t,
    merge_w,
    layer_rows,
    held,
    far_rows,
    merged,
    pick,
    sorted_rows,
    gain_column,
    gain_ref,
    groups_line_ref,
    dest_ref,
    load_sem,
    halo_send,
    halo_recv,
    res_send,
    res_recv,
    shift_send,
    shift_recv,
    gather_send,
    gather_recv,
    spread_send,
    spread_recv,
    back_send,
    back_recv,
    near_send,
    near_recv,
    own_send,
    own_recv,
    pass_send,
    pass_recv,
    far_send,
    far_recv,
    row_send,
    row_recv,
):
    row = lax.axis_index("row")
    me = lax.axis_index("col")
    width, tokens = q_ref.shape
    full = weight.shape[0]
    reach = left.shape[2]
    blocks = tokens // QB
    chunk = tokens // cols
    piece = chunk // PIECES
    part = piece // 4
    groups = tokens // 4
    share = groups // rows
    chips = cols // 2
    core = me % 2
    chip = me // 2
    sibling = me + 1 - 2 * core
    half = full // 2
    line_up = rows // 4
    x_at, z_at = row // line_up, row % line_up

    barrier = pltpu.get_barrier_semaphore()
    for k in range(1, cols):
        pl.semaphore_signal(
            barrier, inc=1, device_id={"col": (me + k) % cols}, device_id_type=MESH
        )
    for k in range(1, rows):
        pl.semaphore_signal(
            barrier, inc=1, device_id={"row": (row + k) % rows}, device_id_type=MESH
        )
    loads = [
        pltpu.make_async_copy(source, target, load_sem.at[i])
        for i, (source, target) in enumerate(
            (
                (qkv_hbm.at[1], kv.at[0]),
                (qkv_hbm.at[2], kv.at[1]),
                (merge_weight_hbm, merge_w.at[0:width]),
                (residual_hbm, res),
                (groups_hbm, groups_line_ref),
                (qkv_hbm.at[0], q_ref),
                (gain_hbm, gain_ref),
                (dest_hbm, dest_ref),
                (out_weight_hbm, weight),
            )
        )
    ]
    for load in loads[:4]:
        load.start()
    for load in loads[:2]:
        load.wait()
    pl.semaphore_wait(barrier, rows + cols - 2)

    after_row, before_row = (row + 1) % rows, (row + rows - 1) % rows
    mine = pl.ds(pl.multiple_of(me * chunk, chunk), chunk)
    my_rows = pl.ds(pl.multiple_of(me * width, 16), width)
    halo = []
    for side, (other, target, at) in enumerate(
        ((after_row, left, tokens - reach), (before_row, right, 0))
    ):
        for i in range(2):
            halo.append(
                pltpu.make_async_remote_copy(
                    src_ref=kv.at[i, :, at : at + reach],
                    dst_ref=target.at[i],
                    send_sem=halo_send.at[2 * side + i],
                    recv_sem=halo_recv.at[2 * side + i],
                    device_id={"row": other},
                    device_id_type=MESH,
                )
            )
    cut = width // 32 * 16 + 16
    spans = ((0, cut, x_at), (cut, width, z_at))
    shift, gather = [], []
    for s, (top, end, at) in enumerate(spans):
        across = pl.ds(pl.multiple_of(at * full, 128), full)
        place = merge_w.at[width + top : width + end, across]
        shift.append(
            pltpu.make_async_remote_copy(
                src_ref=merge_w.at[top:end, across],
                dst_ref=place,
                send_sem=shift_send.at[s],
                recv_sem=shift_recv.at[s],
                device_id={"col": (me + cols // 2) % cols},
                device_id_type=MESH,
            )
        )
        for k in range(1, 4):
            other = x_at * line_up + (z_at + k) % line_up if s else (row + k * line_up) % rows
            gather.append(
                pltpu.make_async_remote_copy(
                    src_ref=place,
                    dst_ref=place,
                    send_sem=gather_send.at[s, k],
                    recv_sem=gather_recv.at[s, k],
                    device_id={"row": other},
                    device_id_type=MESH,
                )
            )
    resident = []
    for k in range(1, cols):
        to = (me + k) % cols
        resident.append(
            pltpu.make_async_remote_copy(
                src_ref=res.at[:, pl.ds(pl.multiple_of(to * chunk, chunk), chunk)],
                dst_ref=residual.at[my_rows],
                send_sem=res_send.at[k],
                recv_sem=res_recv.at[k],
                device_id={"col": to},
                device_id_type=MESH,
            )
        )
    for copy in halo:
        copy.start()
    for load in loads[4:]:
        load.start()
    for load in loads[2:4]:
        load.wait()
    for copy in shift:
        copy.start()
    residual[my_rows, :] = res[:, mine]
    for load in loads[4:6]:
        load.wait()

    images = groups_line_ref.shape[1]
    first = lax.broadcasted_iota(jnp.int32, (images, images), 0)
    second = lax.broadcasted_iota(jnp.int32, (images, images), 1)
    sizes = groups_line_ref[...]
    size = jnp.sum(jnp.where(second == first, sizes, 0), axis=1, keepdims=True) * 4
    begin = (
        jnp.sum(jnp.where(second < first, sizes, 0), axis=1, keepdims=True) * 4 - row * tokens
    )

    def prepare(b, carry):
        at = pl.multiple_of(b * QB, QB)
        token = lax.broadcasted_iota(jnp.int32, (images, QB), 1) + at
        inside = (token >= begin) & (token < begin + size)
        bound_ref[0:1, pl.ds(at, QB)] = jnp.sum(jnp.where(inside, begin, 0), axis=0, keepdims=True)
        bound_ref[1:2, pl.ds(at, QB)] = jnp.sum(jnp.where(inside, size, 0), axis=0, keepdims=True)
        kt[pl.ds(at, QB), :] = jnp.transpose(kv[0, :, pl.ds(at, QB)])
        v0, v1 = split_heads(kv[1, :, pl.ds(at, QB)])
        vt[0, :, pl.ds(at, QB)] = v0
        vt[1, :, pl.ds(at, QB)] = v1
        return carry

    lax.fori_loop(0, blocks, prepare, 0)

    def local_block(b, carry):
        at = pl.multiple_of(b * QB, QB)
        qcat = query_pair(q_ref[:, pl.ds(at, QB)])
        start = bound_ref[0:1, pl.ds(at, QB)]
        length = bound_ref[1:2, pl.ds(at, QB)]
        spot = lax.broadcasted_iota(jnp.int32, (KB, QB), 0) - start
        tops = [jnp.full((1, QB), NEG, jnp.float32) for _ in range(2)]
        for t in range(blocks):
            key = t * KB
            scores = jnp.dot(kt[key : key + KB, :], qcat, preferred_element_type=jnp.float32)
            ok = (spot >= -key) & (spot < length - key)
            for head in range(2):
                masked = jnp.where(ok, scores[:, head * QB : (head + 1) * QB], NEG)
                held_scores[head, t] = masked
                tops[head] = jnp.maximum(tops[head], jnp.max(masked, axis=0, keepdims=True))
        for head in range(2):
            peak = tops[head] * coef
            total = jnp.zeros((1, QB), jnp.float32)
            sums = jnp.zeros((HEAD_DIM, QB), jnp.float32)
            for t in range(blocks):
                expo = jnp.exp2(held_scores[head, t] * coef - peak)
                total = total + jnp.sum(expo, axis=0, keepdims=True)
                sums = sums + jnp.dot(
                    vt[head, :, t * KB : (t + 1) * KB],
                    expo.astype(jnp.bfloat16),
                    preferred_element_type=jnp.float32,
                )
            m_ref[b * 2 + head] = tops[head]
            l_ref[b * 2 + head] = total
            acc_ref[b * 2 + head] = sums
        return carry

    lax.fori_loop(0, blocks // 2, local_block, 0)
    for copy in resident:
        copy.start()
    lax.fori_loop(blocks // 2, blocks, local_block, 0)

    for load in loads[6:]:
        load.wait()

    def turn(i, carry):
        at = pl.multiple_of(i * 128, 128)
        weight_t[pl.ds(at, 128), :] = jnp.transpose(weight[:, pl.ds(at, 128)])
        return carry

    lax.fori_loop(0, full // 128, turn, 0)
    for i in range(full // 128):
        gain_column[i * 128 : (i + 1) * 128, :] = jnp.transpose(
            jnp.broadcast_to(gain_ref[i : i + 1, :], (8, 128))
        )

    before, after, across_chip = (chip + 3) % chips, (chip + 1) % chips, (chip + 2) % chips
    of = [dest_ref[pl.ds(c, 1), :] for c in (chip, before, across_chip, after)]
    span = chunk // 4
    line = jnp.concatenate(
        [
            of[c][:, k * span + p * part : k * span + (p + 1) * part]
            for order in (((0, 0), (0, 1), (1, 0), (3, 1)), ((2, 0), (2, 1), (3, 0), (1, 1)))
            for p in range(PIECES)
            for c, k in order
        ],
        axis=1,
    )
    owner_line = line // groups
    owner_column = jnp.transpose(
        jnp.broadcast_to(owner_line.astype(jnp.float32), (8, groups))
    )[:, 0:1].astype(jnp.int32)
    down = lax.broadcasted_iota(jnp.int32, (groups, groups), 0)
    across = lax.broadcasted_iota(jnp.int32, (groups, groups), 1)
    earlier = (owner_column == owner_line) & (down < across)
    rank = jnp.sum(earlier.astype(jnp.int32), axis=0, keepdims=True)
    pick[...] = jnp.where(down == owner_line * share + rank, 1.0, 0.0).astype(jnp.bfloat16)
    slot = line % groups
    which = lax.broadcasted_iota(jnp.int32, (merged.shape[0] - width, groups), 0)
    digits = jnp.where(which == 0, slot // 16, jnp.where(which == 1, slot % 16, 0))
    merged[width:, :] = digits.astype(jnp.float32).astype(jnp.bfloat16)

    for copy in shift:
        copy.wait_recv()
    for copy in gather:
        copy.start()
    for copy in halo:
        copy.wait_recv()

    def prepare_halo(i, carry):
        at = pl.multiple_of(i * QB, QB)
        for source, base in ((left, 0), (right, reach)):
            to = pl.ds(pl.multiple_of(base + at, QB), QB)
            halo_kt[to, :] = jnp.transpose(source[0, :, pl.ds(at, QB)])
            v0, v1 = split_heads(source[1, :, pl.ds(at, QB)])
            halo_vt[0, :, to] = v0
            halo_vt[1, :, to] = v1
        return carry

    lax.fori_loop(0, reach // QB, prepare_halo, 0)

    def spread_copy(k):
        to = (me + k) % cols
        return pltpu.make_async_remote_copy(
            src_ref=attended.at[to],
            dst_ref=att.at[my_rows],
            send_sem=spread_send.at[k],
            recv_sem=spread_recv.at[k],
            device_id={"col": to},
            device_id_type=MESH,
        )

    def halo_block(b):
        at = pl.multiple_of(b * QB, QB)
        qcat = query_pair(q_ref[:, pl.ds(at, QB)])
        start = bound_ref[0:1, pl.ds(at, QB)]
        length = bound_ref[1:2, pl.ds(at, QB)]
        high = b // (blocks // 2)
        tiles = high * (b - blocks // 2 + 1) + (1 - high) * (blocks // 2 - b)

        def pair(t, inner):
            slot = high * (reach + t * HB) + (1 - high) * (reach - (t + 1) * HB)
            slot = pl.multiple_of(slot, HB)
            key = slot - reach + high * tokens
            spot = lax.broadcasted_iota(jnp.int32, (HB, QB), 0) + (key - start)
            ok = (spot >= 0) & (spot < length)
            halo_step(
                halo_kt[pl.ds(slot, HB), :],
                [halo_vt[head, :, pl.ds(slot, HB)] for head in range(2)],
                qcat,
                ok,
                coef,
                m_ref.at[pl.ds(b * 2, 2)],
                l_ref.at[pl.ds(b * 2, 2)],
                acc_ref.at[pl.ds(b * 2, 2)],
            )
            return inner

        lax.fori_loop(0, (tiles * KB + HB - 1) // HB, pair, 0)
        both = [acc_ref[b * 2 + head] * (1.0 / l_ref[b * 2 + head]) for head in range(2)]
        attended[b] = jnp.concatenate(both, axis=0).astype(jnp.bfloat16)

    def block_of(i, carry):
        halo_block((me + 1 + i) % cols)
        spread_copy(1 + i).start()
        return carry

    lax.fori_loop(0, cols - 1, block_of, 0)
    halo_block(me)
    att[my_rows, :] = attended[me]
    for copy in resident:
        copy.wait()
    for k in range(1, cols):
        spread_copy(k).wait_recv()

    def lanes(owner, p):
        return pl.ds(pl.multiple_of(owner * chunk + p * piece, 128), piece)

    here = lax.broadcasted_iota(jnp.int32, (piece, piece), 0)
    there = lax.broadcasted_iota(jnp.int32, (piece, piece), 1)
    order = jnp.where((here % 4) * part + here // 4 == there, 1.0, 0.0).astype(jnp.bfloat16)
    goal = (chip + 1 + 2 * core) % chips
    near, own, back = [], [], []
    for p in range(PIECES):
        at = slice(p * piece, (p + 1) * piece)
        projected = jnp.dot(weight_t[...], att[:, at], preferred_element_type=jnp.float32)
        rounded = (residual[:, at].astype(jnp.float32) + projected).astype(jnp.bfloat16)
        layer_rows[p] = rounded
        values32 = rounded.astype(jnp.float32)
        centre = jnp.sum(values32, axis=0, keepdims=True) * (1.0 / full)
        spread_of = jnp.sum(jnp.square(values32 - centre), axis=0, keepdims=True) * (1.0 / full)
        scale = lax.rsqrt(spread_of + 1e-06)
        normed = ((values32 - centre) * scale * gain_column[:, 0:1]).astype(jnp.bfloat16)
        held[p, core] = jnp.dot(normed, order, preferred_element_type=jnp.float32).astype(
            jnp.bfloat16
        )
        for h in range(2):
            rows_of = pl.ds(h * half, half)
            copy = pltpu.make_async_remote_copy(
                src_ref=held.at[p, core, rows_of],
                dst_ref=held.at[p, 2 + core, rows_of],
                send_sem=near_send.at[p, h],
                recv_sem=near_recv.at[p, core],
                device_id={"col": goal * 2 + h},
                device_id_type=MESH,
            )
            copy.start()
            near.append(copy)
        copy = pltpu.make_async_remote_copy(
            src_ref=held.at[p, core],
            dst_ref=held.at[p, core],
            send_sem=own_send.at[p],
            recv_sem=own_recv.at[p],
            device_id={"col": sibling},
            device_id_type=MESH,
        )
        copy.start()
        own.append(copy)
        layer_ref[:, lanes(me, p)] = layer_rows[p, my_rows, :]

    for k in range(1, cols):
        spread_copy(k).wait_send()
    passed = []
    my_half = pl.ds(pl.multiple_of(core * half, 16), half)
    for p in range(PIECES):
        for s in range(2):
            arrive = pltpu.make_async_remote_copy(
                src_ref=held.at[p, core, my_half],
                dst_ref=held.at[p, 2 + s, my_half],
                send_sem=near_send.at[p, s],
                recv_sem=near_recv.at[p, s],
                device_id={"col": sibling},
                device_id_type=MESH,
            )
            arrive.wait_recv()
            copy = pltpu.make_async_remote_copy(
                src_ref=held.at[p, 2 + s, my_half],
                dst_ref=held.at[p, 2 + s, my_half],
                send_sem=pass_send.at[p, s],
                recv_sem=pass_recv.at[p, s],
                device_id={"col": sibling},
                device_id_type=MESH,
            )
            copy.start()
            passed.append(copy)
    for copy in near:
        copy.wait_send()

    def send_back(p):
        for k in range(1, cols):
            to = (me + k) % cols
            copy = pltpu.make_async_remote_copy(
                src_ref=layer_rows.at[p, pl.ds(pl.multiple_of(to * width, 16), width)],
                dst_ref=layer_ref.at[:, lanes(me, p)],
                send_sem=back_send.at[p, k],
                recv_sem=back_recv.at[p, k],
                device_id={"col": to},
                device_id_type=MESH,
            )
            copy.start()
            back.append(copy)

    for p in range(PIECES - 1):
        send_back(p)
    for copy in gather:
        copy.wait()
    for copy in own + passed:
        copy.wait()

    total = None
    for j in range(4):
        side = jnp.concatenate(
            [
                held[p, s, :, j * part : (j + 1) * part]
                for p in range(PIECES)
                for s in range(4)
            ],
            axis=1,
        )
        term = jnp.dot(
            merge_w[:, j * full : (j + 1) * full], side, preferred_element_type=jnp.float32
        )
        total = term if total is None else total + term
    far_rows[...] = total[width:].astype(jnp.bfloat16)
    across_y = pltpu.make_async_remote_copy(
        src_ref=far_rows,
        dst_ref=merged.at[0:width, chunk : 2 * chunk],
        send_sem=far_send,
        recv_sem=far_recv,
        device_id={"col": (me + cols // 2) % cols},
        device_id_type=MESH,
    )
    across_y.start()
    merged[0:width, 0:chunk] = total[:width].astype(jnp.bfloat16)
    across_y.wait()
    send_back(PIECES - 1)

    sorted_rows[...] = lax.dot_general(
        pick[...], merged[...], (((1,), (1,)), ((), ())), preferred_element_type=jnp.float32
    ).astype(jnp.bfloat16)
    moves = []
    for k in range(1, rows):
        to = (row + k) % rows
        copy = pltpu.make_async_remote_copy(
            src_ref=sorted_rows.at[pl.ds(pl.multiple_of(to * share, share), share)],
            dst_ref=got_rows.at[pl.ds(pl.multiple_of(row * share, share), share)],
            send_sem=row_send.at[k],
            recv_sem=row_recv.at[k],
            device_id={"row": to},
            device_id_type=MESH,
        )
        copy.start()
        moves.append(copy)
    keep = pl.ds(pl.multiple_of(row * share, share), share)
    got_rows[keep, :] = sorted_rows[keep, :]
    for copy in moves + back:
        copy.wait()
    for copy in halo + shift:
        copy.wait_send()


def place_kernel(layer_hbm, got_hbm, layer_out, image_ref, layer, got_ref, sem):
    load = pltpu.make_async_copy(got_hbm, got_ref, sem.at[0])
    copies = [
        pltpu.make_async_copy(layer_hbm, layer, sem.at[1]),
        pltpu.make_async_copy(layer, layer_out, sem.at[2]),
    ]
    load.start()
    copies[0].start()
    load.wait()
    width, groups = image_ref.shape
    got = got_ref[...]
    target = got[:, width : width + 1].astype(jnp.float32) * 16.0 + got[
        :, width + 1 : width + 2
    ].astype(jnp.float32)
    slot = lax.broadcasted_iota(jnp.int32, (groups, groups), 1).astype(jnp.float32)
    put = jnp.where(target == slot, 1.0, 0.0).astype(jnp.bfloat16)
    copies[0].wait()
    copies[1].start()
    image_ref[...] = lax.dot_general(
        got, put, (((0,), (0,)), ((), ())), preferred_element_type=jnp.float32
    )[:width].astype(jnp.bfloat16)
    copies[1].wait()


def body(qkv, residual_in, out_weight, merge_weight, merge_gain, image_groups, dest_row):
    rows = lax.axis_size("row")
    cols = lax.axis_size("col")
    _, width, tokens = qkv.shape
    full = out_weight.shape[0]
    reach = tokens // 2
    blocks = tokens // QB
    chunk = tokens // cols
    piece = chunk // PIECES
    groups = tokens // 4
    bf16, f32, i32 = jnp.bfloat16, jnp.float32, jnp.int32
    coef = math.log2(math.e) / math.sqrt(HEAD_DIM)
    vmem = pl.BlockSpec(memory_space=pltpu.VMEM)
    hbm = pl.BlockSpec(memory_space=pl.ANY)
    dma = pltpu.SemaphoreType.DMA
    gain = merge_gain.reshape(-1, 128)
    dest = dest_row.reshape(cols // 2, -1)
    sizes = image_groups[None, :]
    layer, got = pl.pallas_call(
        functools.partial(layer_kernel, rows, cols, coef),
        out_shape=(
            jax.ShapeDtypeStruct((width, tokens), bf16),
            jax.ShapeDtypeStruct((groups, width + 16), bf16),
        ),
        in_specs=[hbm] * 7,
        out_specs=(vmem, vmem),
        scratch_shapes=[
            pltpu.VMEM((width, tokens), bf16),
            pltpu.VMEM((2, width, tokens), bf16),
            pltpu.VMEM((tokens, width), bf16),
            pltpu.VMEM((2, HEAD_DIM, tokens), bf16),
            pltpu.VMEM((2, width, reach), bf16),
            pltpu.VMEM((2, width, reach), bf16),
            pltpu.VMEM((2 * reach, width), bf16),
            pltpu.VMEM((2, HEAD_DIM, 2 * reach), bf16),
            pltpu.VMEM((8, tokens), i32),
            pltpu.VMEM((2, blocks, KB, QB), f32),
            pltpu.VMEM((2 * blocks, 1, QB), f32),
            pltpu.VMEM((2 * blocks, 1, QB), f32),
            pltpu.VMEM((2 * blocks, HEAD_DIM, QB), f32),
            pltpu.VMEM((blocks, width, QB), bf16),
            pltpu.VMEM((width, tokens), bf16),
            pltpu.VMEM((full, chunk), bf16),
            pltpu.VMEM((full, chunk), bf16),
            pltpu.VMEM((full, full), bf16),
            pltpu.VMEM((full, full), bf16),
            pltpu.VMEM((2 * width, merge_weight.shape[1]), bf16),
            pltpu.VMEM((PIECES, full, piece), bf16),
            pltpu.VMEM((PIECES, 4, full, piece), bf16),
            pltpu.VMEM((width, chunk), bf16),
            pltpu.VMEM((width + 16, groups), bf16),
            pltpu.VMEM((groups, groups), bf16),
            pltpu.VMEM((groups, width + 16), bf16),
            pltpu.VMEM((full, 8), f32),
            pltpu.VMEM(gain.shape, f32),
            pltpu.VMEM(sizes.shape, i32),
            pltpu.VMEM(dest.shape, i32),
            dma((9,)),
            dma((4,)),
            dma((4,)),
            dma((cols,)),
            dma((cols,)),
            dma((2,)),
            dma((2,)),
            dma((2, 4)),
            dma((2, 4)),
            dma((cols,)),
            dma((cols,)),
            dma((PIECES, cols)),
            dma((PIECES, cols)),
            dma((PIECES, 2)),
            dma((PIECES, 2)),
            dma((PIECES,)),
            dma((PIECES,)),
            dma((PIECES, 2)),
            dma((PIECES, 2)),
            dma,
            dma,
            dma((rows,)),
            dma((rows,)),
        ],
        compiler_params=pltpu.CompilerParams(
            collective_id=0, has_side_effects=True, vmem_limit_bytes=int(60 * 2**20)
        ),
    )(qkv, residual_in, out_weight, merge_weight, gain, sizes, dest)
    return pl.pallas_call(
        place_kernel,
        out_shape=(
            jax.ShapeDtypeStruct((width, tokens), bf16),
            jax.ShapeDtypeStruct((width, groups), bf16),
        ),
        in_specs=[hbm, hbm],
        out_specs=(hbm, vmem),
        scratch_shapes=[
            pltpu.VMEM((width, tokens), bf16),
            pltpu.VMEM((groups, width + 16), bf16),
            dma((3,)),
        ],
        compiler_params=pltpu.CompilerParams(vmem_limit_bytes=60 << 20),
    )(layer, got)


def solution(mesh):
    return jax.shard_map(
        body,
        mesh=mesh,
        in_specs=(P(None, "col", "row"), P("col", "row"), P(), P("col", None), P(), P(), P("row")),
        out_specs=(P("col", "row"), P("col", "row")),
        check_vma=False,
    )
```

```python
import functools
import math

import jax
import jax.numpy as jnp
from jax import lax
from jax.experimental import pallas as pl
from jax.experimental.pallas import tpu as pltpu
from jax.sharding import PartitionSpec as P

HEAD_DIM = 88
QB = 256
KB = 256
HB = 512
PIECES = 2
NEG = -1e30
MESH = pl.DeviceIdType.MESH


def halo_step(keys, values, qcat, ok, coef, m_ref, l_ref, acc_ref):
    width = qcat.shape[1] // 2
    scores = jnp.dot(keys, qcat, preferred_element_type=jnp.float32)
    for head in range(2):
        part = jnp.where(ok, scores[:, head * width : (head + 1) * width], NEG)
        old = m_ref[head]
        new = jnp.maximum(old, jnp.max(part, axis=0, keepdims=True))
        fade = jnp.exp2((old - new) * coef)
        expo = jnp.exp2(part * coef - new * coef)
        l_ref[head] = l_ref[head] * fade + jnp.sum(expo, axis=0, keepdims=True)
        m_ref[head] = new
        acc_ref[head] = acc_ref[head] * fade + jnp.dot(
            values[head], expo.astype(jnp.bfloat16), preferred_element_type=jnp.float32
        )


def split_heads(values):
    wide = values.astype(jnp.float32)
    return wide[:HEAD_DIM].astype(jnp.bfloat16), wide[HEAD_DIM:].astype(jnp.bfloat16)


def query_pair(block):
    feature = lax.broadcasted_iota(jnp.int32, block.shape, 0)
    zero = jnp.zeros_like(block)
    return jnp.concatenate(
        [jnp.where(feature < HEAD_DIM, block, zero), jnp.where(feature < HEAD_DIM, zero, block)],
        axis=1,
    )


def layer_kernel(
    rows,
    cols,
    coef,
    qkv_hbm,
    residual_hbm,
    out_weight_hbm,
    merge_weight_hbm,
    gain_hbm,
    groups_hbm,
    dest_hbm,
    layer_ref,
    got_rows,
    q_ref,
    kv,
    kt,
    vt,
    left,
    right,
    halo_kt,
    halo_vt,
    bound_ref,
    held_scores,
    m_ref,
    l_ref,
    acc_ref,
    attended,
    res,
    residual,
    att,
    weight,
    weight_t,
    merge_w,
    layer_rows,
    held,
    far_rows,
    merged,
    pick,
    sorted_rows,
    gain_column,
    gain_ref,
    groups_line_ref,
    dest_ref,
    load_sem,
    halo_send,
    halo_recv,
    res_send,
    res_recv,
    shift_send,
    shift_recv,
    gather_send,
    gather_recv,
    spread_send,
    spread_recv,
    back_send,
    back_recv,
    near_send,
    near_recv,
    own_send,
    own_recv,
    pass_send,
    pass_recv,
    far_send,
    far_recv,
    row_send,
    row_recv,
):
    row = lax.axis_index("row")
    me = lax.axis_index("col")
    width, tokens = q_ref.shape
    full = weight.shape[0]
    reach = left.shape[2]
    blocks = tokens // QB
    chunk = tokens // cols
    piece = chunk // PIECES
    part = piece // 4
    groups = tokens // 4
    share = groups // rows
    chips = cols // 2
    core = me % 2
    chip = me // 2
    sibling = me + 1 - 2 * core
    half = full // 2
    line_up = rows // 4
    x_at, z_at = row // line_up, row % line_up

    barrier = pltpu.get_barrier_semaphore()
    for k in range(1, cols):
        pl.semaphore_signal(
            barrier, inc=1, device_id={"col": (me + k) % cols}, device_id_type=MESH
        )
    for k in range(1, rows):
        pl.semaphore_signal(
            barrier, inc=1, device_id={"row": (row + k) % rows}, device_id_type=MESH
        )
    loads = [
        pltpu.make_async_copy(source, target, load_sem.at[i])
        for i, (source, target) in enumerate(
            (
                (qkv_hbm.at[1], kv.at[0]),
                (qkv_hbm.at[2], kv.at[1]),
                (merge_weight_hbm, merge_w.at[0:width]),
                (residual_hbm, res),
                (groups_hbm, groups_line_ref),
                (qkv_hbm.at[0], q_ref),
                (gain_hbm, gain_ref),
                (dest_hbm, dest_ref),
                (out_weight_hbm, weight),
            )
        )
    ]
    for load in loads[:4]:
        load.start()
    for load in loads[:2]:
        load.wait()
    pl.semaphore_wait(barrier, rows + cols - 2)

    after_row, before_row = (row + 1) % rows, (row + rows - 1) % rows
    mine = pl.ds(pl.multiple_of(me * chunk, chunk), chunk)
    my_rows = pl.ds(pl.multiple_of(me * width, 16), width)
    halo = []
    for side, (other, target, at) in enumerate(
        ((after_row, left, tokens - reach), (before_row, right, 0))
    ):
        for i in range(2):
            halo.append(
                pltpu.make_async_remote_copy(
                    src_ref=kv.at[i, :, at : at + reach],
                    dst_ref=target.at[i],
                    send_sem=halo_send.at[2 * side + i],
                    recv_sem=halo_recv.at[2 * side + i],
                    device_id={"row": other},
                    device_id_type=MESH,
                )
            )
    cut = width // 32 * 16 + 16
    spans = ((0, cut, x_at), (cut, width, z_at))
    shift, gather = [], []
    for s, (top, end, at) in enumerate(spans):
        across = pl.ds(pl.multiple_of(at * full, 128), full)
        place = merge_w.at[width + top : width + end, across]
        shift.append(
            pltpu.make_async_remote_copy(
                src_ref=merge_w.at[top:end, across],
                dst_ref=place,
                send_sem=shift_send.at[s],
                recv_sem=shift_recv.at[s],
                device_id={"col": (me + cols // 2) % cols},
                device_id_type=MESH,
            )
        )
        for k in range(1, 4):
            other = x_at * line_up + (z_at + k) % line_up if s else (row + k * line_up) % rows
            gather.append(
                pltpu.make_async_remote_copy(
                    src_ref=place,
                    dst_ref=place,
                    send_sem=gather_send.at[s, k],
                    recv_sem=gather_recv.at[s, k],
                    device_id={"row": other},
                    device_id_type=MESH,
                )
            )
    resident = []
    for k in range(1, cols):
        to = (me + k) % cols
        resident.append(
            pltpu.make_async_remote_copy(
                src_ref=res.at[:, pl.ds(pl.multiple_of(to * chunk, chunk), chunk)],
                dst_ref=residual.at[my_rows],
                send_sem=res_send.at[k],
                recv_sem=res_recv.at[k],
                device_id={"col": to},
                device_id_type=MESH,
            )
        )
    for copy in halo:
        copy.start()
    for load in loads[4:]:
        load.start()
    for load in loads[2:4]:
        load.wait()
    for copy in shift:
        copy.start()
    residual[my_rows, :] = res[:, mine]
    for load in loads[4:6]:
        load.wait()

    images = groups_line_ref.shape[1]
    first = lax.broadcasted_iota(jnp.int32, (images, images), 0)
    second = lax.broadcasted_iota(jnp.int32, (images, images), 1)
    sizes = groups_line_ref[...]
    size = jnp.sum(jnp.where(second == first, sizes, 0), axis=1, keepdims=True) * 4
    begin = (
        jnp.sum(jnp.where(second < first, sizes, 0), axis=1, keepdims=True) * 4 - row * tokens
    )

    def prepare(b, carry):
        at = pl.multiple_of(b * QB, QB)
        token = lax.broadcasted_iota(jnp.int32, (images, QB), 1) + at
        inside = (token >= begin) & (token < begin + size)
        bound_ref[0:1, pl.ds(at, QB)] = jnp.sum(jnp.where(inside, begin, 0), axis=0, keepdims=True)
        bound_ref[1:2, pl.ds(at, QB)] = jnp.sum(jnp.where(inside, size, 0), axis=0, keepdims=True)
        kt[pl.ds(at, QB), :] = jnp.transpose(kv[0, :, pl.ds(at, QB)])
        v0, v1 = split_heads(kv[1, :, pl.ds(at, QB)])
        vt[0, :, pl.ds(at, QB)] = v0
        vt[1, :, pl.ds(at, QB)] = v1
        return carry

    lax.fori_loop(0, blocks, prepare, 0)

    def local_block(b, carry):
        at = pl.multiple_of(b * QB, QB)
        qcat = query_pair(q_ref[:, pl.ds(at, QB)])
        start = bound_ref[0:1, pl.ds(at, QB)]
        length = bound_ref[1:2, pl.ds(at, QB)]
        spot = lax.broadcasted_iota(jnp.int32, (KB, QB), 0) - start
        tops = [jnp.full((1, QB), NEG, jnp.float32) for _ in range(2)]
        for t in range(blocks):
            key = t * KB
            scores = jnp.dot(kt[key : key + KB, :], qcat, preferred_element_type=jnp.float32)
            ok = (spot >= -key) & (spot < length - key)
            for head in range(2):
                masked = jnp.where(ok, scores[:, head * QB : (head + 1) * QB], NEG)
                held_scores[head, t] = masked
                tops[head] = jnp.maximum(tops[head], jnp.max(masked, axis=0, keepdims=True))
        for head in range(2):
            peak = tops[head] * coef
            total = jnp.zeros((1, QB), jnp.float32)
            sums = jnp.zeros((HEAD_DIM, QB), jnp.float32)
            for t in range(blocks):
                expo = jnp.exp2(held_scores[head, t] * coef - peak)
                total = total + jnp.sum(expo, axis=0, keepdims=True)
                sums = sums + jnp.dot(
                    vt[head, :, t * KB : (t + 1) * KB],
                    expo.astype(jnp.bfloat16),
                    preferred_element_type=jnp.float32,
                )
            m_ref[b * 2 + head] = tops[head]
            l_ref[b * 2 + head] = total
            acc_ref[b * 2 + head] = sums
        return carry

    lax.fori_loop(0, blocks // 2, local_block, 0)
    for copy in resident:
        copy.start()
    lax.fori_loop(blocks // 2, blocks, local_block, 0)

    for load in loads[6:]:
        load.wait()

    def turn(i, carry):
        at = pl.multiple_of(i * 128, 128)
        weight_t[pl.ds(at, 128), :] = jnp.transpose(weight[:, pl.ds(at, 128)])
        return carry

    lax.fori_loop(0, full // 128, turn, 0)
    for i in range(full // 128):
        gain_column[i * 128 : (i + 1) * 128, :] = jnp.transpose(
            jnp.broadcast_to(gain_ref[i : i + 1, :], (8, 128))
        )

    before, after, across_chip = (chip + 3) % chips, (chip + 1) % chips, (chip + 2) % chips
    of = [dest_ref[pl.ds(c, 1), :] for c in (chip, before, across_chip, after)]
    span = chunk // 4
    line = jnp.concatenate(
        [
            of[c][:, k * span + p * part : k * span + (p + 1) * part]
            for order in (((0, 0), (0, 1), (1, 0), (3, 1)), ((2, 0), (2, 1), (3, 0), (1, 1)))
            for p in range(PIECES)
            for c, k in order
        ],
        axis=1,
    )
    owner_line = line // groups
    owner_column = jnp.transpose(
        jnp.broadcast_to(owner_line.astype(jnp.float32), (8, groups))
    )[:, 0:1].astype(jnp.int32)
    down = lax.broadcasted_iota(jnp.int32, (groups, groups), 0)
    across = lax.broadcasted_iota(jnp.int32, (groups, groups), 1)
    earlier = (owner_column == owner_line) & (down < across)
    rank = jnp.sum(earlier.astype(jnp.int32), axis=0, keepdims=True)
    pick[...] = jnp.where(down == owner_line * share + rank, 1.0, 0.0).astype(jnp.bfloat16)
    slot = line % groups
    which = lax.broadcasted_iota(jnp.int32, (merged.shape[0] - width, groups), 0)
    digits = jnp.where(which == 0, slot // 16, jnp.where(which == 1, slot % 16, 0))
    merged[width:, :] = digits.astype(jnp.float32).astype(jnp.bfloat16)

    for copy in halo:
        copy.wait_recv()
    for copy in shift:
        copy.wait_recv()
    for copy in gather:
        copy.start()

    def prepare_halo(i, carry):
        at = pl.multiple_of(i * QB, QB)
        for source, base in ((left, 0), (right, reach)):
            to = pl.ds(pl.multiple_of(base + at, QB), QB)
            halo_kt[to, :] = jnp.transpose(source[0, :, pl.ds(at, QB)])
            v0, v1 = split_heads(source[1, :, pl.ds(at, QB)])
            halo_vt[0, :, to] = v0
            halo_vt[1, :, to] = v1
        return carry

    lax.fori_loop(0, reach // QB, prepare_halo, 0)

    def spread_copy(k):
        to = (me + k) % cols
        return pltpu.make_async_remote_copy(
            src_ref=attended.at[to],
            dst_ref=att.at[my_rows],
            send_sem=spread_send.at[k],
            recv_sem=spread_recv.at[k],
            device_id={"col": to},
            device_id_type=MESH,
        )

    def halo_block(b):
        at = pl.multiple_of(b * QB, QB)
        qcat = query_pair(q_ref[:, pl.ds(at, QB)])
        start = bound_ref[0:1, pl.ds(at, QB)]
        length = bound_ref[1:2, pl.ds(at, QB)]
        high = b // (blocks // 2)
        tiles = high * (b - blocks // 2 + 1) + (1 - high) * (blocks // 2 - b)

        def pair(t, inner):
            slot = high * (reach + t * HB) + (1 - high) * (reach - (t + 1) * HB)
            slot = pl.multiple_of(slot, HB)
            key = slot - reach + high * tokens
            spot = lax.broadcasted_iota(jnp.int32, (HB, QB), 0) + (key - start)
            ok = (spot >= 0) & (spot < length)
            halo_step(
                halo_kt[pl.ds(slot, HB), :],
                [halo_vt[head, :, pl.ds(slot, HB)] for head in range(2)],
                qcat,
                ok,
                coef,
                m_ref.at[pl.ds(b * 2, 2)],
                l_ref.at[pl.ds(b * 2, 2)],
                acc_ref.at[pl.ds(b * 2, 2)],
            )
            return inner

        lax.fori_loop(0, (tiles * KB + HB - 1) // HB, pair, 0)
        both = [acc_ref[b * 2 + head] * (1.0 / l_ref[b * 2 + head]) for head in range(2)]
        attended[b] = jnp.concatenate(both, axis=0).astype(jnp.bfloat16)

    def block_of(i, carry):
        halo_block((me + 1 + i) % cols)
        spread_copy(1 + i).start()
        return carry

    lax.fori_loop(0, cols - 1, block_of, 0)
    halo_block(me)
    att[my_rows, :] = attended[me]
    for copy in resident:
        copy.wait()
    for k in range(1, cols):
        spread_copy(k).wait_recv()

    def lanes(owner, p):
        return pl.ds(pl.multiple_of(owner * chunk + p * piece, 128), piece)

    here = lax.broadcasted_iota(jnp.int32, (piece, piece), 0)
    there = lax.broadcasted_iota(jnp.int32, (piece, piece), 1)
    order = jnp.where((here % 4) * part + here // 4 == there, 1.0, 0.0).astype(jnp.bfloat16)
    goal = (chip + 1 + 2 * core) % chips
    near, own, back = [], [], []
    for p in range(PIECES):
        at = slice(p * piece, (p + 1) * piece)
        projected = jnp.dot(weight_t[...], att[:, at], preferred_element_type=jnp.float32)
        rounded = (residual[:, at].astype(jnp.float32) + projected).astype(jnp.bfloat16)
        layer_rows[p] = rounded
        values32 = rounded.astype(jnp.float32)
        centre = jnp.sum(values32, axis=0, keepdims=True) * (1.0 / full)
        spread_of = jnp.sum(jnp.square(values32 - centre), axis=0, keepdims=True) * (1.0 / full)
        scale = lax.rsqrt(spread_of + 1e-06)
        normed = ((values32 - centre) * scale * gain_column[:, 0:1]).astype(jnp.bfloat16)
        held[p, core] = jnp.dot(normed, order, preferred_element_type=jnp.float32).astype(
            jnp.bfloat16
        )
        for h in range(2):
            rows_of = pl.ds(h * half, half)
            copy = pltpu.make_async_remote_copy(
                src_ref=held.at[p, core, rows_of],
                dst_ref=held.at[p, 2 + core, rows_of],
                send_sem=near_send.at[p, h],
                recv_sem=near_recv.at[p, core],
                device_id={"col": goal * 2 + h},
                device_id_type=MESH,
            )
            copy.start()
            near.append(copy)
        copy = pltpu.make_async_remote_copy(
            src_ref=held.at[p, core],
            dst_ref=held.at[p, core],
            send_sem=own_send.at[p],
            recv_sem=own_recv.at[p],
            device_id={"col": sibling},
            device_id_type=MESH,
        )
        copy.start()
        own.append(copy)
        layer_ref[:, lanes(me, p)] = layer_rows[p, my_rows, :]

    for k in range(1, cols):
        spread_copy(k).wait_send()
    passed = []
    my_half = pl.ds(pl.multiple_of(core * half, 16), half)
    for p in range(PIECES):
        for s in range(2):
            arrive = pltpu.make_async_remote_copy(
                src_ref=held.at[p, core, my_half],
                dst_ref=held.at[p, 2 + s, my_half],
                send_sem=near_send.at[p, s],
                recv_sem=near_recv.at[p, s],
                device_id={"col": sibling},
                device_id_type=MESH,
            )
            arrive.wait_recv()
            copy = pltpu.make_async_remote_copy(
                src_ref=held.at[p, 2 + s, my_half],
                dst_ref=held.at[p, 2 + s, my_half],
                send_sem=pass_send.at[p, s],
                recv_sem=pass_recv.at[p, s],
                device_id={"col": sibling},
                device_id_type=MESH,
            )
            copy.start()
            passed.append(copy)
    for copy in near:
        copy.wait_send()

    def send_back(p):
        for k in range(1, cols):
            to = (me + k) % cols
            copy = pltpu.make_async_remote_copy(
                src_ref=layer_rows.at[p, pl.ds(pl.multiple_of(to * width, 16), width)],
                dst_ref=layer_ref.at[:, lanes(me, p)],
                send_sem=back_send.at[p, k],
                recv_sem=back_recv.at[p, k],
                device_id={"col": to},
                device_id_type=MESH,
            )
            copy.start()
            back.append(copy)

    for p in range(PIECES - 1):
        send_back(p)
    for copy in gather:
        copy.wait()
    for copy in own + passed:
        copy.wait()

    total = None
    for j in range(4):
        side = jnp.concatenate(
            [
                held[p, s, :, j * part : (j + 1) * part]
                for p in range(PIECES)
                for s in range(4)
            ],
            axis=1,
        )
        term = jnp.dot(
            merge_w[:, j * full : (j + 1) * full], side, preferred_element_type=jnp.float32
        )
        total = term if total is None else total + term
    far_rows[...] = total[width:].astype(jnp.bfloat16)
    across_y = pltpu.make_async_remote_copy(
        src_ref=far_rows,
        dst_ref=merged.at[0:width, chunk : 2 * chunk],
        send_sem=far_send,
        recv_sem=far_recv,
        device_id={"col": (me + cols // 2) % cols},
        device_id_type=MESH,
    )
    across_y.start()
    merged[0:width, 0:chunk] = total[:width].astype(jnp.bfloat16)
    across_y.wait()
    send_back(PIECES - 1)

    sorted_rows[...] = lax.dot_general(
        pick[...], merged[...], (((1,), (1,)), ((), ())), preferred_element_type=jnp.float32
    ).astype(jnp.bfloat16)
    moves = []
    for k in range(1, rows):
        to = (row + k) % rows
        copy = pltpu.make_async_remote_copy(
            src_ref=sorted_rows.at[pl.ds(pl.multiple_of(to * share, share), share)],
            dst_ref=got_rows.at[pl.ds(pl.multiple_of(row * share, share), share)],
            send_sem=row_send.at[k],
            recv_sem=row_recv.at[k],
            device_id={"row": to},
            device_id_type=MESH,
        )
        copy.start()
        moves.append(copy)
    keep = pl.ds(pl.multiple_of(row * share, share), share)
    got_rows[keep, :] = sorted_rows[keep, :]
    for copy in moves + back:
        copy.wait()
    for copy in halo + shift:
        copy.wait_send()


def place_kernel(layer_hbm, got_hbm, layer_out, image_ref, layer, got_ref, sem):
    load = pltpu.make_async_copy(got_hbm, got_ref, sem.at[0])
    copies = [
        pltpu.make_async_copy(layer_hbm, layer, sem.at[1]),
        pltpu.make_async_copy(layer, layer_out, sem.at[2]),
    ]
    load.start()
    copies[0].start()
    load.wait()
    width, groups = image_ref.shape
    got = got_ref[...]
    target = got[:, width : width + 1].astype(jnp.float32) * 16.0 + got[
        :, width + 1 : width + 2
    ].astype(jnp.float32)
    slot = lax.broadcasted_iota(jnp.int32, (groups, groups), 1).astype(jnp.float32)
    put = jnp.where(target == slot, 1.0, 0.0).astype(jnp.bfloat16)
    copies[0].wait()
    copies[1].start()
    image_ref[...] = lax.dot_general(
        got, put, (((0,), (0,)), ((), ())), preferred_element_type=jnp.float32
    )[:width].astype(jnp.bfloat16)
    copies[1].wait()


def body(qkv, residual_in, out_weight, merge_weight, merge_gain, image_groups, dest_row):
    rows = lax.axis_size("row")
    cols = lax.axis_size("col")
    _, width, tokens = qkv.shape
    full = out_weight.shape[0]
    reach = tokens // 2
    blocks = tokens // QB
    chunk = tokens // cols
    piece = chunk // PIECES
    groups = tokens // 4
    bf16, f32, i32 = jnp.bfloat16, jnp.float32, jnp.int32
    coef = math.log2(math.e) / math.sqrt(HEAD_DIM)
    vmem = pl.BlockSpec(memory_space=pltpu.VMEM)
    hbm = pl.BlockSpec(memory_space=pl.ANY)
    dma = pltpu.SemaphoreType.DMA
    gain = merge_gain.reshape(-1, 128)
    dest = dest_row.reshape(cols // 2, -1)
    sizes = image_groups[None, :]
    layer, got = pl.pallas_call(
        functools.partial(layer_kernel, rows, cols, coef),
        out_shape=(
            jax.ShapeDtypeStruct((width, tokens), bf16),
            jax.ShapeDtypeStruct((groups, width + 16), bf16),
        ),
        in_specs=[hbm] * 7,
        out_specs=(vmem, vmem),
        scratch_shapes=[
            pltpu.VMEM((width, tokens), bf16),
            pltpu.VMEM((2, width, tokens), bf16),
            pltpu.VMEM((tokens, width), bf16),
            pltpu.VMEM((2, HEAD_DIM, tokens), bf16),
            pltpu.VMEM((2, width, reach), bf16),
            pltpu.VMEM((2, width, reach), bf16),
            pltpu.VMEM((2 * reach, width), bf16),
            pltpu.VMEM((2, HEAD_DIM, 2 * reach), bf16),
            pltpu.VMEM((8, tokens), i32),
            pltpu.VMEM((2, blocks, KB, QB), f32),
            pltpu.VMEM((2 * blocks, 1, QB), f32),
            pltpu.VMEM((2 * blocks, 1, QB), f32),
            pltpu.VMEM((2 * blocks, HEAD_DIM, QB), f32),
            pltpu.VMEM((blocks, width, QB), bf16),
            pltpu.VMEM((width, tokens), bf16),
            pltpu.VMEM((full, chunk), bf16),
            pltpu.VMEM((full, chunk), bf16),
            pltpu.VMEM((full, full), bf16),
            pltpu.VMEM((full, full), bf16),
            pltpu.VMEM((2 * width, merge_weight.shape[1]), bf16),
            pltpu.VMEM((PIECES, full, piece), bf16),
            pltpu.VMEM((PIECES, 4, full, piece), bf16),
            pltpu.VMEM((width, chunk), bf16),
            pltpu.VMEM((width + 16, groups), bf16),
            pltpu.VMEM((groups, groups), bf16),
            pltpu.VMEM((groups, width + 16), bf16),
            pltpu.VMEM((full, 8), f32),
            pltpu.VMEM(gain.shape, f32),
            pltpu.VMEM(sizes.shape, i32),
            pltpu.VMEM(dest.shape, i32),
            dma((9,)),
            dma((4,)),
            dma((4,)),
            dma((cols,)),
            dma((cols,)),
            dma((2,)),
            dma((2,)),
            dma((2, 4)),
            dma((2, 4)),
            dma((cols,)),
            dma((cols,)),
            dma((PIECES, cols)),
            dma((PIECES, cols)),
            dma((PIECES, 2)),
            dma((PIECES, 2)),
            dma((PIECES,)),
            dma((PIECES,)),
            dma((PIECES, 2)),
            dma((PIECES, 2)),
            dma,
            dma,
            dma((rows,)),
            dma((rows,)),
        ],
        compiler_params=pltpu.CompilerParams(
            collective_id=0, has_side_effects=True, vmem_limit_bytes=int(60 * 2**20)
        ),
    )(qkv, residual_in, out_weight, merge_weight, gain, sizes, dest)
    return pl.pallas_call(
        place_kernel,
        out_shape=(
            jax.ShapeDtypeStruct((width, tokens), bf16),
            jax.ShapeDtypeStruct((width, groups), bf16),
        ),
        in_specs=[hbm, hbm],
        out_specs=(hbm, vmem),
        scratch_shapes=[
            pltpu.VMEM((width, tokens), bf16),
            pltpu.VMEM((groups, width + 16), bf16),
            dma((3,)),
        ],
        compiler_params=pltpu.CompilerParams(vmem_limit_bytes=60 << 20),
    )(layer, got)


def solution(mesh):
    return jax.shard_map(
        body,
        mesh=mesh,
        in_specs=(P(None, "col", "row"), P("col", "row"), P(), P("col", None), P(), P(), P("row")),
        out_specs=(P("col", "row"), P("col", "row")),
        check_vma=False,
    )
```

```python
import functools
import math

import jax
import jax.numpy as jnp
from jax import lax
from jax.experimental import pallas as pl
from jax.experimental.pallas import tpu as pltpu
from jax.sharding import PartitionSpec as P

HEAD_DIM = 88
QB = 256
KB = 256
HB = 512
PIECES = 2
NEG = -1e30
MESH = pl.DeviceIdType.MESH


def halo_step(keys, values, qcat, ok, coef, m_ref, l_ref, acc_ref):
    width = qcat.shape[1] // 2
    scores = jnp.dot(keys, qcat, preferred_element_type=jnp.float32)
    for head in range(2):
        part = jnp.where(ok, scores[:, head * width : (head + 1) * width], NEG)
        old = m_ref[head]
        new = jnp.maximum(old, jnp.max(part, axis=0, keepdims=True))
        fade = jnp.exp2((old - new) * coef)
        expo = jnp.exp2(part * coef - new * coef)
        l_ref[head] = l_ref[head] * fade + jnp.sum(expo, axis=0, keepdims=True)
        m_ref[head] = new
        acc_ref[head] = acc_ref[head] * fade + jnp.dot(
            values[head], expo.astype(jnp.bfloat16), preferred_element_type=jnp.float32
        )


def split_heads(values):
    wide = values.astype(jnp.float32)
    return wide[:HEAD_DIM].astype(jnp.bfloat16), wide[HEAD_DIM:].astype(jnp.bfloat16)


def query_pair(block):
    feature = lax.broadcasted_iota(jnp.int32, block.shape, 0)
    zero = jnp.zeros_like(block)
    return jnp.concatenate(
        [jnp.where(feature < HEAD_DIM, block, zero), jnp.where(feature < HEAD_DIM, zero, block)],
        axis=1,
    )


def layer_kernel(
    rows,
    cols,
    coef,
    qkv_hbm,
    residual_hbm,
    out_weight_hbm,
    merge_weight_hbm,
    gain_hbm,
    groups_hbm,
    dest_hbm,
    layer_ref,
    got_rows,
    q_ref,
    kv,
    kt,
    vt,
    left,
    right,
    halo_kt,
    halo_vt,
    bound_ref,
    held_scores,
    m_ref,
    l_ref,
    acc_ref,
    attended,
    res,
    residual,
    att,
    weight,
    weight_t,
    merge_w,
    layer_rows,
    held,
    far_rows,
    merged,
    pick,
    sorted_rows,
    gain_column,
    gain_ref,
    groups_line_ref,
    dest_ref,
    load_sem,
    halo_send,
    halo_recv,
    res_send,
    res_recv,
    shift_send,
    shift_recv,
    gather_send,
    gather_recv,
    spread_send,
    spread_recv,
    back_send,
    back_recv,
    near_send,
    near_recv,
    own_send,
    own_recv,
    pass_send,
    pass_recv,
    far_send,
    far_recv,
    row_send,
    row_recv,
):
    row = lax.axis_index("row")
    me = lax.axis_index("col")
    width, tokens = q_ref.shape
    full = weight.shape[0]
    reach = left.shape[2]
    blocks = tokens // QB
    chunk = tokens // cols
    piece = chunk // PIECES
    part = piece // 4
    groups = tokens // 4
    share = groups // rows
    chips = cols // 2
    core = me % 2
    chip = me // 2
    sibling = me + 1 - 2 * core
    half = full // 2
    line_up = rows // 4
    x_at, z_at = row // line_up, row % line_up

    barrier = pltpu.get_barrier_semaphore()
    for k in range(1, cols):
        pl.semaphore_signal(
            barrier, inc=1, device_id={"col": (me + k) % cols}, device_id_type=MESH
        )
    for k in range(1, rows):
        pl.semaphore_signal(
            barrier, inc=1, device_id={"row": (row + k) % rows}, device_id_type=MESH
        )
    loads = [
        pltpu.make_async_copy(source, target, load_sem.at[i])
        for i, (source, target) in enumerate(
            (
                (qkv_hbm.at[1], kv.at[0]),
                (qkv_hbm.at[2], kv.at[1]),
                (merge_weight_hbm, merge_w.at[0:width]),
                (residual_hbm, res),
                (groups_hbm, groups_line_ref),
                (qkv_hbm.at[0], q_ref),
                (gain_hbm, gain_ref),
                (dest_hbm, dest_ref),
                (out_weight_hbm, weight),
            )
        )
    ]
    for load in loads:
        load.start()
    for load in loads[:4]:
        load.wait()
    pl.semaphore_wait(barrier, rows + cols - 2)

    after_row, before_row = (row + 1) % rows, (row + rows - 1) % rows
    mine = pl.ds(pl.multiple_of(me * chunk, chunk), chunk)
    my_rows = pl.ds(pl.multiple_of(me * width, 16), width)
    halo = []
    for side, (other, target, at) in enumerate(
        ((after_row, left, tokens - reach), (before_row, right, 0))
    ):
        for i in range(2):
            halo.append(
                pltpu.make_async_remote_copy(
                    src_ref=kv.at[i, :, at : at + reach],
                    dst_ref=target.at[i],
                    send_sem=halo_send.at[2 * side + i],
                    recv_sem=halo_recv.at[2 * side + i],
                    device_id={"row": other},
                    device_id_type=MESH,
                )
            )
    cut = width // 32 * 16 + 16
    spans = ((0, cut, x_at), (cut, width, z_at))
    shift, gather = [], []
    for s, (top, end, at) in enumerate(spans):
        across = pl.ds(pl.multiple_of(at * full, 128), full)
        place = merge_w.at[width + top : width + end, across]
        shift.append(
            pltpu.make_async_remote_copy(
                src_ref=merge_w.at[top:end, across],
                dst_ref=place,
                send_sem=shift_send.at[s],
                recv_sem=shift_recv.at[s],
                device_id={"col": (me + cols // 2) % cols},
                device_id_type=MESH,
            )
        )
        for k in range(1, 4):
            other = x_at * line_up + (z_at + k) % line_up if s else (row + k * line_up) % rows
            gather.append(
                pltpu.make_async_remote_copy(
                    src_ref=place,
                    dst_ref=place,
                    send_sem=gather_send.at[s, k],
                    recv_sem=gather_recv.at[s, k],
                    device_id={"row": other},
                    device_id_type=MESH,
                )
            )
    resident = []
    for k in range(1, cols):
        to = (me + k) % cols
        resident.append(
            pltpu.make_async_remote_copy(
                src_ref=res.at[:, pl.ds(pl.multiple_of(to * chunk, chunk), chunk)],
                dst_ref=residual.at[my_rows],
                send_sem=res_send.at[k],
                recv_sem=res_recv.at[k],
                device_id={"col": to},
                device_id_type=MESH,
            )
        )
    for copy in halo + shift:
        copy.start()
    residual[my_rows, :] = res[:, mine]
    for load in loads[4:]:
        load.wait()

    images = groups_line_ref.shape[1]
    first = lax.broadcasted_iota(jnp.int32, (images, images), 0)
    second = lax.broadcasted_iota(jnp.int32, (images, images), 1)
    sizes = groups_line_ref[...]
    size = jnp.sum(jnp.where(second == first, sizes, 0), axis=1, keepdims=True) * 4
    begin = (
        jnp.sum(jnp.where(second < first, sizes, 0), axis=1, keepdims=True) * 4 - row * tokens
    )

    def prepare(b, carry):
        at = pl.multiple_of(b * QB, QB)
        token = lax.broadcasted_iota(jnp.int32, (images, QB), 1) + at
        inside = (token >= begin) & (token < begin + size)
        bound_ref[0:1, pl.ds(at, QB)] = jnp.sum(jnp.where(inside, begin, 0), axis=0, keepdims=True)
        bound_ref[1:2, pl.ds(at, QB)] = jnp.sum(jnp.where(inside, size, 0), axis=0, keepdims=True)
        kt[pl.ds(at, QB), :] = jnp.transpose(kv[0, :, pl.ds(at, QB)])
        v0, v1 = split_heads(kv[1, :, pl.ds(at, QB)])
        vt[0, :, pl.ds(at, QB)] = v0
        vt[1, :, pl.ds(at, QB)] = v1
        return carry

    lax.fori_loop(0, blocks, prepare, 0)

    def local_block(b, carry):
        at = pl.multiple_of(b * QB, QB)
        qcat = query_pair(q_ref[:, pl.ds(at, QB)])
        start = bound_ref[0:1, pl.ds(at, QB)]
        length = bound_ref[1:2, pl.ds(at, QB)]
        spot = lax.broadcasted_iota(jnp.int32, (KB, QB), 0) - start
        tops = [jnp.full((1, QB), NEG, jnp.float32) for _ in range(2)]
        for t in range(blocks):
            key = t * KB
            scores = jnp.dot(kt[key : key + KB, :], qcat, preferred_element_type=jnp.float32)
            ok = (spot >= -key) & (spot < length - key)
            for head in range(2):
                masked = jnp.where(ok, scores[:, head * QB : (head + 1) * QB], NEG)
                held_scores[head, t] = masked
                tops[head] = jnp.maximum(tops[head], jnp.max(masked, axis=0, keepdims=True))
        for head in range(2):
            peak = tops[head] * coef
            total = jnp.zeros((1, QB), jnp.float32)
            sums = jnp.zeros((HEAD_DIM, QB), jnp.float32)
            for t in range(blocks):
                expo = jnp.exp2(held_scores[head, t] * coef - peak)
                total = total + jnp.sum(expo, axis=0, keepdims=True)
                sums = sums + jnp.dot(
                    vt[head, :, t * KB : (t + 1) * KB],
                    expo.astype(jnp.bfloat16),
                    preferred_element_type=jnp.float32,
                )
            m_ref[b * 2 + head] = tops[head]
            l_ref[b * 2 + head] = total
            acc_ref[b * 2 + head] = sums
        return carry

    lax.fori_loop(0, blocks // 2, local_block, 0)
    for copy in resident:
        copy.start()
    lax.fori_loop(blocks // 2, blocks, local_block, 0)

    def turn(i, carry):
        at = pl.multiple_of(i * 128, 128)
        weight_t[pl.ds(at, 128), :] = jnp.transpose(weight[:, pl.ds(at, 128)])
        return carry

    lax.fori_loop(0, full // 128, turn, 0)
    for i in range(full // 128):
        gain_column[i * 128 : (i + 1) * 128, :] = jnp.transpose(
            jnp.broadcast_to(gain_ref[i : i + 1, :], (8, 128))
        )

    before, after, across_chip = (chip + 3) % chips, (chip + 1) % chips, (chip + 2) % chips
    of = [dest_ref[pl.ds(c, 1), :] for c in (chip, before, across_chip, after)]
    span = chunk // 4
    line = jnp.concatenate(
        [
            of[c][:, k * span + p * part : k * span + (p + 1) * part]
            for order in (((0, 0), (0, 1), (1, 0), (3, 1)), ((2, 0), (2, 1), (3, 0), (1, 1)))
            for p in range(PIECES)
            for c, k in order
        ],
        axis=1,
    )
    owner_line = line // groups
    owner_column = jnp.transpose(
        jnp.broadcast_to(owner_line.astype(jnp.float32), (8, groups))
    )[:, 0:1].astype(jnp.int32)
    down = lax.broadcasted_iota(jnp.int32, (groups, groups), 0)
    across = lax.broadcasted_iota(jnp.int32, (groups, groups), 1)
    earlier = (owner_column == owner_line) & (down < across)
    rank = jnp.sum(earlier.astype(jnp.int32), axis=0, keepdims=True)
    pick[...] = jnp.where(down == owner_line * share + rank, 1.0, 0.0).astype(jnp.bfloat16)
    slot = line % groups
    which = lax.broadcasted_iota(jnp.int32, (merged.shape[0] - width, groups), 0)
    digits = jnp.where(which == 0, slot // 16, jnp.where(which == 1, slot % 16, 0))
    merged[width:, :] = digits.astype(jnp.float32).astype(jnp.bfloat16)

    for copy in shift:
        copy.wait_recv()
    for copy in gather:
        copy.start()
    for copy in halo:
        copy.wait_recv()

    def prepare_halo(i, carry):
        at = pl.multiple_of(i * QB, QB)
        for source, base in ((left, 0), (right, reach)):
            to = pl.ds(pl.multiple_of(base + at, QB), QB)
            halo_kt[to, :] = jnp.transpose(source[0, :, pl.ds(at, QB)])
            v0, v1 = split_heads(source[1, :, pl.ds(at, QB)])
            halo_vt[0, :, to] = v0
            halo_vt[1, :, to] = v1
        return carry

    lax.fori_loop(0, reach // QB, prepare_halo, 0)

    def spread_copy(k):
        to = (me + k) % cols
        return pltpu.make_async_remote_copy(
            src_ref=attended.at[to],
            dst_ref=att.at[my_rows],
            send_sem=spread_send.at[k],
            recv_sem=spread_recv.at[k],
            device_id={"col": to},
            device_id_type=MESH,
        )

    def halo_block(b):
        at = pl.multiple_of(b * QB, QB)
        qcat = query_pair(q_ref[:, pl.ds(at, QB)])
        start = bound_ref[0:1, pl.ds(at, QB)]
        length = bound_ref[1:2, pl.ds(at, QB)]
        high = b // (blocks // 2)
        tiles = high * (b - blocks // 2 + 1) + (1 - high) * (blocks // 2 - b)

        def pair(t, inner):
            slot = high * (reach + t * HB) + (1 - high) * (reach - (t + 1) * HB)
            slot = pl.multiple_of(slot, HB)
            key = slot - reach + high * tokens
            spot = lax.broadcasted_iota(jnp.int32, (HB, QB), 0) + (key - start)
            ok = (spot >= 0) & (spot < length)
            halo_step(
                halo_kt[pl.ds(slot, HB), :],
                [halo_vt[head, :, pl.ds(slot, HB)] for head in range(2)],
                qcat,
                ok,
                coef,
                m_ref.at[pl.ds(b * 2, 2)],
                l_ref.at[pl.ds(b * 2, 2)],
                acc_ref.at[pl.ds(b * 2, 2)],
            )
            return inner

        lax.fori_loop(0, (tiles * KB + HB - 1) // HB, pair, 0)
        both = [acc_ref[b * 2 + head] * (1.0 / l_ref[b * 2 + head]) for head in range(2)]
        attended[b] = jnp.concatenate(both, axis=0).astype(jnp.bfloat16)

    def block_of(i, carry):
        halo_block((me + 1 + i) % cols)
        spread_copy(1 + i).start()
        return carry

    lax.fori_loop(0, cols - 1, block_of, 0)
    halo_block(me)
    att[my_rows, :] = attended[me]
    for copy in resident:
        copy.wait()
    for k in range(1, cols):
        spread_copy(k).wait_recv()

    def lanes(owner, p):
        return pl.ds(pl.multiple_of(owner * chunk + p * piece, 128), piece)

    here = lax.broadcasted_iota(jnp.int32, (piece, piece), 0)
    there = lax.broadcasted_iota(jnp.int32, (piece, piece), 1)
    order = jnp.where((here % 4) * part + here // 4 == there, 1.0, 0.0).astype(jnp.bfloat16)
    goal = (chip + 1 + 2 * core) % chips
    near, own, back = [], [], []
    for p in range(PIECES):
        at = slice(p * piece, (p + 1) * piece)
        projected = jnp.dot(weight_t[...], att[:, at], preferred_element_type=jnp.float32)
        rounded = (residual[:, at].astype(jnp.float32) + projected).astype(jnp.bfloat16)
        layer_rows[p] = rounded
        values32 = rounded.astype(jnp.float32)
        centre = jnp.sum(values32, axis=0, keepdims=True) * (1.0 / full)
        spread_of = jnp.sum(jnp.square(values32 - centre), axis=0, keepdims=True) * (1.0 / full)
        scale = lax.rsqrt(spread_of + 1e-06)
        normed = ((values32 - centre) * scale * gain_column[:, 0:1]).astype(jnp.bfloat16)
        held[p, core] = jnp.dot(normed, order, preferred_element_type=jnp.float32).astype(
            jnp.bfloat16
        )
        for h in range(2):
            rows_of = pl.ds(h * half, half)
            copy = pltpu.make_async_remote_copy(
                src_ref=held.at[p, core, rows_of],
                dst_ref=held.at[p, 2 + core, rows_of],
                send_sem=near_send.at[p, h],
                recv_sem=near_recv.at[p, core],
                device_id={"col": goal * 2 + h},
                device_id_type=MESH,
            )
            copy.start()
            near.append(copy)
        copy = pltpu.make_async_remote_copy(
            src_ref=held.at[p, core],
            dst_ref=held.at[p, core],
            send_sem=own_send.at[p],
            recv_sem=own_recv.at[p],
            device_id={"col": sibling},
            device_id_type=MESH,
        )
        copy.start()
        own.append(copy)
        layer_ref[:, lanes(me, p)] = layer_rows[p, my_rows, :]

    for k in range(1, cols):
        spread_copy(k).wait_send()
    passed = []
    my_half = pl.ds(pl.multiple_of(core * half, 16), half)
    for p in range(PIECES):
        for s in range(2):
            arrive = pltpu.make_async_remote_copy(
                src_ref=held.at[p, core, my_half],
                dst_ref=held.at[p, 2 + s, my_half],
                send_sem=near_send.at[p, s],
                recv_sem=near_recv.at[p, s],
                device_id={"col": sibling},
                device_id_type=MESH,
            )
            arrive.wait_recv()
            copy = pltpu.make_async_remote_copy(
                src_ref=held.at[p, 2 + s, my_half],
                dst_ref=held.at[p, 2 + s, my_half],
                send_sem=pass_send.at[p, s],
                recv_sem=pass_recv.at[p, s],
                device_id={"col": sibling},
                device_id_type=MESH,
            )
            copy.start()
            passed.append(copy)

    def send_back(p):
        for k in range(1, cols):
            to = (me + k) % cols
            copy = pltpu.make_async_remote_copy(
                src_ref=layer_rows.at[p, pl.ds(pl.multiple_of(to * width, 16), width)],
                dst_ref=layer_ref.at[:, lanes(me, p)],
                send_sem=back_send.at[p, k],
                recv_sem=back_recv.at[p, k],
                device_id={"col": to},
                device_id_type=MESH,
            )
            copy.start()
            back.append(copy)

    for p in range(PIECES - 1):
        send_back(p)
    for copy in gather:
        copy.wait()
    for copy in own + passed:
        copy.wait()
    for copy in near:
        copy.wait_send()

    total = None
    for j in range(4):
        side = jnp.concatenate(
            [
                held[p, s, :, j * part : (j + 1) * part]
                for p in range(PIECES)
                for s in range(4)
            ],
            axis=1,
        )
        term = jnp.dot(
            merge_w[:, j * full : (j + 1) * full], side, preferred_element_type=jnp.float32
        )
        total = term if total is None else total + term
    far_rows[...] = total[width:].astype(jnp.bfloat16)
    across_y = pltpu.make_async_remote_copy(
        src_ref=far_rows,
        dst_ref=merged.at[0:width, chunk : 2 * chunk],
        send_sem=far_send,
        recv_sem=far_recv,
        device_id={"col": (me + cols // 2) % cols},
        device_id_type=MESH,
    )
    across_y.start()
    merged[0:width, 0:chunk] = total[:width].astype(jnp.bfloat16)
    across_y.wait()
    send_back(PIECES - 1)

    sorted_rows[...] = lax.dot_general(
        pick[...], merged[...], (((1,), (1,)), ((), ())), preferred_element_type=jnp.float32
    ).astype(jnp.bfloat16)
    moves = []
    for k in range(1, rows):
        to = (row + k) % rows
        copy = pltpu.make_async_remote_copy(
            src_ref=sorted_rows.at[pl.ds(pl.multiple_of(to * share, share), share)],
            dst_ref=got_rows.at[pl.ds(pl.multiple_of(row * share, share), share)],
            send_sem=row_send.at[k],
            recv_sem=row_recv.at[k],
            device_id={"row": to},
            device_id_type=MESH,
        )
        copy.start()
        moves.append(copy)
    keep = pl.ds(pl.multiple_of(row * share, share), share)
    got_rows[keep, :] = sorted_rows[keep, :]
    for copy in moves + back:
        copy.wait()
    for copy in halo + shift:
        copy.wait_send()


def place_kernel(layer_hbm, got_hbm, layer_out, image_ref, layer, got_ref, sem):
    load = pltpu.make_async_copy(got_hbm, got_ref, sem.at[0])
    copies = [
        pltpu.make_async_copy(layer_hbm, layer, sem.at[1]),
        pltpu.make_async_copy(layer, layer_out, sem.at[2]),
    ]
    load.start()
    copies[0].start()
    load.wait()
    width, groups = image_ref.shape
    got = got_ref[...]
    target = got[:, width : width + 1].astype(jnp.float32) * 16.0 + got[
        :, width + 1 : width + 2
    ].astype(jnp.float32)
    slot = lax.broadcasted_iota(jnp.int32, (groups, groups), 1).astype(jnp.float32)
    put = jnp.where(target == slot, 1.0, 0.0).astype(jnp.bfloat16)
    copies[0].wait()
    copies[1].start()
    image_ref[...] = lax.dot_general(
        got, put, (((0,), (0,)), ((), ())), preferred_element_type=jnp.float32
    )[:width].astype(jnp.bfloat16)
    copies[1].wait()


def body(qkv, residual_in, out_weight, merge_weight, merge_gain, image_groups, dest_row):
    rows = lax.axis_size("row")
    cols = lax.axis_size("col")
    _, width, tokens = qkv.shape
    full = out_weight.shape[0]
    reach = tokens // 2
    blocks = tokens // QB
    chunk = tokens // cols
    piece = chunk // PIECES
    groups = tokens // 4
    bf16, f32, i32 = jnp.bfloat16, jnp.float32, jnp.int32
    coef = math.log2(math.e) / math.sqrt(HEAD_DIM)
    vmem = pl.BlockSpec(memory_space=pltpu.VMEM)
    hbm = pl.BlockSpec(memory_space=pl.ANY)
    dma = pltpu.SemaphoreType.DMA
    gain = merge_gain.reshape(-1, 128)
    dest = dest_row.reshape(cols // 2, -1)
    sizes = image_groups[None, :]
    layer, got = pl.pallas_call(
        functools.partial(layer_kernel, rows, cols, coef),
        out_shape=(
            jax.ShapeDtypeStruct((width, tokens), bf16),
            jax.ShapeDtypeStruct((groups, width + 16), bf16),
        ),
        in_specs=[hbm] * 7,
        out_specs=(vmem, vmem),
        scratch_shapes=[
            pltpu.VMEM((width, tokens), bf16),
            pltpu.VMEM((2, width, tokens), bf16),
            pltpu.VMEM((tokens, width), bf16),
            pltpu.VMEM((2, HEAD_DIM, tokens), bf16),
            pltpu.VMEM((2, width, reach), bf16),
            pltpu.VMEM((2, width, reach), bf16),
            pltpu.VMEM((2 * reach, width), bf16),
            pltpu.VMEM((2, HEAD_DIM, 2 * reach), bf16),
            pltpu.VMEM((8, tokens), i32),
            pltpu.VMEM((2, blocks, KB, QB), f32),
            pltpu.VMEM((2 * blocks, 1, QB), f32),
            pltpu.VMEM((2 * blocks, 1, QB), f32),
            pltpu.VMEM((2 * blocks, HEAD_DIM, QB), f32),
            pltpu.VMEM((blocks, width, QB), bf16),
            pltpu.VMEM((width, tokens), bf16),
            pltpu.VMEM((full, chunk), bf16),
            pltpu.VMEM((full, chunk), bf16),
            pltpu.VMEM((full, full), bf16),
            pltpu.VMEM((full, full), bf16),
            pltpu.VMEM((2 * width, merge_weight.shape[1]), bf16),
            pltpu.VMEM((PIECES, full, piece), bf16),
            pltpu.VMEM((PIECES, 4, full, piece), bf16),
            pltpu.VMEM((width, chunk), bf16),
            pltpu.VMEM((width + 16, groups), bf16),
            pltpu.VMEM((groups, groups), bf16),
            pltpu.VMEM((groups, width + 16), bf16),
            pltpu.VMEM((full, 8), f32),
            pltpu.VMEM(gain.shape, f32),
            pltpu.VMEM(sizes.shape, i32),
            pltpu.VMEM(dest.shape, i32),
            dma((9,)),
            dma((4,)),
            dma((4,)),
            dma((cols,)),
            dma((cols,)),
            dma((2,)),
            dma((2,)),
            dma((2, 4)),
            dma((2, 4)),
            dma((cols,)),
            dma((cols,)),
            dma((PIECES, cols)),
            dma((PIECES, cols)),
            dma((PIECES, 2)),
            dma((PIECES, 2)),
            dma((PIECES,)),
            dma((PIECES,)),
            dma((PIECES, 2)),
            dma((PIECES, 2)),
            dma,
            dma,
            dma((rows,)),
            dma((rows,)),
        ],
        compiler_params=pltpu.CompilerParams(
            collective_id=0, has_side_effects=True, vmem_limit_bytes=int(60 * 2**20)
        ),
    )(qkv, residual_in, out_weight, merge_weight, gain, sizes, dest)
    return pl.pallas_call(
        place_kernel,
        out_shape=(
            jax.ShapeDtypeStruct((width, tokens), bf16),
            jax.ShapeDtypeStruct((width, groups), bf16),
        ),
        in_specs=[hbm, hbm],
        out_specs=(hbm, vmem),
        scratch_shapes=[
            pltpu.VMEM((width, tokens), bf16),
            pltpu.VMEM((groups, width + 16), bf16),
            dma((3,)),
        ],
        compiler_params=pltpu.CompilerParams(vmem_limit_bytes=60 << 20),
    )(layer, got)


def solution(mesh):
    return jax.shard_map(
        body,
        mesh=mesh,
        in_specs=(P(None, "col", "row"), P("col", "row"), P(), P("col", None), P(), P(), P("row")),
        out_specs=(P("col", "row"), P("col", "row")),
        check_vma=False,
    )
```
